128 devices in a mesh: seq: 64 (over y_lo, x, z, core), ch: 2 (over y_hi).
Axes of the slice: x: 4, y: 4 (y_hi: 2, y_lo: 2; y = y_hi * 2 + y_lo), z: 4, core: 2. Of those that a mesh axis runs over, the one named last changes fastest.
Arguments:
- out_grad: bfloat16 [8192, 4096], P('seq', 'ch'), may hold values from -6 to 6
- out_weight: bfloat16 [4096, 4096], P(('seq', 'ch')), may hold values from -0.09375 to 0.09375
- outer_gate: bfloat16 [8192, 4096], P('seq', 'ch'), may hold values from -6 to 6
- long_out: bfloat16 [8192, 4096], P('seq', 'ch'), may hold values from -6 to 6
- inner_gate: bfloat16 [8192, 4096], P('seq', 'ch'), may hold values from -6 to 6
- conv_input: bfloat16 [8192, 4096], P('seq', 'ch'), may hold values from -6 to 6
- short_out: bfloat16 [8192, 4096], P('seq', 'ch'), may hold values from -6 to 6
- medium_out: bfloat16 [8192, 4096], P('seq', 'ch'), may hold values from -6 to 6
- long_filter: bfloat16 [8192, 4096], P('seq', 'ch'), may hold values from -6 to 6
- taps_short: bfloat16 [7, 4096], P(None, 'ch'), may hold values from -2 to 2
- taps_medium: bfloat16 [128, 4096], P(None, 'ch'), may hold values from -0.5 to 0.5
Outputs:
- grad_outer: bfloat16 [8192, 4096], P('seq', 'ch')
- grad_inner: bfloat16 [8192, 4096], P('seq', 'ch')
- grad_input: bfloat16 [8192, 4096], P('seq', 'ch')
- grad_filter: float32 [8192, 4096], P('seq', 'ch')
- grad_short: float32 [7, 4096], P(None, 'ch')
- grad_medium: float32 [128, 4096], P(None, 'ch')
The draws below stay inside these ranges and needn't reach their ends.
All inputs are finite; a program needn't handle non-finite values.
Results may differ from the reference program's by a relative error of at most 0.0065.
Values may be sent and summed in bfloat16 or wider, within the bound.
A program may use at most 128 MiB of HBM per device.

```python
import jax
import jax.numpy as jnp

D = 4096
SHORT = 7
MEDIUM = 128
NTOK = 8192


def level_of(key, extent, cuts, smallest, high):
    def one(position, shards_of):
        heights = jax.random.uniform(jax.random.fold_in(jax.random.fold_in(key, 6), position), (shards_of,), jnp.float32, smallest / len(cuts), high / len(cuts))
        return jnp.repeat(jnp.exp(heights), extent[position] // shards_of).reshape((-1,) + (1,) * (len(extent) - position - 1))

    gain = one(*cuts[0])
    for cut in cuts[1:]:
        gain = gain * one(*cut)
    return gain


def noise(rng, extent, spread, bound, shards=(), held_as=jnp.bfloat16):
    drawn = spread * jax.random.normal(rng, extent, jnp.float32)
    if shards:
        drawn = drawn * level_of(rng, extent, shards, -0.22, 0.18)
    return jnp.clip(drawn, -bound, bound).astype(held_as)


def setup_inputs(seed: int = 0) -> dict:
    key_list = jax.random.split(jax.random.key(seed), 12)
    return {
        "out_grad": noise(key_list[0], (NTOK, D), 1.0, 6.0, ((0, 64), (1, 2))),
        "out_weight": noise(key_list[1], (D, D), D ** -0.5, 0.09375, ((0, 128),)),
        "outer_gate": noise(key_list[2], (NTOK, D), 1.0, 6.0, ((0, 64), (1, 2))),
        "long_out": noise(key_list[3], (NTOK, D), 1.0, 6.0, ((0, 64), (1, 2))),
        "inner_gate": noise(key_list[4], (NTOK, D), 1.0, 6.0, ((0, 64), (1, 2))),
        "conv_input": noise(key_list[5], (NTOK, D), 1.0, 6.0, ((0, 64), (1, 2))),
        "short_out": noise(key_list[6], (NTOK, D), 1.0, 6.0, ((0, 64), (1, 2))),
        "medium_out": noise(key_list[7], (NTOK, D), 1.0, 6.0, ((0, 64), (1, 2))),
        "long_filter": noise(key_list[8], (NTOK, D), 1.0, 6.0, ((0, 64), (1, 2))),
        "taps_short": noise(key_list[9], (SHORT, D), SHORT ** -0.5, 2.0, ((1, 2),)),
        "taps_medium": noise(key_list[10], (MEDIUM, D), MEDIUM ** -0.5, 0.5, ((1, 2),)),
    }


def correlate(first, second):
    length = second.shape[0]
    first_spec = jnp.fft.rfft(first.astype(jnp.float32), n=2 * length, axis=0)
    second_spec = jnp.fft.rfft(second.astype(jnp.float32), n=2 * length, axis=0)
    return jnp.fft.irfft(jnp.conj(first_spec) * second_spec, n=2 * length, axis=0)[:length]


def adjoint_taps(grads, taps):
    return correlate(taps, grads)


def tap_products(grads, values, count):
    return correlate(values, grads)[:count]


def reference(out_grad, out_weight, outer_gate, long_out, inner_gate, conv_input, short_out, medium_out, long_filter, taps_short, taps_medium):
    factor = NTOK ** -0.5
    hidden = jnp.dot(out_grad, out_weight, preferred_element_type=jnp.float32)
    grad_outer = (hidden * long_out.astype(jnp.float32)).astype(jnp.bfloat16)
    long_grad = (hidden * outer_gate.astype(jnp.float32)).astype(jnp.bfloat16)
    product = (inner_gate.astype(jnp.float32) * medium_out.astype(jnp.float32)).astype(jnp.bfloat16)
    point_grad = factor * correlate(long_filter, long_grad)
    grad_filter = factor * correlate(product, long_grad)
    medium_grad = (point_grad * inner_gate.astype(jnp.float32)).astype(jnp.bfloat16)
    grad_inner = (point_grad * medium_out.astype(jnp.float32)).astype(jnp.bfloat16)
    short_grad = adjoint_taps(medium_grad, taps_medium).astype(jnp.bfloat16)
    grad_input = adjoint_taps(short_grad, taps_short).astype(jnp.bfloat16)
    grad_medium = factor * tap_products(medium_grad, short_out, MEDIUM)
    grad_short = factor * tap_products(short_grad, conv_input, SHORT)
    return grad_outer, grad_inner, grad_input, grad_filter, grad_short, grad_medium
```

```python
import math

import jax
import jax.numpy as jnp
import numpy as np
from jax import lax
from jax.experimental import pallas as pl
from jax.experimental.pallas import tpu as pltpu
from jax.sharding import PartitionSpec as P

SHORT = 7
MEDIUM = 128
LANES = 128
F32 = jnp.float32
BF16 = jnp.bfloat16
VMEM_LIMIT = 60 * 1024 * 1024


def split_np(table):
    high = table.astype(np.float32).astype(jnp.bfloat16)
    low = (table - high.astype(np.float64)).astype(np.float32).astype(jnp.bfloat16)
    return high, low


def tables(rows):
    total = 2 * rows * LANES
    freq = np.arange(rows)[:, None] + 0.5
    place = np.arange(rows)[None, :]
    angle = 2.0 * np.pi * freq * place / (2 * rows)
    first = np.concatenate([np.cos(angle), -np.sin(angle)], 0)
    first = np.concatenate(split_np(first), 1)
    twist = 2.0 * np.pi * freq * np.arange(LANES)[None, :] / total
    inner = 2.0 * np.pi * np.outer(np.arange(LANES), np.arange(LANES)) / LANES
    cosine, sine = np.cos(inner), np.sin(inner)
    forward = np.block([[cosine, -sine], [sine, cosine]])
    inverse = np.block([[cosine, sine], [-sine, cosine]])
    scale = (rows * LANES) ** -0.5 * 2.0 / total
    last = np.concatenate([np.cos(angle.T), -np.sin(angle.T)], 1) * scale
    twists = np.concatenate([np.cos(twist), np.sin(twist)], 1).astype(np.float32)
    flip = np.eye(LANES)[::-1].astype(jnp.bfloat16)
    return (
        first,
        twists,
        np.concatenate(split_np(forward), 0),
        np.concatenate(split_np(inverse), 0),
        np.concatenate(split_np(last), 0),
        flip,
    )


def dot(a, b):
    return jnp.dot(a, b, preferred_element_type=F32)


def dot_t(a, b):
    return lax.dot_general(a, b, (((1,), (1,)), ((), ())), preferred_element_type=F32)


def split(x):
    high = x.astype(BF16)
    return high, (x - high.astype(F32)).astype(BF16)


def dot3(high, low, table):
    size = table.shape[0] // 2
    return dot(high, table[:size]) + dot(high, table[size:]) + dot(low, table[:size])


def outer_stage(pair, first, twists):
    rows = pair.shape[0]
    spread = dot(first, jnp.concatenate([pair, pair], 0))
    cosine = jnp.concatenate([twists[:, :LANES]] * 2, 1)
    sine = jnp.concatenate([twists[:, LANES:]] * 2, 1)
    real, imag = spread[:rows], spread[rows:]
    new_real = real * cosine + imag * sine
    new_imag = imag * cosine - real * sine
    return (
        jnp.concatenate([new_real[:, :LANES], new_imag[:, :LANES]], 1),
        jnp.concatenate([new_real[:, LANES:], new_imag[:, LANES:]], 1),
    )


def toeplitz(line):
    row = jnp.concatenate([line, jnp.zeros_like(line)], 1)
    block = jnp.broadcast_to(row, (LANES, 2 * LANES))
    return pltpu.roll(block, 0, 1, stride=1, stride_axis=0)


def prepare_kernel(
    early_ref, taps_ref, first_ref, twists_ref, forward_ref, flip_ref,
    spec_ref, gates_ref, bands_ref, turned_ref,
    lines, zh, zl,
):
    rows, width = early_ref.shape[0], early_ref.shape[2]

    @pl.loop(0, rows)
    def _(i):
        at = pl.ds(pl.multiple_of(i * width, width), width)
        for k in range(5):
            lines[k, at, :] = early_ref[i, k].astype(F32)

    @pl.loop(0, width)
    def _(c):
        pick = pl.ds(c, rows, stride=width)
        inner, medium = lines[0, pick, :], lines[1, pick, :]
        mine = pl.ds(pl.multiple_of(c * rows, rows), rows)
        gates_ref[0, mine, :] = inner
        gates_ref[1, mine, :] = medium
        product = (inner * medium).astype(BF16)
        pair = jnp.concatenate([product, lines[4, pick, :].astype(BF16)], 1)
        for k, part in enumerate(outer_stage(pair, first_ref[...], twists_ref[...])):
            high, low = split(part)
            there = pl.ds(pl.multiple_of(k * rows * width + c * rows, rows), rows)
            zh[there, :] = high
            zl[there, :] = low
        wide = pl.ds(pl.multiple_of(c * LANES, LANES), LANES)
        for k in range(2):
            bands_ref[k, wide, :] = toeplitz(taps_ref[k, pl.ds(c, 1), :]).astype(BF16)
            saved = lines[2 + k, pick, :].astype(BF16)
            turned_ref[k, wide, :] = dot_t(flip_ref[...], saved).astype(BF16)

    step = 512

    @pl.loop(0, 2 * rows * width // step)
    def _(b):
        at = pl.ds(pl.multiple_of(b * step, step), step)
        spec_ref[at, :] = dot3(zh[at, :], zl[at, :], forward_ref[...])


def finish_kernel(
    late_ref, spec_ref, gates_ref, bands_ref, turned_ref,
    first_ref, twists_ref, forward_ref, inverse_ref, last_ref,
    out_ref, taps_ref,
    lines, zh, zl, ch, cl, results,
):
    rows, width = late_ref.shape[0], late_ref.shape[1]
    high_row = rows - 1

    @pl.loop(0, rows)
    def _(i):
        at = pl.ds(pl.multiple_of(i * width, width), width)
        lines[at, :] = late_ref[i].astype(F32)

    @pl.loop(0, width // 2)
    def _(c):
        pair = jnp.concatenate(
            [lines[pl.ds(2 * c + k, rows, stride=width), :] for k in range(2)], 1
        ).astype(BF16)
        for k, part in enumerate(outer_stage(pair, first_ref[...], twists_ref[...])):
            high, low = split(part)
            there = pl.ds(pl.multiple_of((2 * c + k) * rows, rows), rows)
            zh[there, :] = high
            zl[there, :] = low

    many = 4
    step = many * rows

    @pl.loop(0, width // many)
    def _(b):
        at = pl.ds(pl.multiple_of(b * step, step), step)
        grad = dot3(zh[at, :], zl[at, :], forward_ref[...])
        grad_real, grad_imag = grad[:, :LANES], grad[:, LANES:]
        cosine = jnp.concatenate([twists_ref[:, :LANES]] * many, 0)
        sine = jnp.concatenate([twists_ref[:, LANES:]] * many, 0)
        reals, imags = [], []
        for k in range(2):
            source = 1 - k
            other = spec_ref[
                pl.ds(pl.multiple_of(source * rows * width + b * step, step), step), :
            ]
            real, imag = other[:, :LANES], other[:, LANES:]
            term = jnp.concatenate(
                [real * grad_real + imag * grad_imag, real * grad_imag - imag * grad_real], 1
            )
            back = dot3(*split(term), inverse_ref[...])
            real, imag = back[:, :LANES], back[:, LANES:]
            reals.append(real * cosine - imag * sine)
            imags.append(real * sine + imag * cosine)
        real, imag = jnp.concatenate(reals, 1), jnp.concatenate(imags, 1)
        for k in range(many):
            both = jnp.concatenate(
                [real[k * rows : (k + 1) * rows], imag[k * rows : (k + 1) * rows]], 0
            )
            high, low = split(both)
            there = pl.ds(
                pl.multiple_of((b * many + k) * 2 * rows, 2 * rows), 2 * rows
            )
            ch[there, :] = high
            cl[there, :] = low

    row = lax.broadcasted_iota(jnp.int32, (rows, LANES), 0)

    def with_next(x):
        following = jnp.where(row == high_row, 0.0, pltpu.roll(x, high_row, 0))
        return jnp.concatenate([x, following], 1).astype(BF16)

    def diagonals(c, k, both):
        wide = pl.ds(pl.multiple_of(c * LANES, LANES), LANES)
        products = dot(turned_ref[k, wide, :], both)
        slid = pltpu.roll(products, 0, 1, stride=1, stride_axis=0)
        return jnp.sum(slid, axis=0, keepdims=True)

    def channel(c):
        there = pl.ds(pl.multiple_of(c * 2 * rows, 2 * rows), 2 * rows)
        mine = pl.ds(pl.multiple_of(c * rows, rows), rows)
        wide = pl.ds(pl.multiple_of(c * LANES, LANES), LANES)
        high, low = ch[there, :], cl[there, :]
        point = dot(last_ref[:rows], high) + dot(last_ref[:rows], low) + dot(last_ref[rows:], high)
        point, filt = point[:, :LANES], point[:, LANES:]
        medium_grad = (point * gates_ref[0, mine, :]).astype(BF16).astype(F32)
        both = with_next(medium_grad)
        short_grad = dot_t(both, bands_ref[0, wide, :]).astype(BF16).astype(F32)
        pair = with_next(short_grad)
        grad_input = dot_t(pair, bands_ref[1, wide, :])
        pick = pl.ds(c, rows, stride=width)
        results[0, pick, :] = point * gates_ref[1, mine, :]
        results[1, pick, :] = grad_input
        results[2, pick, :] = filt
        taps_ref[0, pl.ds(c, 1), :] = diagonals(c, 0, both)
        taps_ref[1, pl.ds(c, 1), :] = diagonals(c, 1, pair)

    unroll = 4

    @pl.loop(0, width // unroll)
    def _(b):
        for k in range(unroll):
            channel(b * unroll + k)

    @pl.loop(0, rows)
    def _(i):
        at = pl.ds(pl.multiple_of(i * width, width), width)
        for k in range(3):
            out_ref[i, k] = results[k, at, :].astype(BF16)


def whole(n):
    return [pl.BlockSpec(memory_space=pltpu.VMEM)] * n


def prepare(early, taps, first, twists, forward, flip):
    rows, _, width, _ = early.shape
    area = rows * width
    return pl.pallas_call(
        prepare_kernel,
        out_shape=(
            jax.ShapeDtypeStruct((2 * area, 2 * LANES), F32),
            jax.ShapeDtypeStruct((2, area, LANES), F32),
            jax.ShapeDtypeStruct((2, width * LANES, 2 * LANES), BF16),
            jax.ShapeDtypeStruct((2, width * LANES, rows), BF16),
        ),
        in_specs=whole(6),
        out_specs=whole(4),
        scratch_shapes=[
            pltpu.VMEM((5, area, LANES), F32),
            pltpu.VMEM((2 * area, 2 * LANES), BF16),
            pltpu.VMEM((2 * area, 2 * LANES), BF16),
        ],
        compiler_params=pltpu.CompilerParams(vmem_limit_bytes=VMEM_LIMIT),
        cost_estimate=pl.CostEstimate(flops=4 * 10**9, bytes_accessed=20 * 2**20, transcendentals=0),
        name="prepare",
    )(early, taps, first, twists, forward, flip)


def finish(late, spec, gates, bands, turned, first, twists, forward, inverse, last):
    rows, width, _ = late.shape
    area = rows * width
    return pl.pallas_call(
        finish_kernel,
        out_shape=(
            jax.ShapeDtypeStruct((rows, 3, width, LANES), BF16),
            jax.ShapeDtypeStruct((2, width, 2 * LANES), F32),
        ),
        in_specs=whole(10),
        out_specs=whole(2),
        scratch_shapes=[
            pltpu.VMEM((area, LANES), F32),
            pltpu.VMEM((area, 2 * LANES), BF16),
            pltpu.VMEM((area, 2 * LANES), BF16),
            pltpu.VMEM((2 * area, 2 * LANES), BF16),
            pltpu.VMEM((2 * area, 2 * LANES), BF16),
            pltpu.VMEM((3, area, LANES), F32),
        ],
        compiler_params=pltpu.CompilerParams(vmem_limit_bytes=VMEM_LIMIT),
        cost_estimate=pl.CostEstimate(flops=8 * 10**9, bytes_accessed=20 * 2**20, transcendentals=0),
        name="finish",
    )(late, spec, gates, bands, turned, first, twists, forward, inverse, last)


def turn_kernel(*refs):
    *ins, out = refs
    blocks, _, width, _ = out.shape
    for k, ref in enumerate(ins):
        out[:, k] = ref[...].astype(F32).T.astype(BF16).reshape(blocks, width, LANES)


def to_blocks(arrays, devices):
    height, channels = arrays[0].shape
    width = channels // devices
    span = 8
    return pl.pallas_call(
        turn_kernel,
        grid=(devices // span,),
        out_shape=jax.ShapeDtypeStruct((devices, len(arrays), width, height), BF16),
        in_specs=[pl.BlockSpec((height, span * width), lambda i: (0, i))] * len(arrays),
        out_specs=pl.BlockSpec((span, len(arrays), width, height), lambda i: (i, 0, 0, 0)),
        cost_estimate=pl.CostEstimate(
            flops=0, bytes_accessed=4 * len(arrays) * height * channels, transcendentals=0
        ),
        name="to_blocks",
    )(*arrays)


def unturn_kernel(in_ref, *outs):
    blocks, _, width, height = in_ref.shape
    for k, out in enumerate(outs):
        block = in_ref[:, k].astype(F32).reshape(blocks * width, height)
        out[...] = block.T.astype(out.dtype)


def from_blocks(block, dtypes):
    devices, count, width, height = block.shape
    span = 8
    return pl.pallas_call(
        unturn_kernel,
        grid=(devices // span,),
        out_shape=[jax.ShapeDtypeStruct((height, devices * width), t) for t in dtypes],
        in_specs=[pl.BlockSpec((span, count, width, height), lambda i: (i, 0, 0, 0))],
        out_specs=[pl.BlockSpec((height, span * width), lambda i: (0, i))] * count,
        cost_estimate=pl.CostEstimate(
            flops=0, bytes_accessed=8 * count * height * devices * width, transcendentals=0
        ),
        name="from_blocks",
    )(block)


def per_device(
    out_grad, out_weight, outer_gate, long_out, inner_gate, conv_input,
    short_out, medium_out, long_filter, taps_short, taps_medium,
):
    height = out_grad.shape[0]
    channels = outer_gate.shape[1]
    devices = lax.axis_size("seq")
    width = channels // devices
    first, twists, forward, inverse, last, flip = tables(devices)

    both = jnp.broadcast_to(out_grad[None], (2, *out_grad.shape))
    features = lax.all_to_all(both, "ch", 0, 0, tiled=True)
    aligned = lax.all_to_all(out_weight, "ch", split_axis=1, concat_axis=0, tiled=True)
    weight = lax.all_gather(aligned, "seq", axis=0, tiled=True)

    early = to_blocks((inner_gate, medium_out, short_out, conv_input, long_filter), devices)
    early = lax.all_to_all(early, "seq", 0, 0, tiled=True)
    at = lax.axis_index("seq") * width
    own = [lax.dynamic_slice_in_dim(t, at, width, 1) for t in (taps_medium, taps_short)]
    own[1] = jnp.pad(own[1], ((0, MEDIUM - SHORT), (0, 0)))
    taps = jnp.stack([t.astype(F32).T for t in own])
    spec, gates, bands, turned = prepare(early, taps, first, twists, forward, flip)

    half = features.shape[2]
    hidden = jnp.dot(
        jnp.concatenate([features[0], features[1]], 1), weight, preferred_element_type=F32
    )
    grad_outer = (hidden * long_out.astype(F32)).astype(BF16)
    long_grad = (hidden * outer_gate.astype(F32)).astype(BF16)
    late = lax.all_to_all(to_blocks((long_grad,), devices), "seq", 0, 0, tiled=True)
    late = late.reshape(devices, width, height)
    results, sums = finish(
        late, spec, gates, bands, turned, first, twists, forward, inverse, last
    )
    results = lax.all_to_all(results, "seq", 0, 0, tiled=True)
    grad_inner, grad_input, grad_filter = from_blocks(results, (BF16, BF16, F32))
    factor = (height * devices) ** -0.5
    lags = jnp.concatenate(
        [sums[0, :, MEDIUM - 1 : 2 * MEDIUM - 1], sums[1, :, MEDIUM - 1 : MEDIUM - 1 + 8]], 1
    )
    lags = lax.all_gather(lags.T * factor, "seq", axis=1, tiled=True)
    return grad_outer, grad_inner, grad_input, grad_filter, lags[MEDIUM : MEDIUM + SHORT], lags[:MEDIUM]


def solution(mesh):
    rows = P("seq", "ch")
    return jax.shard_map(
        per_device,
        mesh=mesh,
        in_specs=(rows, P(("seq", "ch"), None)) + (rows,) * 7 + (P(None, "ch"),) * 2,
        out_specs=(rows,) * 4 + (P(None, "ch"),) * 2,
        check_vma=False,
    )
```

```python
import math

import jax
import jax.numpy as jnp
import numpy as np
from jax import lax
from jax.experimental import pallas as pl
from jax.experimental.pallas import tpu as pltpu
from jax.sharding import PartitionSpec as P

SHORT = 7
MEDIUM = 128
LANES = 128
F32 = jnp.float32
BF16 = jnp.bfloat16
VMEM_LIMIT = 60 * 1024 * 1024
PAD = 16
SIDE = 4
PLANE = SIDE * SIDE
MESH = pl.DeviceIdType.MESH


def split_np(table):
    high = table.astype(np.float32).astype(jnp.bfloat16)
    low = (table - high.astype(np.float64)).astype(np.float32).astype(jnp.bfloat16)
    return high, low


def tables(rows):
    total = 2 * rows * LANES
    freq = np.arange(rows)[:, None] + 0.5
    place = np.arange(rows)[None, :]
    angle = 2.0 * np.pi * freq * place / (2 * rows)
    first = np.concatenate([np.cos(angle), -np.sin(angle)], 0)
    first = np.concatenate(split_np(first), 1)
    twist = 2.0 * np.pi * freq * np.arange(LANES)[None, :] / total
    inner = 2.0 * np.pi * np.outer(np.arange(LANES), np.arange(LANES)) / LANES
    cosine, sine = np.cos(inner), np.sin(inner)
    forward = np.block([[cosine, -sine], [sine, cosine]])
    inverse = np.block([[cosine, sine], [-sine, cosine]])
    scale = (rows * LANES) ** -0.5 * 2.0 / total
    last = np.concatenate([np.cos(angle.T), -np.sin(angle.T)], 1) * scale
    twists = np.concatenate([np.cos(twist), np.sin(twist)], 1).astype(np.float32)
    flip = np.eye(LANES)[::-1].astype(jnp.bfloat16)
    return (
        first,
        twists,
        np.concatenate(split_np(forward), 0),
        np.concatenate(split_np(inverse), 0),
        np.concatenate(split_np(last), 0),
        flip,
    )


def dot(a, b):
    return jnp.dot(a, b, preferred_element_type=F32)


def dot_t(a, b):
    return lax.dot_general(a, b, (((1,), (1,)), ((), ())), preferred_element_type=F32)


def split(x):
    high = x.astype(BF16)
    return high, (x - high.astype(F32)).astype(BF16)


def dot3(high, low, table):
    size = table.shape[0] // 2
    return dot(high, table[:size]) + dot(high, table[size:]) + dot(low, table[:size])


def outer_stage(pair, first, twists):
    rows = pair.shape[0]
    spread = dot(first, jnp.concatenate([pair, pair], 0))
    cosine = jnp.concatenate([twists[:, :LANES]] * 2, 1)
    sine = jnp.concatenate([twists[:, LANES:]] * 2, 1)
    real, imag = spread[:rows], spread[rows:]
    new_real = real * cosine + imag * sine
    new_imag = imag * cosine - real * sine
    return (
        jnp.concatenate([new_real[:, :LANES], new_imag[:, :LANES]], 1),
        jnp.concatenate([new_real[:, LANES:], new_imag[:, LANES:]], 1),
    )


def toeplitz(line):
    row = jnp.concatenate([line, jnp.zeros_like(line)], 1)
    block = jnp.broadcast_to(row, (LANES, 2 * LANES))
    return pltpu.roll(block, 0, 1, stride=1, stride_axis=0)


def prepare_kernel(
    early_ref, taps_ref, first_ref, twists_ref, forward_ref, flip_ref,
    spec_ref, gates_ref, bands_ref, turned_ref,
    lines, zh, zl,
):
    rows, width = early_ref.shape[0], early_ref.shape[2]

    @pl.loop(0, rows)
    def _(i):
        at = pl.ds(pl.multiple_of(i * width, width), width)
        for k in range(5):
            lines[k, at, :] = early_ref[i, k].astype(F32)

    @pl.loop(0, width)
    def _(c):
        pick = pl.ds(c, rows, stride=width)
        inner, medium = lines[0, pick, :], lines[1, pick, :]
        mine = pl.ds(pl.multiple_of(c * rows, rows), rows)
        gates_ref[0, mine, :] = inner
        gates_ref[1, mine, :] = medium
        product = (inner * medium).astype(BF16)
        pair = jnp.concatenate([product, lines[4, pick, :].astype(BF16)], 1)
        for k, part in enumerate(outer_stage(pair, first_ref[...], twists_ref[...])):
            high, low = split(part)
            there = pl.ds(pl.multiple_of(k * rows * width + c * rows, rows), rows)
            zh[there, :] = high
            zl[there, :] = low
        wide = pl.ds(pl.multiple_of(c * LANES, LANES), LANES)
        for k in range(2):
            bands_ref[k, wide, :] = toeplitz(taps_ref[k, pl.ds(c, 1), :]).astype(BF16)
            saved = lines[2 + k, pick, :].astype(BF16)
            turned_ref[k, wide, :] = dot_t(flip_ref[...], saved).astype(BF16)

    step = 512

    @pl.loop(0, 2 * rows * width // step)
    def _(b):
        at = pl.ds(pl.multiple_of(b * step, step), step)
        spec_ref[at, :] = dot3(zh[at, :], zl[at, :], forward_ref[...])


def finish_kernel(
    late_ref, spec_ref, gates_ref, bands_ref, turned_ref,
    first_ref, twists_ref, forward_ref, inverse_ref, last_ref,
    out_ref,
    lines, zh, zl, ch, cl, results, sums,
):
    rows, width = late_ref.shape[0], late_ref.shape[1]
    high_row = rows - 1

    @pl.loop(0, rows)
    def _(i):
        at = pl.ds(pl.multiple_of(i * width, width), width)
        lines[at, :] = late_ref[i].astype(F32)

    @pl.loop(0, width // 2)
    def _(c):
        pair = jnp.concatenate(
            [lines[pl.ds(2 * c + k, rows, stride=width), :] for k in range(2)], 1
        ).astype(BF16)
        for k, part in enumerate(outer_stage(pair, first_ref[...], twists_ref[...])):
            high, low = split(part)
            there = pl.ds(pl.multiple_of((2 * c + k) * rows, rows), rows)
            zh[there, :] = high
            zl[there, :] = low

    many = 4
    step = many * rows

    @pl.loop(0, width // many)
    def _(b):
        at = pl.ds(pl.multiple_of(b * step, step), step)
        grad = dot3(zh[at, :], zl[at, :], forward_ref[...])
        grad_real, grad_imag = grad[:, :LANES], grad[:, LANES:]
        cosine = jnp.concatenate([twists_ref[:, :LANES]] * many, 0)
        sine = jnp.concatenate([twists_ref[:, LANES:]] * many, 0)
        reals, imags = [], []
        for k in range(2):
            source = 1 - k
            other = spec_ref[
                pl.ds(pl.multiple_of(source * rows * width + b * step, step), step), :
            ]
            real, imag = other[:, :LANES], other[:, LANES:]
            term = jnp.concatenate(
                [real * grad_real + imag * grad_imag, real * grad_imag - imag * grad_real], 1
            )
            back = dot3(*split(term), inverse_ref[...])
            real, imag = back[:, :LANES], back[:, LANES:]
            reals.append(real * cosine - imag * sine)
            imags.append(real * sine + imag * cosine)
        real, imag = jnp.concatenate(reals, 1), jnp.concatenate(imags, 1)
        for k in range(many):
            both = jnp.concatenate(
                [real[k * rows : (k + 1) * rows], imag[k * rows : (k + 1) * rows]], 0
            )
            high, low = split(both)
            there = pl.ds(
                pl.multiple_of((b * many + k) * 2 * rows, 2 * rows), 2 * rows
            )
            ch[there, :] = high
            cl[there, :] = low

    row = lax.broadcasted_iota(jnp.int32, (rows, LANES), 0)

    def with_next(x):
        following = jnp.where(row == high_row, 0.0, pltpu.roll(x, high_row, 0))
        return jnp.concatenate([x, following], 1).astype(BF16)

    def diagonals(c, k, both):
        wide = pl.ds(pl.multiple_of(c * LANES, LANES), LANES)
        products = dot(turned_ref[k, wide, :], both)
        slid = pltpu.roll(products, 0, 1, stride=1, stride_axis=0)
        return jnp.sum(slid, axis=0, keepdims=True)

    def channel(c):
        there = pl.ds(pl.multiple_of(c * 2 * rows, 2 * rows), 2 * rows)
        mine = pl.ds(pl.multiple_of(c * rows, rows), rows)
        wide = pl.ds(pl.multiple_of(c * LANES, LANES), LANES)
        high, low = ch[there, :], cl[there, :]
        point = dot(last_ref[:rows], high) + dot(last_ref[:rows], low) + dot(last_ref[rows:], high)
        point, filt = point[:, :LANES], point[:, LANES:]
        medium_grad = (point * gates_ref[0, mine, :]).astype(BF16).astype(F32)
        both = with_next(medium_grad)
        short_grad = dot_t(both, bands_ref[0, wide, :]).astype(BF16).astype(F32)
        pair = with_next(short_grad)
        grad_input = dot_t(pair, bands_ref[1, wide, :])
        pick = pl.ds(c, rows, stride=width)
        results[0, pick, :] = point * gates_ref[1, mine, :]
        results[1, pick, :] = grad_input
        results[2, pick, :] = filt
        sums[0, pl.ds(c, 1), :] = diagonals(c, 0, both)
        sums[1, pl.ds(c, 1), :] = diagonals(c, 1, pair)

    unroll = 4

    @pl.loop(0, width // unroll)
    def _(b):
        for k in range(unroll):
            channel(b * unroll + k)

    factor = (rows * LANES) ** -0.5
    lags = [pltpu.roll(sums[k], LANES + 1, 1)[:, :LANES] * factor for k in range(2)]
    medium = lags[0].astype(BF16)
    square = jnp.concatenate([lags[1], jnp.zeros((LANES - width, LANES), F32)], 0)
    short = square.T[:PAD].astype(BF16)

    @pl.loop(0, rows)
    def _(i):
        at = pl.ds(pl.multiple_of(i * width, width), width)
        for k in range(3):
            out_ref[i, k * width : (k + 1) * width] = results[k, at, :].astype(BF16)
        out_ref[i, 3 * width : 4 * width] = medium
        out_ref[i, 4 * width :] = short


def whole(n):
    return [pl.BlockSpec(memory_space=pltpu.VMEM)] * n


def prepare(early, taps, first, twists, forward, flip):
    rows, _, width, _ = early.shape
    area = rows * width
    return pl.pallas_call(
        prepare_kernel,
        out_shape=(
            jax.ShapeDtypeStruct((2 * area, 2 * LANES), F32),
            jax.ShapeDtypeStruct((2, area, LANES), F32),
            jax.ShapeDtypeStruct((2, width * LANES, 2 * LANES), BF16),
            jax.ShapeDtypeStruct((2, width * LANES, rows), BF16),
        ),
        in_specs=whole(6),
        out_specs=whole(4),
        scratch_shapes=[
            pltpu.VMEM((5, area, LANES), F32),
            pltpu.VMEM((2 * area, 2 * LANES), BF16),
            pltpu.VMEM((2 * area, 2 * LANES), BF16),
        ],
        compiler_params=pltpu.CompilerParams(vmem_limit_bytes=VMEM_LIMIT),
        cost_estimate=pl.CostEstimate(flops=4 * 10**9, bytes_accessed=20 * 2**20, transcendentals=0),
        name="prepare",
    )(early, taps, first, twists, forward, flip)


def finish(late, spec, gates, bands, turned, first, twists, forward, inverse, last):
    rows, width, _ = late.shape
    area = rows * width
    return pl.pallas_call(
        finish_kernel,
        out_shape=jax.ShapeDtypeStruct((rows, 4 * width + PAD, LANES), BF16),
        in_specs=whole(10),
        out_specs=whole(1)[0],
        scratch_shapes=[
            pltpu.VMEM((area, LANES), F32),
            pltpu.VMEM((area, 2 * LANES), BF16),
            pltpu.VMEM((area, 2 * LANES), BF16),
            pltpu.VMEM((2 * area, 2 * LANES), BF16),
            pltpu.VMEM((2 * area, 2 * LANES), BF16),
            pltpu.VMEM((3, area, LANES), F32),
            pltpu.VMEM((2, width, 2 * LANES), F32),
        ],
        compiler_params=pltpu.CompilerParams(vmem_limit_bytes=VMEM_LIMIT),
        cost_estimate=pl.CostEstimate(flops=8 * 10**9, bytes_accessed=20 * 2**20, transcendentals=0),
        name="finish",
    )(late, spec, gates, bands, turned, first, twists, forward, inverse, last)


def turn_kernel(*refs):
    *ins, out = refs
    _, blocks, _, _, width, _ = out.shape
    for k, ref in enumerate(ins):
        out[0, :, 0, k] = ref[...].astype(F32).T.astype(BF16).reshape(blocks, width, LANES)


def block_place(i):
    return i // 4, i % 2, (i // 2) % 2


def to_blocks(arrays, devices):
    height, channels = arrays[0].shape
    width = channels // devices
    span = PLANE // 2
    count = len(arrays)
    out = pl.pallas_call(
        turn_kernel,
        grid=(devices // span,),
        out_shape=jax.ShapeDtypeStruct((2, PLANE, 2, count, width, height), BF16),
        in_specs=[pl.BlockSpec((height, span * width), lambda i: (0, i))] * count,
        out_specs=pl.BlockSpec(
            (1, span, 1, count, width, height), lambda i: (*block_place(i), 0, 0, 0)
        ),
        cost_estimate=pl.CostEstimate(
            flops=0, bytes_accessed=4 * count * height * channels, transcendentals=0
        ),
        name="to_blocks",
    )(*arrays)
    return out.reshape(devices, count, width, height)


def unturn_kernel(in_ref, *outs):
    blocks, height = in_ref.shape[1], in_ref.shape[4]
    width = outs[0].shape[1] // blocks
    for k, out in enumerate(outs):
        block = in_ref[0, :, 0, k * width : (k + 1) * width].astype(F32)
        out[...] = block.reshape(blocks * width, height).T.astype(out.dtype)


def from_blocks(block, width, dtypes):
    devices, lines, height = block.shape
    span = PLANE // 2
    count = len(dtypes)
    return pl.pallas_call(
        unturn_kernel,
        grid=(devices // span,),
        out_shape=[jax.ShapeDtypeStruct((height, devices * width), t) for t in dtypes],
        in_specs=[
            pl.BlockSpec((1, span, 1, lines, height), lambda i: (*block_place(i), 0, 0))
        ],
        out_specs=[pl.BlockSpec((height, span * width), lambda i: (0, i))] * count,
        cost_estimate=pl.CostEstimate(
            flops=0, bytes_accessed=8 * count * height * devices * width, transcendentals=0
        ),
        name="from_blocks",
    )(block.reshape(2, PLANE, 2, lines, height))


def wrap(i):
    return lax.rem(i + SIDE, SIDE)


class Here:
    def __init__(self):
        seq = lax.axis_index("seq")
        self.y_hi = lax.axis_index("ch")
        self.core = seq % 2
        self.z = (seq // 2) % SIDE
        self.x = (seq // (2 * SIDE)) % SIDE
        self.y_lo = seq // (2 * PLANE)
        self.y = self.y_hi * 2 + self.y_lo

    def at(self, x=None, y=None, z=None, core=None):
        x = self.x if x is None else x
        y = self.y if y is None else y
        z = self.z if z is None else z
        core = self.core if core is None else core
        seq = (((y % 2) * SIDE + x) * SIDE + z) * 2 + core
        return {"seq": seq, "ch": y // 2}


def send(source, target, sends, recvs, device):
    copy = pltpu.make_async_remote_copy(
        src_ref=source,
        dst_ref=target,
        send_sem=sends,
        recv_sem=recvs,
        device_id=device,
        device_id_type=MESH,
    )
    copy.start()


def await_bytes(ref, sem):
    pltpu.make_async_copy(ref, ref, sem).wait()


class Ring:
    def __init__(self, here, axis, item, half, sends, recvs, source=None):
        self.at = lambda p: here.at(**{axis: p})
        self.place = getattr(here, axis)
        self.item, self.half = item, half
        self.sends, self.recvs = sends, recvs
        self.source = item(self.place) if source is None else source

    def step(self, i, source, target, to):
        send(source, target, self.sends.at[i], self.recvs.at[i], self.at(wrap(self.place + to)))

    def start(self):
        self.step(0, self.source, self.item(self.place), 1)
        self.step(1, self.source, self.item(self.place), -1)

    def relay(self):
        for i, to in ((0, 1), (1, -1)):
            other = wrap(self.place - to)
            await_bytes(self.item(other), self.recvs.at[i])
            half = self.half(self.item(other), i)
            self.step(2 + i, half, half, to)

    def finish(self):
        opposite = self.item(wrap(self.place + 2))
        for i in range(2):
            await_bytes(self.half(opposite, i), self.recvs.at[2 + i])

    def drain(self):
        opposite = self.item(wrap(self.place + 2))
        for i in range(2):
            await_bytes(self.item(self.place), self.sends.at[i])
            await_bytes(self.half(opposite, i), self.sends.at[2 + i])


def project_kernel(
    grad_ref, weight_ref, gate_ref, long_ref,
    outer_ref, late_ref,
    feats, weights, gates, total, turned, hidden, arrived,
    local, spread_s, spread_r, gate_s, gate_r, feat_s, feat_r, pass_s, pass_r,
    ring_s, ring_r, late_s, late_r, back_s, back_r,
):
    here = Here()
    me = here.y_lo * 2 + here.core
    cell = here.x * SIDE + here.z
    columns = gates.shape[2]
    height = grad_ref.shape[0]

    def column_peers():
        for dy in range(SIDE):
            for dc in range(2):
                if dy or dc:
                    yield dy * 2 + dc - 1, wrap(here.y + dy), (here.core + dc) % 2

    def plane_peers():
        for dx in range(SIDE):
            for dz in range(SIDE):
                if dx or dz:
                    yield dx * SIDE + dz - 1, wrap(here.x + dx), wrap(here.z + dz)

    barrier = pltpu.get_barrier_semaphore()
    for _, y, core in column_peers():
        pl.semaphore_signal(barrier, 1, device_id=here.at(y=y, core=core), device_id_type=MESH)
    for _, x, z in plane_peers():
        pl.semaphore_signal(barrier, 1, device_id=here.at(x=x, z=z), device_id_type=MESH)
    pl.semaphore_wait(barrier, 22)

    def weight_columns(y, core):
        return weight_ref.at[:, pl.ds(pl.multiple_of((y * 2 + core) * columns, columns), columns)]

    def gate_columns(index):
        return gate_ref.at[:, pl.ds(pl.multiple_of(index * columns, columns), columns)]

    row_block = here.core * 2 + here.y_hi
    own_rows = weights.at[here.y_lo, here.x, here.z, row_block]
    for i, y, core in column_peers():
        send(weight_columns(y, core), own_rows, spread_s.at[i], spread_r.at[i], here.at(y=y, core=core))
    copies = [
        pltpu.make_async_copy(weight_columns(here.y, here.core), own_rows, local.at[0]),
        pltpu.make_async_copy(grad_ref, feats.at[here.y_hi, me], local.at[1]),
        pltpu.make_async_copy(gate_columns(me), gates.at[me], local.at[2]),
    ]
    for copy in copies:
        copy.start()

    def half_tokens(ref, i):
        return ref.at[pl.ds(i * (height // 2), height // 2)]

    features = Ring(
        here, "y", lambda y: feats.at[y // 2, (y % 2) * 2 + here.core], half_tokens,
        feat_s, feat_r, source=grad_ref,
    )
    features.start()
    partner = here.at(core=1 - here.core)

    def feat(y, core):
        return feats.at[y // 2, (y % 2) * 2 + core]

    def pass_on(i, y):
        send(grad_ref if i == 0 else feat(y, here.core), feat(y, here.core), pass_s.at[i], pass_r.at[i], partner)

    pass_on(0, here.y)
    share = [(0, 1), (1, 0), (1, 1)]
    for i, (dy, dc) in enumerate(share):
        y_lo, core = (here.y_lo + dy) % 2, (here.core + dc) % 2
        send(
            gate_columns(y_lo * 2 + core), gates.at[me], gate_s.at[i], gate_r.at[i],
            here.at(y=here.y_hi * 2 + y_lo, core=core),
        )

    for i, y, core in column_peers():
        source_y, source_core = wrap(2 * here.y - y + SIDE), core
        await_bytes(
            weights.at[source_y % 2, here.x, here.z, source_core * 2 + source_y // 2],
            spread_r.at[i],
        )
    copies[0].wait()

    def half_block(ref, i):
        return ref.at[pl.ds(i * 2, 2)]

    def block_ring(k, axis, item):
        return Ring(here, axis, item, half_block, ring_s.at[k], ring_r.at[k])

    first = [
        block_ring(0, "x", lambda x: weights.at[0, x, here.z]),
        block_ring(1, "z", lambda z: weights.at[1, here.x, z]),
    ]
    order = (0, 3, 1, 2)
    second = []
    for j, d in enumerate(order):
        second.append((
            block_ring(2 + 2 * j, "z", lambda z, d=d: weights.at[0, wrap(here.x + d), z]),
            block_ring(3 + 2 * j, "x", lambda x, d=d: weights.at[1, x, wrap(here.z + d)]),
        ))
    for ring in first:
        ring.start()
    for ring in second[0]:
        ring.start()
    for ring in first:
        ring.relay()
    for pair in second[1:3]:
        for ring in pair:
            ring.start()
    for ring in second[0]:
        ring.relay()
    for ring in first:
        ring.finish()
    for ring in second[3]:
        ring.start()
    features.relay()
    pass_on(1, wrap(here.y - 1))
    pass_on(2, wrap(here.y + 1))
    for pair in second[1:]:
        for ring in pair:
            ring.relay()
    features.finish()
    pass_on(3, wrap(here.y + 2))
    for pair in second:
        for ring in pair:
            ring.finish()
    for i, d in enumerate((0, -1, 1, 2)):
        await_bytes(feat(wrap(here.y + d), 1 - here.core), pass_r.at[i])
    copies[1].wait()

    depth = SIDE * weights.shape[3] * weights.shape[4]
    for h in range(2):
        @pl.loop(0, SIDE)
        def _(x):
            part = pl.ds(pl.multiple_of(x * depth, depth), depth)
            left = feats[h, :, :, part].reshape(4 * height, depth)
            term = dot(left, weights[h, x].reshape(depth, columns))
            if h == 0:
                @pl.when(x == 0)
                def _():
                    total[...] = term

                @pl.when(x > 0)
                def _():
                    total[...] += term
            else:
                total[...] += term

    copies[2].wait()
    for i, (dy, dc) in enumerate(share):
        source = ((here.y_lo + dy) % 2) * 2 + (here.core + dc) % 2
        await_bytes(gates.at[source], gate_r.at[i])
    width = late_ref.shape[3]
    for g in range(4):
        part = total[g * height : (g + 1) * height]
        long_grad = (part * gates[g].astype(F32)).astype(BF16).astype(F32)
        turned[:, g // 2, g % 2] = long_grad.T.astype(BF16).reshape(PLANE, width, height)
        hidden[g] = part.astype(BF16)
    keep = pltpu.make_async_copy(turned.at[cell], late_ref.at[:, cell], local.at[0])
    keep.start()
    for i, x, z in plane_peers():
        send(turned.at[x * SIDE + z], late_ref.at[:, cell], late_s.at[i], late_r.at[i], here.at(x=x, z=z))
    for i, (dy, dc) in enumerate(share):
        y_lo, core = (here.y_lo + dy) % 2, (here.core + dc) % 2
        send(
            hidden.at[y_lo * 2 + core], arrived.at[me], back_s.at[i], back_r.at[i],
            here.at(y=here.y_hi * 2 + y_lo, core=core),
        )
    own = pltpu.make_async_copy(hidden.at[me], arrived.at[me], local.at[1])
    own.start()
    own.wait()
    for i, (dy, dc) in enumerate(share):
        source = ((here.y_lo + dy) % 2) * 2 + (here.core + dc) % 2
        await_bytes(arrived.at[source], back_r.at[i])
    for g in range(4):
        part = slice(g * columns, (g + 1) * columns)
        outer_ref[:, part] = (arrived[g].astype(F32) * long_ref[:, part].astype(F32)).astype(BF16)
    keep.wait()
    for i, x, z in plane_peers():
        source = wrap(2 * here.x - x + SIDE) * SIDE + wrap(2 * here.z - z + SIDE)
        await_bytes(late_ref.at[:, source], late_r.at[i])

    for i in range(7):
        await_bytes(own_rows, spread_s.at[i])
    for i in range(3):
        await_bytes(gates.at[me], gate_s.at[i])
        await_bytes(hidden.at[me], back_s.at[i])
    for i in range(4):
        await_bytes(feats.at[0, 0], pass_s.at[i])
    for i in range(15):
        await_bytes(turned.at[0], late_s.at[i])
    features.drain()
    for ring in first:
        ring.drain()
    for pair in second:
        for ring in pair:
            ring.drain()


def project(out_grad, out_weight, outer_gate, long_out):
    height, half = out_grad.shape
    rows, model = out_weight.shape
    columns = model // 8
    width = columns // PLANE
    dma = pltpu.SemaphoreType.DMA
    anywhere = pl.BlockSpec(memory_space=pl.ANY)
    in_vmem = pl.BlockSpec(memory_space=pltpu.VMEM)
    outer, late = pl.pallas_call(
        project_kernel,
        out_shape=(
            jax.ShapeDtypeStruct((height, half), BF16),
            jax.ShapeDtypeStruct((2, PLANE, 2, width, height), BF16),
        ),
        in_specs=[anywhere, anywhere, anywhere, in_vmem],
        out_specs=(in_vmem, in_vmem),
        scratch_shapes=[
            pltpu.VMEM((2, 4, height, half), BF16),
            pltpu.VMEM((2, SIDE, SIDE, 4, rows, columns), BF16),
            pltpu.VMEM((4, height, columns), BF16),
            pltpu.VMEM((4 * height, columns), F32),
            pltpu.VMEM((PLANE, 2, 2, width, height), BF16),
            pltpu.VMEM((4, height, columns), BF16),
            pltpu.VMEM((4, height, columns), BF16),
            dma((3,)), dma((7,)), dma((7,)), dma((3,)), dma((3,)), dma((4,)), dma((4,)),
            dma((4,)), dma((4,)), dma((10, 4)), dma((10, 4)), dma((15,)), dma((15,)),
            dma((3,)), dma((3,)),
        ],
        compiler_params=pltpu.CompilerParams(
            collective_id=0, has_side_effects=True, vmem_limit_bytes=40 * 1024 * 1024
        ),
        cost_estimate=pl.CostEstimate(
            flops=2 * 4 * height * model * columns, bytes_accessed=16 * 2**20, transcendentals=0
        ),
        name="project",
    )(out_grad, out_weight, outer_gate, long_out)
    return outer, late.reshape(4 * PLANE, width, height)


def per_device(
    out_grad, out_weight, outer_gate, long_out, inner_gate, conv_input,
    short_out, medium_out, long_filter, taps_short, taps_medium,
):
    height, channels = outer_gate.shape
    devices = lax.axis_size("seq")
    width = channels // devices
    first, twists, forward, inverse, last, flip = tables(devices)

    early = to_blocks((inner_gate, medium_out, short_out, conv_input, long_filter), devices)
    early = lax.all_to_all(early, "seq", 0, 0, tiled=True)
    here = Here()
    at = (((here.y_lo * 2 + here.core) * SIDE + here.x) * SIDE + here.z) * width
    own = [lax.dynamic_slice_in_dim(t, at, width, 1) for t in (taps_medium, taps_short)]
    own[1] = jnp.pad(own[1], ((0, MEDIUM - SHORT), (0, 0)))
    taps = jnp.stack([t.astype(F32).T for t in own])
    grad_outer, late = project(out_grad, out_weight, outer_gate, long_out)
    spec, gates, bands, turned = prepare(early, taps, first, twists, forward, flip)
    results = finish(late, spec, gates, bands, turned, first, twists, forward, inverse, last)
    results = lax.all_to_all(results, "seq", 0, 0, tiled=True)
    grad_inner, grad_input, grad_filter, grad_medium = from_blocks(
        results, width, (BF16, BF16, F32, F32)
    )
    short = results[:, 4 * width : 4 * width + SHORT, :width]
    short = short.reshape(2, PLANE, 2, SHORT, width).transpose(3, 0, 2, 1, 4)
    grad_short = short.reshape(SHORT, channels).astype(F32)
    return grad_outer, grad_inner, grad_input, grad_filter, grad_short, grad_medium


def solution(mesh):
    rows = P("seq", "ch")
    return jax.shard_map(
        per_device,
        mesh=mesh,
        in_specs=(rows, P(("seq", "ch"), None)) + (rows,) * 7 + (P(None, "ch"),) * 2,
        out_specs=(rows,) * 4 + (P(None, "ch"),) * 2,
        check_vma=False,
    )
```

```python
import math

import jax
import jax.numpy as jnp
import numpy as np
from jax import lax
from jax.experimental import pallas as pl
from jax.experimental.pallas import tpu as pltpu
from jax.sharding import PartitionSpec as P

SHORT = 7
MEDIUM = 128
LANES = 128
F32 = jnp.float32
BF16 = jnp.bfloat16
VMEM_LIMIT = 60 * 1024 * 1024
PAD = 16
SIDE = 4
PLANE = SIDE * SIDE
MESH = pl.DeviceIdType.MESH


def split_np(table):
    high = table.astype(np.float32).astype(jnp.bfloat16)
    low = (table - high.astype(np.float64)).astype(np.float32).astype(jnp.bfloat16)
    return high, low


def tables(rows):
    total = 2 * rows * LANES
    freq = np.arange(rows)[:, None] + 0.5
    place = np.arange(rows)[None, :]
    angle = 2.0 * np.pi * freq * place / (2 * rows)
    first = np.concatenate([np.cos(angle), -np.sin(angle)], 0)
    first = np.concatenate(split_np(first), 1)
    twist = 2.0 * np.pi * freq * np.arange(LANES)[None, :] / total
    inner = 2.0 * np.pi * np.outer(np.arange(LANES), np.arange(LANES)) / LANES
    cosine, sine = np.cos(inner), np.sin(inner)
    forward = np.block([[cosine, -sine], [sine, cosine]])
    inverse = np.block([[cosine, sine], [-sine, cosine]])
    scale = (rows * LANES) ** -0.5 * 2.0 / total
    last = np.concatenate([np.cos(angle.T), -np.sin(angle.T)], 1) * scale
    twists = np.concatenate([np.cos(twist), np.sin(twist)], 1).astype(np.float32)
    flip = np.eye(LANES)[::-1].astype(jnp.bfloat16)
    return (
        first,
        twists,
        np.concatenate(split_np(forward), 0),
        np.concatenate(split_np(inverse), 0),
        np.concatenate(split_np(last), 0),
        flip,
    )


def dot(a, b):
    return jnp.dot(a, b, preferred_element_type=F32)


def dot_t(a, b):
    return lax.dot_general(a, b, (((1,), (1,)), ((), ())), preferred_element_type=F32)


def split(x):
    high = x.astype(BF16)
    return high, (x - high.astype(F32)).astype(BF16)


def dot3(high, low, table):
    size = table.shape[0] // 2
    return dot(high, table[:size]) + dot(high, table[size:]) + dot(low, table[:size])


def outer_stage(pair, first, twists):
    rows = pair.shape[0]
    spread = dot(first, jnp.concatenate([pair, pair], 0))
    cosine = jnp.concatenate([twists[:, :LANES]] * 2, 1)
    sine = jnp.concatenate([twists[:, LANES:]] * 2, 1)
    real, imag = spread[:rows], spread[rows:]
    new_real = real * cosine + imag * sine
    new_imag = imag * cosine - real * sine
    return (
        jnp.concatenate([new_real[:, :LANES], new_imag[:, :LANES]], 1),
        jnp.concatenate([new_real[:, LANES:], new_imag[:, LANES:]], 1),
    )


def toeplitz(line):
    row = jnp.concatenate([line, jnp.zeros_like(line)], 1)
    block = jnp.broadcast_to(row, (LANES, 2 * LANES))
    return pltpu.roll(block, 0, 1, stride=1, stride_axis=0)


def prepare_kernel(
    early_ref, taps_ref, first_ref, twists_ref, forward_ref, flip_ref,
    spec_ref, gates_ref, bands_ref, turned_ref,
    lines, zh, zl,
):
    rows, width = early_ref.shape[0], early_ref.shape[2]

    @pl.loop(0, rows)
    def _(i):
        at = pl.ds(pl.multiple_of(i * width, width), width)
        for k in range(5):
            lines[k, at, :] = early_ref[i, k].astype(F32)

    @pl.loop(0, width)
    def _(c):
        pick = pl.ds(c, rows, stride=width)
        inner, medium = lines[0, pick, :], lines[1, pick, :]
        mine = pl.ds(pl.multiple_of(c * rows, rows), rows)
        gates_ref[0, mine, :] = inner
        gates_ref[1, mine, :] = medium
        product = (inner * medium).astype(BF16)
        pair = jnp.concatenate([product, lines[4, pick, :].astype(BF16)], 1)
        for k, part in enumerate(outer_stage(pair, first_ref[...], twists_ref[...])):
            high, low = split(part)
            there = pl.ds(pl.multiple_of(k * rows * width + c * rows, rows), rows)
            zh[there, :] = high
            zl[there, :] = low
        wide = pl.ds(pl.multiple_of(c * LANES, LANES), LANES)
        for k in range(2):
            bands_ref[k, wide, :] = toeplitz(taps_ref[k, pl.ds(c, 1), :]).astype(BF16)
            saved = lines[2 + k, pick, :].astype(BF16)
            turned_ref[k, wide, :] = dot_t(flip_ref[...], saved).astype(BF16)

    step = 512

    @pl.loop(0, 2 * rows * width // step)
    def _(b):
        at = pl.ds(pl.multiple_of(b * step, step), step)
        spec_ref[at, :] = dot3(zh[at, :], zl[at, :], forward_ref[...])


def finish_kernel(
    late_ref, spec_ref, gates_ref, bands_ref, turned_ref,
    first_ref, twists_ref, forward_ref, inverse_ref, last_ref,
    back_ref,
    lines, zh, zl, ch, cl, results, sums, parcels,
    local, sends, recvs,
):
    rows, width = late_ref.shape[0], late_ref.shape[1]
    chunk = parcels.shape[3]
    high_row = rows - 1
    here = Here()
    me = here.seq

    def target(i):
        return here.token_peer(i)

    def origin(i):
        return here.token_peer(i, -1)

    barrier = pltpu.get_barrier_semaphore()

    @pl.loop(1, rows)
    def _(i):
        pl.semaphore_signal(
            barrier, 1, device_id={"seq": target(i), "ch": here.y_hi}, device_id_type=MESH
        )

    @pl.loop(0, rows)
    def _(i):
        at = pl.ds(pl.multiple_of(i * width, width), width)
        lines[at, :] = late_ref[i].astype(F32)

    many = 4
    step = many * rows
    row = lax.broadcasted_iota(jnp.int32, (rows, LANES), 0)

    def with_next(x):
        following = jnp.where(row == high_row, 0.0, pltpu.roll(x, high_row, 0))
        return jnp.concatenate([x, following], 1).astype(BF16)

    def diagonals(wide, k, both):
        products = dot(turned_ref[k, wide, :], both)
        slid = pltpu.roll(products, 0, 1, stride=1, stride_axis=0)
        return jnp.sum(slid, axis=0, keepdims=True)

    def channel(c, within):
        there = pl.ds(pl.multiple_of(within * 2 * rows, 2 * rows), 2 * rows)
        mine = pl.ds(pl.multiple_of(c * rows, rows), rows)
        wide = pl.ds(pl.multiple_of(c * LANES, LANES), LANES)
        high, low = ch[there, :], cl[there, :]
        point = dot(last_ref[:rows], high) + dot(last_ref[:rows], low) + dot(last_ref[rows:], high)
        point, filt = point[:, :LANES], point[:, LANES:]
        medium_grad = (point * gates_ref[0, mine, :]).astype(BF16).astype(F32)
        both = with_next(medium_grad)
        short_grad = dot_t(both, bands_ref[0, wide, :]).astype(BF16).astype(F32)
        pair = with_next(short_grad)
        grad_input = dot_t(pair, bands_ref[1, wide, :])
        pick = pl.ds(within, rows, stride=chunk)
        results[0, pick, :] = point * gates_ref[1, mine, :]
        results[1, pick, :] = grad_input
        results[2, pick, :] = filt
        sums[0, pl.ds(c, 1), :] = diagonals(wide, 0, both)
        sums[1, pl.ds(c, 1), :] = diagonals(wide, 1, pair)

    def compute(start):
        @pl.loop(0, chunk // 2)
        def _(c):
            pair = jnp.concatenate(
                [lines[pl.ds(start + 2 * c + k, rows, stride=width), :] for k in range(2)], 1
            ).astype(BF16)
            for k, part in enumerate(outer_stage(pair, first_ref[...], twists_ref[...])):
                high, low = split(part)
                there = pl.ds(pl.multiple_of((2 * c + k) * rows, rows), rows)
                zh[there, :] = high
                zl[there, :] = low

        @pl.loop(0, chunk // many)
        def _(b):
            at = pl.ds(pl.multiple_of(b * step, step), step)
            grad = dot3(zh[at, :], zl[at, :], forward_ref[...])
            grad_real, grad_imag = grad[:, :LANES], grad[:, LANES:]
            cosine = jnp.concatenate([twists_ref[:, :LANES]] * many, 0)
            sine = jnp.concatenate([twists_ref[:, LANES:]] * many, 0)
            reals, imags = [], []
            for k in range(2):
                place = (1 - k) * rows * width + start * rows + b * step
                other = spec_ref[pl.ds(pl.multiple_of(place, step), step), :]
                real, imag = other[:, :LANES], other[:, LANES:]
                term = jnp.concatenate(
                    [real * grad_real + imag * grad_imag, real * grad_imag - imag * grad_real], 1
                )
                back = dot3(*split(term), inverse_ref[...])
                real, imag = back[:, :LANES], back[:, LANES:]
                reals.append(real * cosine - imag * sine)
                imags.append(real * sine + imag * cosine)
            real, imag = jnp.concatenate(reals, 1), jnp.concatenate(imags, 1)
            for k in range(many):
                both = jnp.concatenate(
                    [real[k * rows : (k + 1) * rows], imag[k * rows : (k + 1) * rows]], 0
                )
                high, low = split(both)
                there = pl.ds(
                    pl.multiple_of((b * many + k) * 2 * rows, 2 * rows), 2 * rows
                )
                ch[there, :] = high
                cl[there, :] = low

        @pl.loop(0, chunk // many)
        def _(b):
            for k in range(many):
                within = b * many + k
                channel(start + within, within)

    factor = (rows * LANES) ** -0.5
    parts = back_ref.shape[1]

    def parcel(ref, k):
        return ref.at[k] if k == parts - 1 else ref.at[k, pl.ds(0, 4)]

    for k in range(parts):
        compute(k * chunk)
        lags = pltpu.roll(sums[0, k * chunk : (k + 1) * chunk], LANES + 1, 1)[:, :LANES]
        medium = (lags * factor).astype(BF16)
        if k == parts - 1:
            lags = pltpu.roll(sums[1], LANES + 1, 1)[:, :LANES] * factor
            square = jnp.concatenate([lags, jnp.zeros((LANES - width, LANES), F32)], 0)
            short = square.T[:chunk].astype(BF16)

        @pl.loop(0, rows)
        def _(i):
            at = pl.ds(pl.multiple_of(i * chunk, chunk), chunk)
            for a in range(3):
                parcels[i, k, a] = results[a, at, :].astype(BF16)
            parcels[i, k, 3] = medium
            if k == parts - 1:
                parcels[i, k, 4] = short

        if k == 0:
            pl.semaphore_wait(barrier, rows - 1)

        @pl.loop(1, rows)
        def _(i):
            to = target(i)
            send(
                parcel(parcels.at[to], k), parcel(back_ref.at[me], k),
                sends.at[k, i], recvs.at[k, i], {"seq": to, "ch": here.y_hi},
            )

        pltpu.make_async_copy(
            parcel(parcels.at[me], k), parcel(back_ref.at[me], k), local.at[k]
        ).start()

    for k in range(parts):
        await_bytes(parcel(back_ref.at[me], k), local.at[k])

        @pl.loop(1, rows)
        def _(i):
            await_bytes(parcel(back_ref.at[origin(i)], k), recvs.at[k, i])
            await_bytes(parcel(parcels.at[me], k), sends.at[k, i])


def whole(n):
    return [pl.BlockSpec(memory_space=pltpu.VMEM)] * n


def prepare(early, taps, first, twists, forward, flip):
    rows, _, width, _ = early.shape
    area = rows * width
    return pl.pallas_call(
        prepare_kernel,
        out_shape=(
            jax.ShapeDtypeStruct((2 * area, 2 * LANES), F32),
            jax.ShapeDtypeStruct((2, area, LANES), F32),
            jax.ShapeDtypeStruct((2, width * LANES, 2 * LANES), BF16),
            jax.ShapeDtypeStruct((2, width * LANES, rows), BF16),
        ),
        in_specs=whole(6),
        out_specs=whole(4),
        scratch_shapes=[
            pltpu.VMEM((5, area, LANES), F32),
            pltpu.VMEM((2 * area, 2 * LANES), BF16),
            pltpu.VMEM((2 * area, 2 * LANES), BF16),
        ],
        compiler_params=pltpu.CompilerParams(vmem_limit_bytes=VMEM_LIMIT),
        cost_estimate=pl.CostEstimate(flops=4 * 10**9, bytes_accessed=20 * 2**20, transcendentals=0),
        name="prepare",
    )(early, taps, first, twists, forward, flip)


def finish(late, spec, gates, bands, turned, first, twists, forward, inverse, last):
    rows, width, _ = late.shape
    area = rows * width
    chunk = width // 2
    dma = pltpu.SemaphoreType.DMA
    return pl.pallas_call(
        finish_kernel,
        out_shape=jax.ShapeDtypeStruct((rows, 2, 5, chunk, LANES), BF16),
        in_specs=whole(10),
        out_specs=pl.BlockSpec(memory_space=pl.ANY),
        scratch_shapes=[
            pltpu.VMEM((area, LANES), F32),
            pltpu.VMEM((area // 2, 2 * LANES), BF16),
            pltpu.VMEM((area // 2, 2 * LANES), BF16),
            pltpu.VMEM((area, 2 * LANES), BF16),
            pltpu.VMEM((area, 2 * LANES), BF16),
            pltpu.VMEM((3, area // 2, LANES), F32),
            pltpu.VMEM((2, width, 2 * LANES), F32),
            pltpu.VMEM((rows, 2, 5, chunk, LANES), BF16),
            dma((2,)), dma((2, rows)), dma((2, rows)),
        ],
        compiler_params=pltpu.CompilerParams(
            collective_id=1, has_side_effects=True, vmem_limit_bytes=VMEM_LIMIT
        ),
        cost_estimate=pl.CostEstimate(flops=8 * 10**9, bytes_accessed=20 * 2**20, transcendentals=0),
        name="finish",
    )(late, spec, gates, bands, turned, first, twists, forward, inverse, last)


def turn_kernel(*refs):
    *ins, out = refs
    _, blocks, _, _, width, _ = out.shape
    for k, ref in enumerate(ins):
        out[0, :, 0, k] = ref[...].astype(F32).T.astype(BF16).reshape(blocks, width, LANES)


def block_place(i):
    return i // 4, i % 2, (i // 2) % 2


def to_blocks(arrays, devices):
    height, channels = arrays[0].shape
    width = channels // devices
    span = PLANE // 2
    count = len(arrays)
    out = pl.pallas_call(
        turn_kernel,
        grid=(devices // span,),
        out_shape=jax.ShapeDtypeStruct((2, PLANE, 2, count, width, height), BF16),
        in_specs=[pl.BlockSpec((height, span * width), lambda i: (0, i))] * count,
        out_specs=pl.BlockSpec(
            (1, span, 1, count, width, height), lambda i: (*block_place(i), 0, 0, 0)
        ),
        cost_estimate=pl.CostEstimate(
            flops=0, bytes_accessed=4 * count * height * channels, transcendentals=0
        ),
        name="to_blocks",
    )(*arrays)
    return out.reshape(devices, count, width, height)


def unturn_kernel(in_ref, *outs):
    height = in_ref.shape[6]
    for k, out in enumerate(outs):
        block = in_ref[0, :, 0, :, k].astype(F32)
        out[...] = block.reshape(out.shape[1], height).T.astype(out.dtype)


def from_blocks(block, dtypes):
    devices, parts, items, chunk, height = block.shape
    span = PLANE // 2
    count = len(dtypes)
    width = parts * chunk
    return pl.pallas_call(
        unturn_kernel,
        grid=(devices // span,),
        out_shape=[jax.ShapeDtypeStruct((height, devices * width), t) for t in dtypes],
        in_specs=[
            pl.BlockSpec(
                (1, span, 1, parts, items, chunk, height),
                lambda i: (*block_place(i), 0, 0, 0, 0),
            )
        ],
        out_specs=[pl.BlockSpec((height, span * width), lambda i: (0, i))] * count,
        cost_estimate=pl.CostEstimate(
            flops=0, bytes_accessed=8 * count * height * devices * width, transcendentals=0
        ),
        name="from_blocks",
    )(block.reshape(2, PLANE, 2, parts, items, chunk, height))


def wrap(i):
    return lax.rem(i + SIDE, SIDE)


class Here:
    def __init__(self):
        seq = lax.axis_index("seq")
        self.seq = seq
        self.y_hi = lax.axis_index("ch")
        self.core = seq % 2
        self.z = (seq // 2) % SIDE
        self.x = (seq // (2 * SIDE)) % SIDE
        self.y_lo = seq // (2 * PLANE)
        self.y = self.y_hi * 2 + self.y_lo

    def token_peer(self, i, sign=1):
        core = (self.core + i) % 2
        z = wrap(self.z + sign * ((i // 2) % SIDE))
        x = wrap(self.x + sign * ((i // (2 * SIDE)) % SIDE))
        y_lo = (self.y_lo + i // (2 * PLANE)) % 2
        return ((y_lo * SIDE + x) * SIDE + z) * 2 + core

    def at(self, x=None, y=None, z=None, core=None):
        x = self.x if x is None else x
        y = self.y if y is None else y
        z = self.z if z is None else z
        core = self.core if core is None else core
        seq = (((y % 2) * SIDE + x) * SIDE + z) * 2 + core
        return {"seq": seq, "ch": y // 2}


def send(source, target, sends, recvs, device):
    copy = pltpu.make_async_remote_copy(
        src_ref=source,
        dst_ref=target,
        send_sem=sends,
        recv_sem=recvs,
        device_id=device,
        device_id_type=MESH,
    )
    copy.start()


def await_bytes(ref, sem):
    pltpu.make_async_copy(ref, ref, sem).wait()


class Ring:
    def __init__(self, here, axis, item, half, sends, recvs, source=None):
        self.at = lambda p: here.at(**{axis: p})
        self.place = getattr(here, axis)
        self.item, self.half = item, half
        self.sends, self.recvs = sends, recvs
        self.source = item(self.place) if source is None else source

    def step(self, i, source, target, to):
        send(source, target, self.sends.at[i], self.recvs.at[i], self.at(wrap(self.place + to)))

    def start(self):
        self.step(0, self.source, self.item(self.place), 1)
        self.step(1, self.source, self.item(self.place), -1)

    def relay(self):
        for i, to in ((0, 1), (1, -1)):
            other = wrap(self.place - to)
            await_bytes(self.item(other), self.recvs.at[i])
            half = self.half(self.item(other), i)
            self.step(2 + i, half, half, to)

    def finish(self):
        opposite = self.item(wrap(self.place + 2))
        for i in range(2):
            await_bytes(self.half(opposite, i), self.recvs.at[2 + i])

    def drain(self):
        opposite = self.item(wrap(self.place + 2))
        for i in range(2):
            await_bytes(self.item(self.place), self.sends.at[i])
            await_bytes(self.half(opposite, i), self.sends.at[2 + i])


def project_kernel(
    grad_ref, weight_ref, gate_ref, long_ref,
    outer_ref, late_ref,
    feats, weights, gates, total, turned, hidden, arrived,
    local, spread_s, spread_r, gate_s, gate_r, feat_s, feat_r, pass_s, pass_r,
    ring_s, ring_r, late_s, late_r, back_s, back_r,
):
    here = Here()
    me = here.y_lo * 2 + here.core
    cell = here.x * SIDE + here.z
    columns = gates.shape[2]
    height = grad_ref.shape[0]

    def column_peers():
        for dy in range(SIDE):
            for dc in range(2):
                if dy or dc:
                    yield dy * 2 + dc - 1, wrap(here.y + dy), (here.core + dc) % 2

    def plane_peers():
        for dx in range(SIDE):
            for dz in range(SIDE):
                if dx or dz:
                    yield dx * SIDE + dz - 1, wrap(here.x + dx), wrap(here.z + dz)

    barrier = pltpu.get_barrier_semaphore()
    for _, y, core in column_peers():
        pl.semaphore_signal(barrier, 1, device_id=here.at(y=y, core=core), device_id_type=MESH)
    for _, x, z in plane_peers():
        pl.semaphore_signal(barrier, 1, device_id=here.at(x=x, z=z), device_id_type=MESH)
    pl.semaphore_wait(barrier, 22)

    def weight_columns(y, core):
        return weight_ref.at[:, pl.ds(pl.multiple_of((y * 2 + core) * columns, columns), columns)]

    def gate_columns(index):
        return gate_ref.at[:, pl.ds(pl.multiple_of(index * columns, columns), columns)]

    row_block = here.core * 2 + here.y_hi
    own_rows = weights.at[here.y_lo, here.x, here.z, row_block]
    for i, y, core in column_peers():
        send(weight_columns(y, core), own_rows, spread_s.at[i], spread_r.at[i], here.at(y=y, core=core))
    copies = [
        pltpu.make_async_copy(weight_columns(here.y, here.core), own_rows, local.at[0]),
        pltpu.make_async_copy(grad_ref, feats.at[here.y_hi, me], local.at[1]),
        pltpu.make_async_copy(gate_columns(me), gates.at[me], local.at[2]),
    ]
    for copy in copies:
        copy.start()

    def half_tokens(ref, i):
        return ref.at[pl.ds(i * (height // 2), height // 2)]

    features = Ring(
        here, "y", lambda y: feats.at[y // 2, (y % 2) * 2 + here.core], half_tokens,
        feat_s, feat_r, source=grad_ref,
    )
    features.start()
    partner = here.at(core=1 - here.core)

    def feat(y, core):
        return feats.at[y // 2, (y % 2) * 2 + core]

    def pass_on(i, y):
        send(grad_ref if i == 0 else feat(y, here.core), feat(y, here.core), pass_s.at[i], pass_r.at[i], partner)

    pass_on(0, here.y)
    share = [(0, 1), (1, 0), (1, 1)]
    for i, (dy, dc) in enumerate(share):
        y_lo, core = (here.y_lo + dy) % 2, (here.core + dc) % 2
        send(
            gate_columns(y_lo * 2 + core), gates.at[me], gate_s.at[i], gate_r.at[i],
            here.at(y=here.y_hi * 2 + y_lo, core=core),
        )

    for i, y, core in column_peers():
        source_y, source_core = wrap(2 * here.y - y + SIDE), core
        await_bytes(
            weights.at[source_y % 2, here.x, here.z, source_core * 2 + source_y // 2],
            spread_r.at[i],
        )
    copies[0].wait()

    def half_block(ref, i):
        return ref.at[pl.ds(i * 2, 2)]

    def block_ring(k, axis, item):
        return Ring(here, axis, item, half_block, ring_s.at[k], ring_r.at[k])

    first = [
        block_ring(0, "x", lambda x: weights.at[0, x, here.z]),
        block_ring(1, "z", lambda z: weights.at[1, here.x, z]),
    ]
    order = (0, 3, 1, 2)
    second = []
    for j, d in enumerate(order):
        second.append((
            block_ring(2 + 2 * j, "z", lambda z, d=d: weights.at[0, wrap(here.x + d), z]),
            block_ring(3 + 2 * j, "x", lambda x, d=d: weights.at[1, x, wrap(here.z + d)]),
        ))
    for ring in first:
        ring.start()
    for ring in second[0]:
        ring.start()
    for ring in first:
        ring.relay()
    for pair in second[1:3]:
        for ring in pair:
            ring.start()
    for ring in second[0]:
        ring.relay()
    for ring in first:
        ring.finish()
    for ring in second[3]:
        ring.start()
    features.relay()
    pass_on(1, wrap(here.y - 1))
    pass_on(2, wrap(here.y + 1))
    for pair in second[1:]:
        for ring in pair:
            ring.relay()
    features.finish()
    pass_on(3, wrap(here.y + 2))
    for pair in second:
        for ring in pair:
            ring.finish()
    for i, d in enumerate((0, -1, 1, 2)):
        await_bytes(feat(wrap(here.y + d), 1 - here.core), pass_r.at[i])
    copies[1].wait()

    depth = SIDE * weights.shape[3] * weights.shape[4]
    for h in range(2):
        @pl.loop(0, SIDE)
        def _(x):
            part = pl.ds(pl.multiple_of(x * depth, depth), depth)
            left = feats[h, :, :, part].reshape(4 * height, depth)
            term = dot(left, weights[h, x].reshape(depth, columns))
            if h == 0:
                @pl.when(x == 0)
                def _():
                    total[...] = term

                @pl.when(x > 0)
                def _():
                    total[...] += term
            else:
                total[...] += term

    copies[2].wait()
    for i, (dy, dc) in enumerate(share):
        source = ((here.y_lo + dy) % 2) * 2 + (here.core + dc) % 2
        await_bytes(gates.at[source], gate_r.at[i])
    width = late_ref.shape[3]
    for g in range(4):
        part = total[g * height : (g + 1) * height]
        long_grad = (part * gates[g].astype(F32)).astype(BF16).astype(F32)
        turned[:, g // 2, g % 2] = long_grad.T.astype(BF16).reshape(PLANE, width, height)
        hidden[g] = part.astype(BF16)
    keep = pltpu.make_async_copy(turned.at[cell], late_ref.at[:, cell], local.at[0])
    keep.start()
    for i, x, z in plane_peers():
        send(turned.at[x * SIDE + z], late_ref.at[:, cell], late_s.at[i], late_r.at[i], here.at(x=x, z=z))
    for i, (dy, dc) in enumerate(share):
        y_lo, core = (here.y_lo + dy) % 2, (here.core + dc) % 2
        send(
            hidden.at[y_lo * 2 + core], arrived.at[me], back_s.at[i], back_r.at[i],
            here.at(y=here.y_hi * 2 + y_lo, core=core),
        )
    own = pltpu.make_async_copy(hidden.at[me], arrived.at[me], local.at[1])
    own.start()
    own.wait()
    for i, (dy, dc) in enumerate(share):
        source = ((here.y_lo + dy) % 2) * 2 + (here.core + dc) % 2
        await_bytes(arrived.at[source], back_r.at[i])
    for g in range(4):
        part = slice(g * columns, (g + 1) * columns)
        outer_ref[:, part] = (arrived[g].astype(F32) * long_ref[:, part].astype(F32)).astype(BF16)
    keep.wait()
    for i, x, z in plane_peers():
        source = wrap(2 * here.x - x + SIDE) * SIDE + wrap(2 * here.z - z + SIDE)
        await_bytes(late_ref.at[:, source], late_r.at[i])

    for i in range(7):
        await_bytes(own_rows, spread_s.at[i])
    for i in range(3):
        await_bytes(gates.at[me], gate_s.at[i])
        await_bytes(hidden.at[me], back_s.at[i])
    for i in range(4):
        await_bytes(feats.at[0, 0], pass_s.at[i])
    for i in range(15):
        await_bytes(turned.at[0], late_s.at[i])
    features.drain()
    for ring in first:
        ring.drain()
    for pair in second:
        for ring in pair:
            ring.drain()


def project(out_grad, out_weight, outer_gate, long_out):
    height, half = out_grad.shape
    rows, model = out_weight.shape
    columns = model // 8
    width = columns // PLANE
    dma = pltpu.SemaphoreType.DMA
    anywhere = pl.BlockSpec(memory_space=pl.ANY)
    in_vmem = pl.BlockSpec(memory_space=pltpu.VMEM)
    outer, late = pl.pallas_call(
        project_kernel,
        out_shape=(
            jax.ShapeDtypeStruct((height, half), BF16),
            jax.ShapeDtypeStruct((2, PLANE, 2, width, height), BF16),
        ),
        in_specs=[anywhere, anywhere, anywhere, in_vmem],
        out_specs=(in_vmem, in_vmem),
        scratch_shapes=[
            pltpu.VMEM((2, 4, height, half), BF16),
            pltpu.VMEM((2, SIDE, SIDE, 4, rows, columns), BF16),
            pltpu.VMEM((4, height, columns), BF16),
            pltpu.VMEM((4 * height, columns), F32),
            pltpu.VMEM((PLANE, 2, 2, width, height), BF16),
            pltpu.VMEM((4, height, columns), BF16),
            pltpu.VMEM((4, height, columns), BF16),
            dma((3,)), dma((7,)), dma((7,)), dma((3,)), dma((3,)), dma((4,)), dma((4,)),
            dma((4,)), dma((4,)), dma((10, 4)), dma((10, 4)), dma((15,)), dma((15,)),
            dma((3,)), dma((3,)),
        ],
        compiler_params=pltpu.CompilerParams(
            collective_id=0, has_side_effects=True, vmem_limit_bytes=40 * 1024 * 1024
        ),
        cost_estimate=pl.CostEstimate(
            flops=2 * 4 * height * model * columns, bytes_accessed=16 * 2**20, transcendentals=0
        ),
        name="project",
    )(out_grad, out_weight, outer_gate, long_out)
    return outer, late.reshape(4 * PLANE, width, height)


def per_device(
    out_grad, out_weight, outer_gate, long_out, inner_gate, conv_input,
    short_out, medium_out, long_filter, taps_short, taps_medium,
):
    height, channels = outer_gate.shape
    devices = lax.axis_size("seq")
    width = channels // devices
    first, twists, forward, inverse, last, flip = tables(devices)

    early = to_blocks((inner_gate, medium_out, short_out, conv_input, long_filter), devices)
    early = lax.all_to_all(early, "seq", 0, 0, tiled=True)
    here = Here()
    at = (((here.y_lo * 2 + here.core) * SIDE + here.x) * SIDE + here.z) * width
    own = [lax.dynamic_slice_in_dim(t, at, width, 1) for t in (taps_medium, taps_short)]
    own[1] = jnp.pad(own[1], ((0, MEDIUM - SHORT), (0, 0)))
    taps = jnp.stack([t.astype(F32).T for t in own])
    grad_outer, late = project(out_grad, out_weight, outer_gate, long_out)
    spec, gates, bands, turned = prepare(early, taps, first, twists, forward, flip)
    results = finish(late, spec, gates, bands, turned, first, twists, forward, inverse, last)
    grad_inner, grad_input, grad_filter, grad_medium = from_blocks(
        results, (BF16, BF16, F32, F32)
    )
    short = results[:, 1, 4, :SHORT, :width]
    short = short.reshape(2, PLANE, 2, SHORT, width).transpose(3, 0, 2, 1, 4)
    grad_short = short.reshape(SHORT, channels).astype(F32)
    return grad_outer, grad_inner, grad_input, grad_filter, grad_short, grad_medium


def solution(mesh):
    rows = P("seq", "ch")
    return jax.shard_map(
        per_device,
        mesh=mesh,
        in_specs=(rows, P(("seq", "ch"), None)) + (rows,) * 7 + (P(None, "ch"),) * 2,
        out_specs=(rows,) * 4 + (P(None, "ch"),) * 2,
        check_vma=False,
    )
```

```python
import math

import jax
import jax.numpy as jnp
import numpy as np
from jax import lax
from jax.experimental import pallas as pl
from jax.experimental.pallas import tpu as pltpu
from jax.sharding import PartitionSpec as P

SHORT = 7
MEDIUM = 128
LANES = 128
F32 = jnp.float32
BF16 = jnp.bfloat16
VMEM_LIMIT = 60 * 1024 * 1024
PAD = 16
SIDE = 4
PLANE = SIDE * SIDE
MESH = pl.DeviceIdType.MESH


def split_np(table):
    high = table.astype(np.float32).astype(jnp.bfloat16)
    low = (table - high.astype(np.float64)).astype(np.float32).astype(jnp.bfloat16)
    return high, low


def tables(rows):
    total = 2 * rows * LANES
    freq = np.arange(rows)[:, None] + 0.5
    place = np.arange(rows)[None, :]
    angle = 2.0 * np.pi * freq * place / (2 * rows)
    first = np.concatenate([np.cos(angle), -np.sin(angle)], 0)
    first = np.concatenate(split_np(first), 1)
    twist = 2.0 * np.pi * freq * np.arange(LANES)[None, :] / total
    inner = 2.0 * np.pi * np.outer(np.arange(LANES), np.arange(LANES)) / LANES
    cosine, sine = np.cos(inner), np.sin(inner)
    forward = np.block([[cosine, -sine], [sine, cosine]])
    inverse = np.block([[cosine, sine], [-sine, cosine]])
    scale = (rows * LANES) ** -0.5 * 2.0 / total
    last = np.concatenate([np.cos(angle.T), -np.sin(angle.T)], 1) * scale
    twists = np.concatenate([np.cos(twist), np.sin(twist)], 1).astype(np.float32)
    flip = np.eye(LANES)[::-1].astype(jnp.bfloat16)
    return (
        first,
        twists,
        np.concatenate(split_np(forward), 0),
        np.concatenate(split_np(inverse), 0),
        np.concatenate(split_np(last), 0),
        flip,
    )


def dot(a, b):
    return jnp.dot(a, b, preferred_element_type=F32)


def dot_t(a, b):
    return lax.dot_general(a, b, (((1,), (1,)), ((), ())), preferred_element_type=F32)


def split(x):
    high = x.astype(BF16)
    return high, (x - high.astype(F32)).astype(BF16)


def dot3(high, low, table):
    size = table.shape[0] // 2
    return dot(high, table[:size]) + dot(high, table[size:]) + dot(low, table[:size])


def outer_stage(pair, first, twists):
    rows = pair.shape[0]
    spread = dot(first, jnp.concatenate([pair, pair], 0))
    cosine = jnp.concatenate([twists[:, :LANES]] * 2, 1)
    sine = jnp.concatenate([twists[:, LANES:]] * 2, 1)
    real, imag = spread[:rows], spread[rows:]
    new_real = real * cosine + imag * sine
    new_imag = imag * cosine - real * sine
    return (
        jnp.concatenate([new_real[:, :LANES], new_imag[:, :LANES]], 1),
        jnp.concatenate([new_real[:, LANES:], new_imag[:, LANES:]], 1),
    )


def toeplitz(line):
    row = jnp.concatenate([line, jnp.zeros_like(line)], 1)
    block = jnp.broadcast_to(row, (LANES, 2 * LANES))
    return pltpu.roll(block, 0, 1, stride=1, stride_axis=0)


def wrap(i):
    return lax.rem(i + SIDE, SIDE)


class Here:
    def __init__(self):
        seq = lax.axis_index("seq")
        self.seq = seq
        self.y_hi = lax.axis_index("ch")
        self.core = seq % 2
        self.z = (seq // 2) % SIDE
        self.x = (seq // (2 * SIDE)) % SIDE
        self.y_lo = seq // (2 * PLANE)
        self.y = self.y_hi * 2 + self.y_lo

    def token_peers(self):
        xs = [wrap(self.x + d) for d in range(SIDE)]
        zs = [wrap(self.z + d) for d in range(SIDE)]
        cores, ys = [self.core, 1 - self.core], [self.y_lo, 1 - self.y_lo]
        for dx in range(SIDE):
            for dz in range(SIDE):
                for dy in range(2):
                    for dc in range(2):
                        if dx or dz or dy or dc:
                            cell = xs[dx] * SIDE + zs[dz]
                            yield (
                                (ys[dy] * PLANE + cell) * 2 + cores[dc],
                                (ys[dy] * 2 + cores[dc]) * PLANE + cell,
                            )

    def at(self, x=None, y=None, z=None, core=None):
        x = self.x if x is None else x
        y = self.y if y is None else y
        z = self.z if z is None else z
        core = self.core if core is None else core
        seq = (((y % 2) * SIDE + x) * SIDE + z) * 2 + core
        return {"seq": seq, "ch": y // 2}


def send(source, target, sends, recvs, device):
    copy = pltpu.make_async_remote_copy(
        src_ref=source,
        dst_ref=target,
        send_sem=sends,
        recv_sem=recvs,
        device_id=device,
        device_id_type=MESH,
    )
    copy.start()


def await_bytes(ref, sem):
    pltpu.make_async_copy(ref, ref, sem).wait()


class Ring:
    def __init__(self, here, axis, item, half, sends, recvs, source=None):
        self.at = lambda p: here.at(**{axis: p})
        self.place = getattr(here, axis)
        self.item, self.half = item, half
        self.sends, self.recvs = sends, recvs
        self.source = item(self.place) if source is None else source

    def step(self, i, source, target, to):
        send(source, target, self.sends.at[i], self.recvs.at[i], self.at(wrap(self.place + to)))

    def start(self):
        self.step(0, self.source, self.item(self.place), 1)
        self.step(1, self.source, self.item(self.place), -1)

    def relay(self):
        for i, to in ((0, 1), (1, -1)):
            other = wrap(self.place - to)
            await_bytes(self.item(other), self.recvs.at[i])
            half = self.half(self.item(other), i)
            self.step(2 + i, half, half, to)

    def finish(self):
        opposite = self.item(wrap(self.place + 2))
        for i in range(2):
            await_bytes(self.half(opposite, i), self.recvs.at[2 + i])

    def drain(self):
        opposite = self.item(wrap(self.place + 2))
        for i in range(2):
            await_bytes(self.item(self.place), self.sends.at[i])
            await_bytes(self.half(opposite, i), self.sends.at[2 + i])


def block_kernel(
    grad_ref, weight_ref, gate_ref, long_ref,
    inner_ref, medium_ref, short_ref, conv_ref, filter_ref, taps_ref,
    first_ref, twists_ref, forward_ref, inverse_ref, last_ref, flip_ref,
    outer_ref, back_ref, lags_ref,
    feats, weights, gates, total, turned, hidden, arrived,
    one_out, one_in, two_out, two_in, late,
    lines, zh, zl, gh, gl, spec, bands, saved, points, results, sums, parcels,
    local, spread_s, spread_r, gate_s, gate_r, feat_s, feat_r, pass_s, pass_r,
    ring_s, ring_r, late_sem, hidden_s, hidden_r, batch_s, batch_r, lag_s, lag_r,
):
    here = Here()
    me = here.y_lo * 2 + here.core
    cell = here.x * SIDE + here.z
    block = me * PLANE + cell
    columns = gates.shape[2]
    height = grad_ref.shape[0]
    rows, width = one_in.shape[0], one_in.shape[2]
    area = rows * width
    chunk = width // 2
    partner = here.at(core=1 - here.core)
    peers = list(here.token_peers())

    def column_peers():
        for dy in range(SIDE):
            for dc in range(2):
                if dy or dc:
                    yield dy * 2 + dc - 1, wrap(here.y + dy), (here.core + dc) % 2

    def plane_peers():
        for dx in range(SIDE):
            for dz in range(SIDE):
                if dx or dz:
                    yield wrap(here.x + dx), wrap(here.z + dz)

    barrier = pltpu.get_barrier_semaphore()
    for seq, _ in peers:
        pl.semaphore_signal(
            barrier, 1, device_id={"seq": seq, "ch": here.y_hi}, device_id_type=MESH
        )
    for y_lo in range(2):
        for core in range(2):
            there = here.at(y=(1 - here.y_hi) * 2 + y_lo, core=core)
            pl.semaphore_signal(barrier, 1, device_id=there, device_id_type=MESH)
    pl.semaphore_wait(barrier, len(peers) + 4)

    def weight_columns(y, core):
        return weight_ref.at[:, pl.ds(pl.multiple_of((y * 2 + core) * columns, columns), columns)]

    def gate_columns(index):
        return gate_ref.at[:, pl.ds(pl.multiple_of(index * columns, columns), columns)]

    own_rows = weights.at[here.y_lo, here.x, here.z, here.core * 2 + here.y_hi]
    for i, y, core in column_peers():
        send(
            weight_columns(y, core), own_rows, spread_s.at[i], spread_r.at[i],
            here.at(y=y, core=core),
        )
    copies = [
        pltpu.make_async_copy(weight_columns(here.y, here.core), own_rows, local.at[0]),
        pltpu.make_async_copy(grad_ref, feats.at[here.y_hi, me], local.at[1]),
        pltpu.make_async_copy(gate_columns(me), gates.at[me], local.at[2]),
    ]
    for copy in copies:
        copy.start()

    def half_tokens(ref, i):
        return ref.at[pl.ds(i * (height // 2), height // 2)]

    def feat(y, core):
        return feats.at[y // 2, (y % 2) * 2 + core]

    features = Ring(
        here, "y", lambda y: feat(y, here.core), half_tokens, feat_s, feat_r, source=grad_ref
    )
    features.start()

    def pass_on(i, y):
        source = grad_ref if i == 0 else feat(y, here.core)
        send(source, feat(y, here.core), pass_s.at[i], pass_r.at[i], partner)

    pass_on(0, here.y)
    share = [(0, 1), (1, 0), (1, 1)]

    def sharer(dy, dc):
        y_lo, core = (here.y_lo + dy) % 2, (here.core + dc) % 2
        return y_lo * 2 + core, here.at(y=here.y_hi * 2 + y_lo, core=core)

    for i, (dy, dc) in enumerate(share):
        index, device = sharer(dy, dc)
        send(gate_columns(index), gates.at[me], gate_s.at[i], gate_r.at[i], device)

    def exchange(batch, piece, arrive):
        for seq, other in peers:
            send(
                piece(seq, other), arrive, batch_s.at[batch], batch_r.at[batch],
                {"seq": seq, "ch": here.y_hi},
            )
        pltpu.make_async_copy(piece(here.seq, block), arrive, batch_r.at[batch]).start()

    span = 8

    def turn(value, out, k):
        @pl.loop(0, rows // span)
        def _(b):
            part = pl.ds(pl.multiple_of(b * span * width, span * width), span * width)
            lined = value(part).T.astype(BF16).reshape(span, width, height)
            out[pl.ds(b * span, span), k] = lined

    def plain(ref):
        return lambda part: ref[:, part].astype(F32)

    def half_block(ref, i):
        return ref.at[pl.ds(i * 2, 2)]

    def block_ring(k, axis, item):
        return Ring(here, axis, item, half_block, ring_s.at[k], ring_r.at[k])

    first = [
        block_ring(0, "x", lambda x: weights.at[0, x, here.z]),
        block_ring(1, "z", lambda z: weights.at[1, here.x, z]),
    ]
    second = []
    for j, d in enumerate((0, 3, 1, 2)):
        second.append((
            block_ring(2 + 2 * j, "z", lambda z, d=d: weights.at[0, wrap(here.x + d), z]),
            block_ring(3 + 2 * j, "x", lambda x, d=d: weights.at[1, x, wrap(here.z + d)]),
        ))

    turn(lambda part: inner_ref[:, part].astype(F32) * medium_ref[:, part].astype(F32), one_out, 0)
    turn(plain(filter_ref), one_out, 1)

    for i, y, core in column_peers():
        source_y = wrap(2 * here.y - y + SIDE)
        await_bytes(
            weights.at[source_y % 2, here.x, here.z, core * 2 + source_y // 2], spread_r.at[i]
        )
    copies[0].wait()
    for ring in first:
        ring.start()
    for ring in second[0]:
        ring.start()
    exchange(0, lambda seq, other: one_out.at[other], one_in.at[here.seq])

    turn(plain(inner_ref), two_out, 0)
    for ring in first:
        ring.relay()
    for pair in second[1:3]:
        for ring in pair:
            ring.start()
    turn(plain(short_ref), two_out, 1)
    for ring in second[0]:
        ring.relay()
    for ring in first:
        ring.finish()
    for ring in second[3]:
        ring.start()
    turn(plain(conv_ref), two_out, 2)
    features.relay()
    pass_on(1, wrap(here.y - 1))
    pass_on(2, wrap(here.y + 1))

    def make_bands(k):
        @pl.loop(0, width)
        def _(c):
            wide = pl.ds(pl.multiple_of(c * LANES, LANES), LANES)
            bands[k, wide, :] = toeplitz(taps_ref[k, pl.ds(c, 1), :]).astype(BF16)

    make_bands(0)
    for ring in second[1]:
        ring.relay()
    make_bands(1)
    for ring in second[2]:
        ring.relay()

    def unpack(source, planes):
        @pl.loop(0, rows)
        def _(i):
            at = pl.ds(pl.multiple_of(i * width, width), width)
            for k, plane in planes:
                value = source[i] if k is None else source[i, k]
                lines[plane, at, :] = value.astype(F32)

    def keep(parts, places):
        for part, place in zip(parts, places):
            high, low = split(part)
            there = pl.ds(pl.multiple_of(place, rows), rows)
            yield there, high, low

    await_bytes(one_in, batch_r.at[0])
    unpack(one_in, ((0, 0), (1, 1)))
    for ring in second[3]:
        ring.relay()

    def spread_pairs(begin, end):
        @pl.loop(begin, end)
        def _(c):
            pick = pl.ds(c, rows, stride=width)
            pair = jnp.concatenate([lines[0, pick, :], lines[1, pick, :]], 1).astype(BF16)
            parts = outer_stage(pair, first_ref[...], twists_ref[...])
            for there, high, low in keep(parts, (c * rows, area + c * rows)):
                zh[there, :] = high
                zl[there, :] = low

    spread_pairs(0, width // 2)
    features.finish()
    pass_on(3, wrap(here.y + 2))
    spread_pairs(width // 2, width)
    step = 512

    @pl.loop(0, 2 * area // step)
    def _(b):
        at = pl.ds(pl.multiple_of(b * step, step), step)
        spec[at, :] = dot3(zh[at, :], zl[at, :], forward_ref[...])

    for pair in second:
        for ring in pair:
            ring.finish()
    for i, d in enumerate((0, -1, 1, 2)):
        await_bytes(feat(wrap(here.y + d), 1 - here.core), pass_r.at[i])
    copies[1].wait()
    depth = SIDE * weights.shape[3] * weights.shape[4]
    for h in range(2):
        @pl.loop(0, SIDE)
        def _(x):
            part = pl.ds(pl.multiple_of(x * depth, depth), depth)
            left = feats[h, :, :, part].reshape(4 * height, depth)
            term = dot(left, weights[h, x].reshape(depth, columns))
            if h == 0:
                @pl.when(x == 0)
                def _():
                    total[...] = term

                @pl.when(x > 0)
                def _():
                    total[...] += term
            else:
                total[...] += term

    copies[2].wait()
    for i, (dy, dc) in enumerate(share):
        await_bytes(gates.at[sharer(dy, dc)[0]], gate_r.at[i])
    for g in range(4):
        part = total[g * height : (g + 1) * height]
        long_grad = (part * gates[g].astype(F32)).astype(BF16).astype(F32)
        turned[:, g // 2, g % 2] = long_grad.T.astype(BF16).reshape(PLANE, width, height)
        hidden[g] = part.astype(BF16)
    pltpu.make_async_copy(turned.at[cell], late.at[:, cell], late_sem.at[1]).start()
    for x, z in plane_peers():
        send(
            turned.at[x * SIDE + z], late.at[:, cell], late_sem.at[0], late_sem.at[1],
            here.at(x=x, z=z),
        )
    exchange(1, lambda seq, other: two_out.at[other], two_in.at[here.seq])
    for i, (dy, dc) in enumerate(share):
        index, device = sharer(dy, dc)
        send(hidden.at[index], arrived.at[me], hidden_s.at[i], hidden_r.at[i], device)
    own = pltpu.make_async_copy(hidden.at[me], arrived.at[me], local.at[1])
    own.start()

    await_bytes(late, late_sem.at[1])
    for y_lo in range(2):
        @pl.loop(0, PLANE)
        def _(i):
            for core in range(2):
                place = ((y_lo * PLANE + i) * 2 + core) * width
                at = pl.ds(pl.multiple_of(place, width), width)
                lines[2, at, :] = late[y_lo, i, core].astype(F32)

    many = 4
    wide_step = many * rows
    row = lax.broadcasted_iota(jnp.int32, (rows, LANES), 0)

    def transform(start):
        @pl.loop(0, chunk // 2)
        def _(c):
            pair = jnp.concatenate(
                [lines[2, pl.ds(start + 2 * c + k, rows, stride=width), :] for k in range(2)], 1
            ).astype(BF16)
            parts = outer_stage(pair, first_ref[...], twists_ref[...])
            for there, high, low in keep(parts, (2 * c * rows, (2 * c + 1) * rows)):
                gh[there, :] = high
                gl[there, :] = low

        @pl.loop(0, chunk // many)
        def _(b):
            at = pl.ds(pl.multiple_of(b * wide_step, wide_step), wide_step)
            grad = dot3(gh[at, :], gl[at, :], forward_ref[...])
            grad_real, grad_imag = grad[:, :LANES], grad[:, LANES:]
            cosine = jnp.concatenate([twists_ref[:, :LANES]] * many, 0)
            sine = jnp.concatenate([twists_ref[:, LANES:]] * many, 0)
            reals, imags = [], []
            for k in range(2):
                place = (1 - k) * area + start * rows + b * wide_step
                other = spec[pl.ds(pl.multiple_of(place, wide_step), wide_step), :]
                real, imag = other[:, :LANES], other[:, LANES:]
                term = jnp.concatenate(
                    [real * grad_real + imag * grad_imag, real * grad_imag - imag * grad_real], 1
                )
                back = dot3(*split(term), inverse_ref[...])
                real, imag = back[:, :LANES], back[:, LANES:]
                reals.append(real * cosine - imag * sine)
                imags.append(real * sine + imag * cosine)
            real, imag = jnp.concatenate(reals, 1), jnp.concatenate(imags, 1)
            for k in range(many):
                both = jnp.concatenate(
                    [real[k * rows : (k + 1) * rows], imag[k * rows : (k + 1) * rows]], 0
                )
                high, low = split(both)
                there = pl.ds(pl.multiple_of((b * many + k) * 2 * rows, 2 * rows), 2 * rows)
                zh[there, :] = high
                zl[there, :] = low

        @pl.loop(0, chunk // many)
        def _(b):
            for k in range(many):
                within = b * many + k
                c = start + within
                there = pl.ds(pl.multiple_of(within * 2 * rows, 2 * rows), 2 * rows)
                high, low = zh[there, :], zl[there, :]
                both = (
                    dot(last_ref[:rows], high) + dot(last_ref[:rows], low)
                    + dot(last_ref[rows:], high)
                )
                pick = pl.ds(within, rows, stride=chunk)
                points[pl.ds(pl.multiple_of(c * rows, rows), rows), :] = both[:, :LANES]
                results[0, pick, :] = both[:, :LANES]
                results[1, pick, :] = both[:, LANES:]

    def pack(k, source, to):
        @pl.loop(0, rows)
        def _(i):
            at = pl.ds(pl.multiple_of(i * chunk, chunk), chunk)
            for a, b in zip(source, to):
                parcels[i, k, b] = results[a, at, :].astype(BF16)

    def pair_of(ref, k):
        return ref.at[k, pl.ds(0, 2)]

    for k in range(2):
        transform(k * chunk)
        pack(k, (0, 1), (0, 1))
        exchange(2 + k, lambda seq, other: pair_of(parcels.at[seq], k), pair_of(back_ref.at[block], k))

    own.wait()
    for i, (dy, dc) in enumerate(share):
        await_bytes(arrived.at[sharer(dy, dc)[0]], hidden_r.at[i])
    for g in range(4):
        part = slice(g * columns, (g + 1) * columns)
        outer_ref[:, part] = (arrived[g].astype(F32) * long_ref[:, part].astype(F32)).astype(BF16)

    await_bytes(two_in, batch_r.at[1])
    unpack(two_in, ((0, 0), (1, 1), (2, 2)))

    @pl.loop(0, width)
    def _(c):
        wide = pl.ds(pl.multiple_of(c * LANES, LANES), LANES)
        for k in range(2):
            value = lines[1 + k, pl.ds(c, rows, stride=width), :].astype(BF16)
            saved[k, wide, :] = dot_t(flip_ref[...], value).astype(BF16)

    def with_next(x):
        following = jnp.where(row == rows - 1, 0.0, pltpu.roll(x, rows - 1, 0))
        return jnp.concatenate([x, following], 1).astype(BF16)

    def diagonals(wide, k, both):
        products = dot(saved[k, wide, :], both)
        slid = pltpu.roll(products, 0, 1, stride=1, stride_axis=0)
        return jnp.sum(slid, axis=0, keepdims=True)

    def convolve(start):
        @pl.loop(0, chunk // many)
        def _(b):
            for k in range(many):
                within = b * many + k
                c = start + within
                wide = pl.ds(pl.multiple_of(c * LANES, LANES), LANES)
                point = points[pl.ds(pl.multiple_of(c * rows, rows), rows), :]
                gate = lines[0, pl.ds(c, rows, stride=width), :]
                both = with_next((point * gate).astype(BF16).astype(F32))
                short_grad = dot_t(both, bands[0, wide, :]).astype(BF16).astype(F32)
                pair = with_next(short_grad)
                pick = pl.ds(within, rows, stride=chunk)
                results[0, pick, :] = dot_t(pair, bands[1, wide, :])
                sums[0, pl.ds(c, 1), :] = diagonals(wide, 0, both)
                sums[1, pl.ds(c, 1), :] = diagonals(wide, 1, pair)

    for k in range(2):
        convolve(k * chunk)
        pack(k, (0,), (2,))
        exchange(4 + k, lambda seq, other: parcels.at[seq, k, 2], back_ref.at[block, k, 2])

    factor = (rows * LANES) ** -0.5
    lags = [pltpu.roll(sums[k], LANES + 1, 1)[:, :LANES] * factor for k in range(2)]
    square = jnp.concatenate([lags[1], jnp.zeros((LANES - width, LANES), F32)], 0)
    mine = lags_ref.at[here.y_lo, here.core]
    lags_ref[here.y_lo, here.core, here.x, here.z, :width] = lags[0].astype(BF16)
    lags_ref[here.y_lo, here.core, here.x, here.z, width:] = square.T[:PAD].astype(BF16)

    def lag_send(i, ref, device):
        send(ref, ref, lag_s.at[i], lag_r.at[i], device)

    for d in range(1, SIDE):
        lag_send(d - 1, mine.at[here.x, here.z], here.at(x=wrap(here.x + d)))
    for d in range(1, SIDE):
        await_bytes(mine.at[wrap(here.x - d), here.z], lag_r.at[d - 1])
    for d in range(1, SIDE):
        lag_send(2 + d, mine.at[:, here.z], here.at(z=wrap(here.z + d)))
    for d in range(1, SIDE):
        await_bytes(mine.at[:, wrap(here.z - d)], lag_r.at[2 + d])
    across = here.at(y=here.y_hi * 2 + 1 - here.y_lo)
    lag_send(6, mine, across)
    lag_send(7, mine, partner)
    await_bytes(lags_ref.at[1 - here.y_lo, here.core], lag_r.at[6])
    lag_send(8, lags_ref.at[1 - here.y_lo, here.core], partner)
    await_bytes(lags_ref.at[here.y_lo, 1 - here.core], lag_r.at[7])
    await_bytes(lags_ref.at[1 - here.y_lo, 1 - here.core], lag_r.at[8])

    for k in range(2):
        await_bytes(back_ref.at[:, k, pl.ds(0, 2)], batch_r.at[2 + k])
        await_bytes(back_ref.at[:, k, 2], batch_r.at[4 + k])
    most = pl.ds(0, rows - 1)
    await_bytes(one_out.at[most], batch_s.at[0])
    await_bytes(two_out.at[most], batch_s.at[1])
    for k in range(2):
        await_bytes(parcels.at[most, k, pl.ds(0, 2)], batch_s.at[2 + k])
        await_bytes(parcels.at[most, k, 2], batch_s.at[4 + k])
    await_bytes(turned.at[pl.ds(0, PLANE - 1)], late_sem.at[0])
    for i in range(7):
        await_bytes(own_rows, spread_s.at[i])
    for i in range(3):
        await_bytes(gates.at[me], gate_s.at[i])
        await_bytes(hidden.at[me], hidden_s.at[i])
        await_bytes(mine.at[here.x, here.z], lag_s.at[i])
        await_bytes(mine.at[:, here.z], lag_s.at[3 + i])
        await_bytes(mine, lag_s.at[6 + i])
    for i in range(4):
        await_bytes(feats.at[0, 0], pass_s.at[i])
    features.drain()
    for ring in first:
        ring.drain()
    for pair in second:
        for ring in pair:
            ring.drain()


def block_call(grad, weight, gate, long, channelwise, taps, constants):
    height, half = grad.shape
    depth, model = weight.shape
    columns = model // 8
    width = columns // PLANE
    rows = half // width
    area = rows * width
    chunk = width // 2
    anywhere = pl.BlockSpec(memory_space=pl.ANY)
    near = pl.BlockSpec(memory_space=pltpu.VMEM)
    dma = pltpu.SemaphoreType.DMA
    vmem = pltpu.VMEM
    return pl.pallas_call(
        block_kernel,
        out_shape=(
            jax.ShapeDtypeStruct((height, half), BF16),
            jax.ShapeDtypeStruct((rows, 2, 3, chunk, height), BF16),
            jax.ShapeDtypeStruct((2, 2, SIDE, SIDE, width + PAD, height), BF16),
        ),
        in_specs=[anywhere] * 3 + [near] * (7 + len(constants)),
        out_specs=(near, anywhere, near),
        scratch_shapes=[
            vmem((2, 4, height, half), BF16),
            vmem((2, SIDE, SIDE, 4, depth, columns), BF16),
            vmem((4, height, columns), BF16),
            vmem((4 * height, columns), F32),
            vmem((PLANE, 2, 2, width, height), BF16),
            vmem((4, height, columns), BF16),
            vmem((4, height, columns), BF16),
            vmem((rows, 2, width, height), BF16),
            vmem((rows, 2, width, height), BF16),
            vmem((rows, 3, width, height), BF16),
            vmem((rows, 3, width, height), BF16),
            vmem((2, PLANE, 2, width, height), BF16),
            vmem((3, area, height), F32),
            vmem((2 * area, 2 * height), BF16),
            vmem((2 * area, 2 * height), BF16),
            vmem((area // 2, 2 * height), BF16),
            vmem((area // 2, 2 * height), BF16),
            vmem((2 * area, 2 * height), F32),
            vmem((2, width * LANES, 2 * LANES), BF16),
            vmem((2, width * LANES, rows), BF16),
            vmem((area, height), F32),
            vmem((2, area // 2, height), F32),
            vmem((2, width, 2 * LANES), F32),
            vmem((rows, 2, 3, chunk, height), BF16),
            dma((3,)), dma((7,)), dma((7,)), dma((3,)), dma((3,)), dma((4,)), dma((4,)),
            dma((4,)), dma((4,)), dma((10, 4)), dma((10, 4)), dma((2,)), dma((3,)), dma((3,)),
            dma((6,)), dma((6,)), dma((9,)), dma((9,)),
        ],
        compiler_params=pltpu.CompilerParams(
            collective_id=0, has_side_effects=True, vmem_limit_bytes=VMEM_LIMIT
        ),
        cost_estimate=pl.CostEstimate(
            flops=16 * 10**9, bytes_accessed=32 * 2**20, transcendentals=0
        ),
        name="block",
    )(grad, weight, gate, long, *channelwise, taps, *constants)


def unturn_kernel(in_ref, lags_ref, medium_ref, inner_out, input_out, filter_out, lags_out):
    size, height = inner_out.shape[1], in_ref.shape[4]

    def lined(value):
        return value.astype(F32).reshape(size, height).T

    inner_out[...] = (lined(in_ref[:, :, 0]) * medium_ref[...].astype(F32)).astype(BF16)
    filter_out[...] = lined(in_ref[:, :, 1])
    input_out[...] = lined(in_ref[:, :, 2]).astype(BF16)
    lags_out[...] = lined(lags_ref[:, : size // in_ref.shape[0]])


def from_blocks(block, lags, medium_out):
    devices, parts, items, chunk, height = block.shape
    span = 8
    size = span * parts * chunk
    channels = devices * parts * chunk
    rows = pl.BlockSpec((height, size), lambda i: (0, i))
    return pl.pallas_call(
        unturn_kernel,
        grid=(devices // span,),
        out_shape=[
            jax.ShapeDtypeStruct((height, channels), t) for t in (BF16, BF16, F32, F32)
        ],
        in_specs=[
            pl.BlockSpec((span, parts, items, chunk, height), lambda i: (i, 0, 0, 0, 0)),
            pl.BlockSpec((span, lags.shape[1], height), lambda i: (i, 0, 0)),
            rows,
        ],
        out_specs=[rows] * 4,
        cost_estimate=pl.CostEstimate(
            flops=0, bytes_accessed=24 * height * channels, transcendentals=0
        ),
        name="from_blocks",
    )(block, lags, medium_out)


def per_device(
    out_grad, out_weight, outer_gate, long_out, inner_gate, conv_input,
    short_out, medium_out, long_filter, taps_short, taps_medium,
):
    channels = outer_gate.shape[1]
    devices = lax.axis_size("seq")
    width = channels // devices
    here = Here()
    at = (((here.y_lo * 2 + here.core) * SIDE + here.x) * SIDE + here.z) * width
    own = [lax.dynamic_slice_in_dim(t, at, width, 1) for t in (taps_medium, taps_short)]
    own[1] = jnp.pad(own[1], ((0, MEDIUM - SHORT), (0, 0)))
    taps = jnp.stack([t.astype(F32).T for t in own])
    grad_outer, results, lags = block_call(
        out_grad, out_weight, outer_gate, long_out,
        (inner_gate, medium_out, short_out, conv_input, long_filter), taps, tables(devices),
    )
    lags = lags.reshape(devices, width + PAD, LANES)
    grad_inner, grad_input, grad_filter, grad_medium = from_blocks(results, lags, medium_out)
    short = lags[:, width : width + SHORT, :width].transpose(1, 0, 2)
    grad_short = short.reshape(SHORT, channels).astype(F32)
    return grad_outer, grad_inner, grad_input, grad_filter, grad_short, grad_medium


def solution(mesh):
    rows = P("seq", "ch")
    return jax.shard_map(
        per_device,
        mesh=mesh,
        in_specs=(rows, P(("seq", "ch"), None)) + (rows,) * 7 + (P(None, "ch"),) * 2,
        out_specs=(rows,) * 4 + (P(None, "ch"),) * 2,
        check_vma=False,
    )
```

```python
import math

import jax
import jax.numpy as jnp
import numpy as np
from jax import lax
from jax.experimental import pallas as pl
from jax.experimental.pallas import tpu as pltpu
from jax.sharding import PartitionSpec as P

SHORT = 7
MEDIUM = 128
LANES = 128
F32 = jnp.float32
BF16 = jnp.bfloat16
VMEM_LIMIT = 60 * 1024 * 1024
PAD = 16
SIDE = 4
PLANE = SIDE * SIDE
ORDER = (0, 3, 1, 2)
MESH = pl.DeviceIdType.MESH


def split_np(table):
    high = table.astype(np.float32).astype(jnp.bfloat16)
    low = (table - high.astype(np.float64)).astype(np.float32).astype(jnp.bfloat16)
    return high, low


def tables(rows):
    total = 2 * rows * LANES
    freq = np.arange(rows)[:, None] + 0.5
    place = np.arange(rows)[None, :]
    angle = 2.0 * np.pi * freq * place / (2 * rows)
    first = np.concatenate([np.cos(angle), -np.sin(angle)], 0)
    first = np.concatenate(split_np(first), 1)
    twist = 2.0 * np.pi * freq * np.arange(LANES)[None, :] / total
    inner = 2.0 * np.pi * np.outer(np.arange(LANES), np.arange(LANES)) / LANES
    cosine, sine = np.cos(inner), np.sin(inner)
    forward = np.block([[cosine, -sine], [sine, cosine]])
    inverse = np.block([[cosine, sine], [-sine, cosine]])
    scale = (rows * LANES) ** -0.5 * 2.0 / total
    last = np.concatenate([np.cos(angle.T), -np.sin(angle.T)], 1) * scale
    twists = np.concatenate([np.cos(twist), np.sin(twist)], 1).astype(np.float32)
    flip = np.eye(LANES)[::-1].astype(jnp.bfloat16)
    return (
        first,
        twists,
        np.concatenate(split_np(forward), 0),
        np.concatenate(split_np(inverse), 0),
        np.concatenate(split_np(last), 0),
        flip,
        np.eye(2 * LANES).astype(jnp.bfloat16),
    )


def dot(a, b):
    return jnp.dot(a, b, preferred_element_type=F32)


def dot_t(a, b):
    return lax.dot_general(a, b, (((1,), (1,)), ((), ())), preferred_element_type=F32)


def split(x):
    high = x.astype(BF16)
    return high, (x - high.astype(F32)).astype(BF16)


def dot3(high, low, table):
    size = table.shape[0] // 2
    return dot(high, table[:size]) + dot(high, table[size:]) + dot(low, table[:size])


def outer_stage(pair, first, twists):
    rows = pair.shape[0]
    spread = dot(first, jnp.concatenate([pair, pair], 0))
    cosine = jnp.concatenate([twists[:, :LANES]] * 2, 1)
    sine = jnp.concatenate([twists[:, LANES:]] * 2, 1)
    real, imag = spread[:rows], spread[rows:]
    new_real = real * cosine + imag * sine
    new_imag = imag * cosine - real * sine
    return (
        jnp.concatenate([new_real[:, :LANES], new_imag[:, :LANES]], 1),
        jnp.concatenate([new_real[:, LANES:], new_imag[:, LANES:]], 1),
    )


def toeplitz(line):
    row = jnp.concatenate([line, jnp.zeros_like(line)], 1)
    block = jnp.broadcast_to(row, (LANES, 2 * LANES))
    return pltpu.roll(block, 0, 1, stride=1, stride_axis=0)


def wrap(i):
    return lax.rem(i + SIDE, SIDE)


class Here:
    def __init__(self):
        seq = lax.axis_index("seq")
        self.seq = seq
        self.y_hi = lax.axis_index("ch")
        self.core = seq % 2
        self.z = (seq // 2) % SIDE
        self.x = (seq // (2 * SIDE)) % SIDE
        self.y_lo = seq // (2 * PLANE)
        self.y = self.y_hi * 2 + self.y_lo

    def token_peers(self):
        xs = [wrap(self.x + d) for d in range(SIDE)]
        zs = [wrap(self.z + d) for d in range(SIDE)]
        cores, ys = [self.core, 1 - self.core], [self.y_lo, 1 - self.y_lo]
        for dx in range(SIDE):
            for dz in range(SIDE):
                for dy in range(2):
                    for dc in range(2):
                        if dx or dz or dy or dc:
                            cell = xs[dx] * SIDE + zs[dz]
                            yield (
                                (ys[dy] * PLANE + cell) * 2 + cores[dc],
                                (ys[dy] * 2 + cores[dc]) * PLANE + cell,
                            )

    def at(self, x=None, y=None, z=None, core=None):
        x = self.x if x is None else x
        y = self.y if y is None else y
        z = self.z if z is None else z
        core = self.core if core is None else core
        seq = (((y % 2) * SIDE + x) * SIDE + z) * 2 + core
        return {"seq": seq, "ch": y // 2}


def send(source, target, sends, recvs, device):
    copy = pltpu.make_async_remote_copy(
        src_ref=source,
        dst_ref=target,
        send_sem=sends,
        recv_sem=recvs,
        device_id=device,
        device_id_type=MESH,
    )
    copy.start()


def await_bytes(ref, sem):
    pltpu.make_async_copy(ref, ref, sem).wait()


class Ring:
    def __init__(self, here, axis, item, half, sends, recvs, source=None):
        self.at = lambda p: here.at(**{axis: p})
        self.place = getattr(here, axis)
        self.item, self.half = item, half
        self.sends, self.recvs = sends, recvs
        self.source = item(self.place) if source is None else source

    def step(self, i, source, target, to):
        send(source, target, self.sends.at[i], self.recvs.at[i], self.at(wrap(self.place + to)))

    def start(self):
        self.step(0, self.source, self.item(self.place), 1)
        self.step(1, self.source, self.item(self.place), -1)

    def relay(self):
        for i, to in ((0, 1), (1, -1)):
            other = wrap(self.place - to)
            await_bytes(self.item(other), self.recvs.at[i])
            half = self.half(self.item(other), i)
            self.step(2 + i, half, half, to)

    def finish(self):
        opposite = self.item(wrap(self.place + 2))
        for i in range(2):
            await_bytes(self.half(opposite, i), self.recvs.at[2 + i])

    def drain(self):
        opposite = self.item(wrap(self.place + 2))
        for i in range(2):
            await_bytes(self.item(self.place), self.sends.at[i])
            await_bytes(self.half(opposite, i), self.sends.at[2 + i])


def block_kernel(
    grad_ref, weight_ref, gate_ref, long_ref,
    inner_ref, medium_ref, short_ref, conv_ref, filter_ref, taps_short_ref, taps_medium_ref,
    first_ref, twists_ref, forward_ref, inverse_ref, last_ref, flip_ref, eye_ref,
    outer_ref, back_ref, lags_ref,
    feats, weights, gates, total, turned, hidden, arrived,
    one_out, one_in, two_out, two_in, three_out, three_in, late,
    lines, zh, zl, gh, gl, spec, bands, taps, points, pairs, results, sums, parcels,
    local, spread_s, spread_r, gate_s, gate_r, feat_s, feat_r, pass_s, pass_r,
    ring_s, ring_r, late_sem, hidden_s, hidden_r, batch_s, batch_r, lag_s, lag_r,
):
    here = Here()
    me = here.y_lo * 2 + here.core
    cell = here.x * SIDE + here.z
    block = me * PLANE + cell
    columns = gates.shape[2]
    height = grad_ref.shape[0]
    rows, width = one_in.shape[0], one_in.shape[2]
    area = rows * width
    chunk = width // 2
    partner = here.at(core=1 - here.core)
    peers = list(here.token_peers())

    def column_peers():
        for dy in range(SIDE):
            for dc in range(2):
                if dy or dc:
                    yield dy * 2 + dc - 1, wrap(here.y + dy), (here.core + dc) % 2

    def plane_peers():
        for dx in range(SIDE):
            for dz in range(SIDE):
                if dx or dz:
                    yield wrap(here.x + dx), wrap(here.z + dz)

    barrier = pltpu.get_barrier_semaphore()
    for seq, _ in peers:
        pl.semaphore_signal(
            barrier, 1, device_id={"seq": seq, "ch": here.y_hi}, device_id_type=MESH
        )
    for y_lo in range(2):
        for core in range(2):
            there = here.at(y=(1 - here.y_hi) * 2 + y_lo, core=core)
            pl.semaphore_signal(barrier, 1, device_id=there, device_id_type=MESH)
    pl.semaphore_wait(barrier, len(peers) + 4)

    def weight_columns(y, core):
        return weight_ref.at[:, pl.ds(pl.multiple_of((y * 2 + core) * columns, columns), columns)]

    def gate_columns(index):
        return gate_ref.at[:, pl.ds(pl.multiple_of(index * columns, columns), columns)]

    own_rows = weights.at[here.y_lo, here.x, here.z, here.core * 2 + here.y_hi]
    for i, y, core in column_peers():
        send(
            weight_columns(y, core), own_rows, spread_s.at[i], spread_r.at[i],
            here.at(y=y, core=core),
        )
    copies = [
        pltpu.make_async_copy(weight_columns(here.y, here.core), own_rows, local.at[0]),
        pltpu.make_async_copy(grad_ref, feats.at[here.y_hi, me], local.at[1]),
        pltpu.make_async_copy(gate_columns(me), gates.at[me], local.at[2]),
    ]
    for copy in copies:
        copy.start()

    def feat(y, core):
        return feats.at[y // 2, (y % 2) * 2 + core]

    def half_tokens(ref, i):
        return ref.at[pl.ds(i * (height // 2), height // 2)]

    near_y = here.y_hi * 2 + 1 - here.y_lo
    far_y = wrap(here.y + 2 * here.y_lo - 1)
    opposite_y = wrap(here.y + 2)

    def feat_send(k, source, target, y):
        send(source, target, feat_s.at[k], feat_r.at[k], here.at(y=y))

    own_feat = feat(here.y, here.core)
    for i in range(2):
        feat_send(i, half_tokens(grad_ref, i), half_tokens(own_feat, i), near_y)
    feat_send(2, grad_ref, own_feat, far_y)

    def feat_relay(i):
        half = half_tokens(feat(near_y, here.core), i)
        await_bytes(half, feat_r.at[i])
        feat_send(3 + i, half, half, far_y)

    def pass_on(k, source, target):
        send(source, target, pass_s.at[k], pass_r.at[k], partner)

    pass_on(0, grad_ref, own_feat)
    share = [(0, 1), (1, 0), (1, 1)]

    def sharer(dy, dc):
        y_lo, core = (here.y_lo + dy) % 2, (here.core + dc) % 2
        return y_lo * 2 + core, here.at(y=here.y_hi * 2 + y_lo, core=core)

    for i, (dy, dc) in enumerate(share):
        index, device = sharer(dy, dc)
        send(gate_columns(index), gates.at[me], gate_s.at[i], gate_r.at[i], device)

    def exchange(batch, piece, arrive):
        for seq, other in peers:
            send(
                piece(seq, other), arrive, batch_s.at[batch], batch_r.at[batch],
                {"seq": seq, "ch": here.y_hi},
            )
        pltpu.make_async_copy(piece(here.seq, block), arrive, batch_r.at[batch]).start()

    span = 8

    def turn(value, put):
        @pl.loop(0, rows // span)
        def _(b):
            part = pl.ds(pl.multiple_of(b * span * width, span * width), span * width)
            lined = dot_t(eye_ref[...], value(part)).astype(BF16)
            put(pl.ds(b * span, span), lined.reshape(span, width, height))

    def into(out, k):
        def put(at, value):
            out[at, k] = value

        return put

    def into_two(at, value):
        two_out[at] = value

    def plain(ref):
        return lambda part: ref[:, part]

    def product(part):
        return (inner_ref[:, part].astype(F32) * medium_ref[:, part].astype(F32)).astype(BF16)

    def half_block(ref, i):
        return ref.at[pl.ds(i * 2, 2)]

    def block_ring(k, axis, item):
        return Ring(here, axis, item, half_block, ring_s.at[k], ring_r.at[k])

    first = [
        block_ring(0, "x", lambda x: weights.at[0, x, here.z]),
        block_ring(1, "z", lambda z: weights.at[1, here.x, z]),
    ]
    second = []
    for j, d in enumerate(ORDER):
        second.append((
            block_ring(2 + 2 * j, "z", lambda z, d=d: weights.at[0, wrap(here.x + d), z]),
            block_ring(3 + 2 * j, "x", lambda x, d=d: weights.at[1, x, wrap(here.z + d)]),
        ))

    turn(product, into(one_out, 0))
    turn(plain(filter_ref), into(one_out, 1))
    exchange(0, lambda seq, other: one_out.at[other], one_in.at[here.seq])

    for i, y, core in column_peers():
        source_y = wrap(2 * here.y - y + SIDE)
        await_bytes(
            weights.at[source_y % 2, here.x, here.z, core * 2 + source_y // 2], spread_r.at[i]
        )
    copies[0].wait()
    for ring in first:
        ring.start()
    for ring in second[0]:
        ring.start()
    turn(plain(inner_ref), into_two)
    for ring in first:
        ring.relay()
    for pair in second[1:3]:
        for ring in pair:
            ring.start()
    turn(plain(short_ref), into(three_out, 0))
    for ring in second[0]:
        ring.relay()
    for ring in first:
        ring.finish()
    for ring in second[3]:
        ring.start()
    feat_relay(0)
    turn(plain(conv_ref), into(three_out, 1))
    feat_relay(1)
    pass_on(1, feat(near_y, here.core), feat(near_y, here.core))

    def unpack(source, planes):
        @pl.loop(0, rows)
        def _(i):
            at = pl.ds(pl.multiple_of(i * width, width), width)
            for k, plane in planes:
                value = source[i] if k is None else source[i, k]
                lines[plane, at, :] = value.astype(F32)

    def keep(parts, places):
        for part, place in zip(parts, places):
            high, low = split(part)
            there = pl.ds(pl.multiple_of(place, rows), rows)
            yield there, high, low

    await_bytes(one_in, batch_r.at[0])
    unpack(one_in, ((0, 0), (1, 1)))
    for ring in second[1]:
        ring.relay()

    def spread_pairs(part):
        size = width // 4

        @pl.loop(part * size // 2, (part + 1) * size // 2)
        def _(b):
            for j in range(2):
                c = 2 * b + j
                pick = pl.ds(c, rows, stride=width)
                pair = jnp.concatenate([lines[0, pick, :], lines[1, pick, :]], 1).astype(BF16)
                parts = outer_stage(pair, first_ref[...], twists_ref[...])
                for there, high, low in keep(parts, (c * rows, area + c * rows)):
                    zh[there, :] = high
                    zl[there, :] = low

    spread_pairs(0)
    await_bytes(feat(far_y, here.core), feat_r.at[2])
    pass_on(2, feat(far_y, here.core), feat(far_y, here.core))
    for ring in second[2]:
        ring.relay()
    spread_pairs(1)
    for ring in second[3]:
        ring.relay()
    spread_pairs(2)
    for i in range(2):
        half = half_tokens(feat(opposite_y, here.core), i)
        await_bytes(half, feat_r.at[3 + i])
        pass_on(3 + i, half, half)
    spread_pairs(3)
    step = 512

    def transform_pairs(begin, end):
        @pl.loop(begin, end)
        def _(b):
            at = pl.ds(pl.multiple_of(b * step, step), step)
            spec[at, :] = dot3(zh[at, :], zl[at, :], forward_ref[...])

    halves = area // step
    transform_pairs(0, halves)

    other_core = 1 - here.core
    copies[1].wait()
    for k, y in ((0, here.y), (1, near_y), (2, far_y)):
        await_bytes(feat(y, other_core), pass_r.at[k])
    for i in range(2):
        await_bytes(half_tokens(feat(opposite_y, other_core), i), pass_r.at[3 + i])
    exchange(1, lambda seq, other: two_out.at[other], two_in.at[here.seq])
    rows_of = weights.shape[3] * weights.shape[4]
    depth = SIDE * rows_of
    for j, d in enumerate(ORDER):
        for ring in second[j]:
            ring.finish()
        x, z = wrap(here.x + d), wrap(here.z + d)
        left = feats[0, :, :, pl.ds(pl.multiple_of(x * depth, depth), depth)]
        term = dot(left.reshape(4 * height, depth), weights[0, x].reshape(depth, columns))
        if j == 0:
            total[...] = term
        else:
            total[...] += term
        left = jnp.concatenate(
            [
                feats[1, :, :, pl.ds(pl.multiple_of(k * depth + z * rows_of, rows_of), rows_of)]
                for k in range(SIDE)
            ],
            2,
        )
        total[...] += dot(
            left.reshape(4 * height, depth), weights[1, :, z].reshape(depth, columns)
        )

    copies[2].wait()
    for i, (dy, dc) in enumerate(share):
        await_bytes(gates.at[sharer(dy, dc)[0]], gate_r.at[i])
    block_size = eye_ref.shape[0]
    cells = block_size // width
    for g in range(4):
        part = total[g * height : (g + 1) * height]
        long_grad = (part * gates[g].astype(F32)).astype(BF16)
        for k in range(columns // block_size):
            lined = dot_t(eye_ref[...], long_grad[:, k * block_size : (k + 1) * block_size])
            turned[k * cells : (k + 1) * cells, g // 2, g % 2] = lined.astype(BF16).reshape(
                cells, width, height
            )
        hidden[g] = part.astype(BF16)
    pltpu.make_async_copy(turned.at[cell], late.at[:, cell], late_sem.at[1]).start()
    for x, z in plane_peers():
        send(
            turned.at[x * SIDE + z], late.at[:, cell], late_sem.at[0], late_sem.at[1],
            here.at(x=x, z=z),
        )
    exchange(2, lambda seq, other: three_out.at[other], three_in.at[here.seq])
    for i, (dy, dc) in enumerate(share):
        index, device = sharer(dy, dc)
        send(hidden.at[index], arrived.at[me], hidden_s.at[i], hidden_r.at[i], device)
    own = pltpu.make_async_copy(hidden.at[me], arrived.at[me], local.at[1])
    own.start()

    place = pl.multiple_of((me * PLANE + here.x * SIDE) * width, LANES)
    chosen = lax.broadcasted_iota(jnp.int32, (width, LANES), 1)
    chosen = chosen == lax.broadcasted_iota(jnp.int32, (width, LANES), 0) + here.z * width
    chosen = chosen.astype(F32).astype(BF16)
    taps[0] = dot_t(chosen, taps_medium_ref[:, pl.ds(place, LANES)])
    sums[0, : width // 4, :LANES] = jnp.zeros((width // 4, LANES), F32)
    sums[0, :SHORT, :LANES] = taps_short_ref[:, pl.ds(place, LANES)].astype(F32)
    padded = jnp.concatenate(
        [sums[0, : width // 4, :LANES], jnp.zeros((LANES - width // 4, LANES), F32)], 0
    )
    taps[1] = dot_t(chosen, padded.astype(BF16))

    @pl.loop(0, width)
    def _(c):
        wide = pl.ds(pl.multiple_of(c * LANES, LANES), LANES)
        for k in range(2):
            bands[k, wide, :] = toeplitz(taps[k, pl.ds(c, 1), :]).astype(BF16)

    transform_pairs(halves, 2 * halves)
    await_bytes(late, late_sem.at[1])
    for y_lo in range(2):
        @pl.loop(0, PLANE)
        def _(i):
            for core in range(2):
                place = ((y_lo * PLANE + i) * 2 + core) * width
                at = pl.ds(pl.multiple_of(place, width), width)
                lines[2, at, :] = late[y_lo, i, core].astype(F32)

    many = 4
    wide_step = many * rows
    row = lax.broadcasted_iota(jnp.int32, (rows, LANES), 0)

    def transform(start):
        @pl.loop(0, chunk // 2)
        def _(c):
            pair = jnp.concatenate(
                [lines[2, pl.ds(start + 2 * c + k, rows, stride=width), :] for k in range(2)], 1
            ).astype(BF16)
            parts = outer_stage(pair, first_ref[...], twists_ref[...])
            for there, high, low in keep(parts, (2 * c * rows, (2 * c + 1) * rows)):
                gh[there, :] = high
                gl[there, :] = low

        @pl.loop(0, chunk // many)
        def _(b):
            at = pl.ds(pl.multiple_of(b * wide_step, wide_step), wide_step)
            grad = dot3(gh[at, :], gl[at, :], forward_ref[...])
            grad_real, grad_imag = grad[:, :LANES], grad[:, LANES:]
            cosine = jnp.concatenate([twists_ref[:, :LANES]] * many, 0)
            sine = jnp.concatenate([twists_ref[:, LANES:]] * many, 0)
            reals, imags = [], []
            for k in range(2):
                place = (1 - k) * area + start * rows + b * wide_step
                other = spec[pl.ds(pl.multiple_of(place, wide_step), wide_step), :]
                real, imag = other[:, :LANES], other[:, LANES:]
                term = jnp.concatenate(
                    [real * grad_real + imag * grad_imag, real * grad_imag - imag * grad_real], 1
                )
                back = dot3(*split(term), inverse_ref[...])
                real, imag = back[:, :LANES], back[:, LANES:]
                reals.append(real * cosine - imag * sine)
                imags.append(real * sine + imag * cosine)
            real, imag = jnp.concatenate(reals, 1), jnp.concatenate(imags, 1)
            for k in range(many):
                both = jnp.concatenate(
                    [real[k * rows : (k + 1) * rows], imag[k * rows : (k + 1) * rows]], 0
                )
                high, low = split(both)
                there = pl.ds(pl.multiple_of((b * many + k) * 2 * rows, 2 * rows), 2 * rows)
                zh[there, :] = high
                zl[there, :] = low

        @pl.loop(0, chunk // many)
        def _(b):
            for k in range(many):
                within = b * many + k
                c = start + within
                there = pl.ds(pl.multiple_of(within * 2 * rows, 2 * rows), 2 * rows)
                high, low = zh[there, :], zl[there, :]
                both = (
                    dot(last_ref[:rows], high) + dot(last_ref[:rows], low)
                    + dot(last_ref[rows:], high)
                )
                pick = pl.ds(within, rows, stride=chunk)
                points[pl.ds(pl.multiple_of(c * rows, rows), rows), :] = both[:, :LANES]
                results[0, pick, :] = both[:, :LANES]
                results[1, pick, :] = both[:, LANES:]

    def pack(k, source, to):
        @pl.loop(0, rows)
        def _(i):
            at = pl.ds(pl.multiple_of(i * chunk, chunk), chunk)
            for a, b in zip(source, to):
                parcels[i, k, b] = results[a, at, :].astype(BF16)

    def pair_of(ref, k):
        return ref.at[k, pl.ds(0, 2)]

    for k in range(2):
        transform(k * chunk)
        pack(k, (0, 1), (0, 1))
        exchange(3 + k, lambda seq, other: pair_of(parcels.at[seq], k), pair_of(back_ref.at[block], k))

    await_bytes(two_in, batch_r.at[1])
    await_bytes(three_in, batch_r.at[2])

    @pl.loop(0, rows)
    def _(i):
        at = pl.ds(pl.multiple_of(i * width, width), width)
        lines[0, at, :] = two_in[i].astype(F32)
        for k in range(2):
            lines[1 + k, at, :] = three_in[i, k].astype(F32)

    def with_next(x):
        following = jnp.where(row == rows - 1, 0.0, pltpu.roll(x, rows - 1, 0))
        return jnp.concatenate([x, following], 1).astype(BF16)

    def diagonals(c, k, both):
        value = lines[1 + k, pl.ds(c, rows, stride=width), :].astype(BF16)
        products = dot(dot_t(flip_ref[...], value).astype(BF16), both)
        slid = pltpu.roll(products, 0, 1, stride=1, stride_axis=0)
        sums[k, pl.ds(c, 1), :] = jnp.sum(slid, axis=0, keepdims=True)

    @pl.loop(0, width // many)
    def _(b):
        for k in range(many):
            c = b * many + k
            wide = pl.ds(pl.multiple_of(c * LANES, LANES), LANES)
            there = pl.ds(pl.multiple_of(c * rows, rows), rows)
            gate = lines[0, pl.ds(c, rows, stride=width), :]
            both = with_next((points[there, :] * gate).astype(BF16).astype(F32))
            short_grad = dot_t(both, bands[0, wide, :]).astype(BF16).astype(F32)
            pair = with_next(short_grad)
            pairs[there, :] = pair
            diagonals(c, 0, both)
            diagonals(c, 1, pair)

    factor = (rows * LANES) ** -0.5
    lags = [pltpu.roll(sums[k], LANES + 1, 1)[:, :LANES] * factor for k in range(2)]
    square = jnp.concatenate([lags[1], jnp.zeros((LANES - width, LANES), F32)], 0)
    mine = lags_ref.at[here.y_lo, here.core]
    lags_ref[here.y_lo, here.core, here.x, here.z, :width] = lags[0].astype(BF16)
    lags_ref[here.y_lo, here.core, here.x, here.z, width:] = square.T[:PAD].astype(BF16)

    def lag_send(i, ref, device):
        send(ref, ref, lag_s.at[i], lag_r.at[i], device)

    for d in range(1, SIDE):
        lag_send(d - 1, mine.at[here.x, here.z], here.at(x=wrap(here.x + d)))

    def convolve(start):
        @pl.loop(0, chunk // many)
        def _(b):
            for k in range(many):
                within = b * many + k
                c = start + within
                wide = pl.ds(pl.multiple_of(c * LANES, LANES), LANES)
                there = pl.ds(pl.multiple_of(c * rows, rows), rows)
                results[0, pl.ds(within, rows, stride=chunk), :] = dot_t(
                    pairs[there, :], bands[1, wide, :]
                )

    for k in range(2):
        convolve(k * chunk)
        pack(k, (0,), (2,))
        if k == 0:
            for d in range(1, SIDE):
                await_bytes(mine.at[wrap(here.x - d), here.z], lag_r.at[d - 1])
            for d in range(1, SIDE):
                lag_send(2 + d, mine.at[:, here.z], here.at(z=wrap(here.z + d)))
        exchange(5 + k, lambda seq, other: parcels.at[seq, k, 2], back_ref.at[block, k, 2])

    for d in range(1, SIDE):
        await_bytes(mine.at[:, wrap(here.z - d)], lag_r.at[2 + d])
    lag_send(6, mine, here.at(y=near_y))
    lag_send(7, mine, partner)

    own.wait()
    for i, (dy, dc) in enumerate(share):
        await_bytes(arrived.at[sharer(dy, dc)[0]], hidden_r.at[i])
    for g in range(4):
        part = slice(g * columns, (g + 1) * columns)
        outer_ref[:, part] = (arrived[g].astype(F32) * long_ref[:, part].astype(F32)).astype(BF16)

    await_bytes(lags_ref.at[1 - here.y_lo, here.core], lag_r.at[6])
    lag_send(8, lags_ref.at[1 - here.y_lo, here.core], partner)
    await_bytes(lags_ref.at[here.y_lo, 1 - here.core], lag_r.at[7])
    await_bytes(lags_ref.at[1 - here.y_lo, 1 - here.core], lag_r.at[8])

    for k in range(2):
        await_bytes(back_ref.at[:, k, pl.ds(0, 2)], batch_r.at[3 + k])
        await_bytes(back_ref.at[:, k, 2], batch_r.at[5 + k])
    most = pl.ds(0, rows - 1)
    for k, ref in enumerate((one_out, two_out, three_out)):
        await_bytes(ref.at[most], batch_s.at[k])
    for k in range(2):
        await_bytes(parcels.at[most, k, pl.ds(0, 2)], batch_s.at[3 + k])
        await_bytes(parcels.at[most, k, 2], batch_s.at[5 + k])
    await_bytes(turned.at[pl.ds(0, PLANE - 1)], late_sem.at[0])
    for i in range(7):
        await_bytes(own_rows, spread_s.at[i])
    for i in range(3):
        await_bytes(gates.at[me], gate_s.at[i])
        await_bytes(hidden.at[me], hidden_s.at[i])
        await_bytes(mine.at[here.x, here.z], lag_s.at[i])
        await_bytes(mine.at[:, here.z], lag_s.at[3 + i])
        await_bytes(mine, lag_s.at[6 + i])
    for i in range(3):
        await_bytes(own_feat, pass_s.at[i])
    await_bytes(own_feat, feat_s.at[2])
    for i in range(2):
        half = half_tokens(own_feat, i)
        await_bytes(half, pass_s.at[3 + i])
        await_bytes(half, feat_s.at[i])
        await_bytes(half, feat_s.at[3 + i])
    for ring in first:
        ring.drain()
    for pair in second:
        for ring in pair:
            ring.drain()


def block_call(grad, weight, gate, long, channelwise, constants):
    height, half = grad.shape
    depth, model = weight.shape
    columns = model // 8
    width = columns // PLANE
    rows = half // width
    area = rows * width
    chunk = width // 2
    anywhere = pl.BlockSpec(memory_space=pl.ANY)
    near = pl.BlockSpec(memory_space=pltpu.VMEM)
    dma = pltpu.SemaphoreType.DMA
    vmem = pltpu.VMEM
    return pl.pallas_call(
        block_kernel,
        out_shape=(
            jax.ShapeDtypeStruct((height, half), BF16),
            jax.ShapeDtypeStruct((rows, 2, 3, chunk, height), BF16),
            jax.ShapeDtypeStruct((2, 2, SIDE, SIDE, width + PAD, height), BF16),
        ),
        in_specs=[anywhere] * 3 + [near] * (1 + len(channelwise) + len(constants)),
        out_specs=(near, anywhere, near),
        scratch_shapes=[
            vmem((2, 4, height, half), BF16),
            vmem((2, SIDE, SIDE, 4, depth, columns), BF16),
            vmem((4, height, columns), BF16),
            vmem((4 * height, columns), F32),
            vmem((PLANE, 2, 2, width, height), BF16),
            vmem((4, height, columns), BF16),
            vmem((4, height, columns), BF16),
            vmem((rows, 2, width, height), BF16),
            vmem((rows, 2, width, height), BF16),
            vmem((rows, width, height), BF16),
            vmem((rows, width, height), BF16),
            vmem((rows, 2, width, height), BF16),
            vmem((rows, 2, width, height), BF16),
            vmem((2, PLANE, 2, width, height), BF16),
            vmem((3, area, height), F32),
            vmem((2 * area, 2 * height), BF16),
            vmem((2 * area, 2 * height), BF16),
            vmem((area // 2, 2 * height), BF16),
            vmem((area // 2, 2 * height), BF16),
            vmem((2 * area, 2 * height), F32),
            vmem((2, width * LANES, 2 * LANES), BF16),
            vmem((2, width, LANES), F32),
            vmem((area, height), F32),
            vmem((area, 2 * height), BF16),
            vmem((2, area // 2, height), F32),
            vmem((2, width, 2 * LANES), F32),
            vmem((rows, 2, 3, chunk, height), BF16),
            dma((3,)), dma((7,)), dma((7,)), dma((3,)), dma((3,)), dma((5,)), dma((5,)),
            dma((5,)), dma((5,)), dma((10, 4)), dma((10, 4)), dma((2,)), dma((3,)), dma((3,)),
            dma((7,)), dma((7,)), dma((9,)), dma((9,)),
        ],
        compiler_params=pltpu.CompilerParams(
            collective_id=0, has_side_effects=True, vmem_limit_bytes=VMEM_LIMIT
        ),
        cost_estimate=pl.CostEstimate(
            flops=16 * 10**9, bytes_accessed=32 * 2**20, transcendentals=0
        ),
        name="block",
    )(grad, weight, gate, long, *channelwise, *constants)


def unturn_kernel(
    in_ref, lags_ref, medium_ref, eye_ref,
    inner_out, input_out, filter_out, lags_out, short_out,
):
    size, height = inner_out.shape[1], in_ref.shape[4]
    blocks = in_ref.shape[0]
    width = size // blocks

    def lined(value):
        return dot_t(eye_ref[...], value.reshape(size, height))

    inner_out[...] = (lined(in_ref[:, :, 0]) * medium_ref[...].astype(F32)).astype(BF16)
    filter_out[...] = lined(in_ref[:, :, 1])
    input_out[...] = lined(in_ref[:, :, 2]).astype(BF16)
    lags_out[...] = lined(lags_ref[:, :width])
    lane = lax.broadcasted_iota(jnp.int32, (height, size), 0)
    column = lax.broadcasted_iota(jnp.int32, (height, size), 1)
    short = jnp.zeros((PAD, size), F32)
    for b in range(blocks):
        place = (column == lane + b * width) & (lane < width)
        short += dot(lags_ref[b, width:], place.astype(F32).astype(BF16))
    short_out[...] = short[:SHORT]


def from_blocks(block, lags, medium_out):
    devices, parts, items, chunk, height = block.shape
    span = 8
    size = span * parts * chunk
    channels = devices * parts * chunk
    rows = pl.BlockSpec((height, size), lambda i: (0, i))
    eye = np.eye(height).astype(jnp.bfloat16)
    return pl.pallas_call(
        unturn_kernel,
        grid=(devices // span,),
        out_shape=[
            jax.ShapeDtypeStruct((height, channels), t) for t in (BF16, BF16, F32, F32)
        ] + [jax.ShapeDtypeStruct((SHORT, channels), F32)],
        in_specs=[
            pl.BlockSpec((span, parts, items, chunk, height), lambda i: (i, 0, 0, 0, 0)),
            pl.BlockSpec((span, lags.shape[1], height), lambda i: (i, 0, 0)),
            rows,
            pl.BlockSpec((height, height), lambda i: (0, 0)),
        ],
        out_specs=[rows] * 4 + [pl.BlockSpec((SHORT, size), lambda i: (0, i))],
        cost_estimate=pl.CostEstimate(
            flops=0, bytes_accessed=24 * height * channels, transcendentals=0
        ),
        name="from_blocks",
    )(block, lags, medium_out, eye)


def per_device(
    out_grad, out_weight, outer_gate, long_out, inner_gate, conv_input,
    short_out, medium_out, long_filter, taps_short, taps_medium,
):
    channels = outer_gate.shape[1]
    devices = lax.axis_size("seq")
    width = channels // devices
    grad_outer, results, lags = block_call(
        out_grad, out_weight, outer_gate, long_out,
        (inner_gate, medium_out, short_out, conv_input, long_filter, taps_short, taps_medium),
        tables(devices),
    )
    lags = lags.reshape(devices, width + PAD, LANES)
    grad_inner, grad_input, grad_filter, grad_medium, grad_short = from_blocks(
        results, lags, medium_out
    )
    return grad_outer, grad_inner, grad_input, grad_filter, grad_short, grad_medium


def solution(mesh):
    rows = P("seq", "ch")
    return jax.shard_map(
        per_device,
        mesh=mesh,
        in_specs=(rows, P(("seq", "ch"), None)) + (rows,) * 7 + (P(None, "ch"),) * 2,
        out_specs=(rows,) * 4 + (P(None, "ch"),) * 2,
        check_vma=False,
    )
```

```python
import math

import jax
import jax.numpy as jnp
import numpy as np
from jax import lax
from jax.experimental import pallas as pl
from jax.experimental.pallas import tpu as pltpu
from jax.sharding import PartitionSpec as P

SHORT = 7
MEDIUM = 128
LANES = 128
F32 = jnp.float32
BF16 = jnp.bfloat16
VMEM_LIMIT = 60 * 1024 * 1024
PAD = 16
SIDE = 4
PLANE = SIDE * SIDE
ORDER = (0, 3, 1, 2)
MESH = pl.DeviceIdType.MESH


def split_np(table):
    high = table.astype(np.float32).astype(jnp.bfloat16)
    low = (table - high.astype(np.float64)).astype(np.float32).astype(jnp.bfloat16)
    return high, low


def tables(rows):
    total = 2 * rows * LANES
    freq = np.arange(rows)[:, None] + 0.5
    place = np.arange(rows)[None, :]
    angle = 2.0 * np.pi * freq * place / (2 * rows)
    first = np.concatenate([np.cos(angle), -np.sin(angle)], 0)
    first = np.concatenate(split_np(first), 1)
    twist = 2.0 * np.pi * freq * np.arange(LANES)[None, :] / total
    inner = 2.0 * np.pi * np.outer(np.arange(LANES), np.arange(LANES)) / LANES
    cosine, sine = np.cos(inner), np.sin(inner)
    forward = np.block([[cosine, -sine], [sine, cosine]])
    inverse = np.block([[cosine, sine], [-sine, cosine]])
    scale = (rows * LANES) ** -0.5 * 2.0 / total
    last = np.concatenate([np.cos(angle.T), -np.sin(angle.T)], 1) * scale
    twists = np.concatenate([np.cos(twist), np.sin(twist)], 1).astype(np.float32)
    flip = np.eye(LANES)[::-1].astype(jnp.bfloat16)
    return (
        first,
        twists,
        np.concatenate(split_np(forward), 0),
        np.concatenate(split_np(inverse), 0),
        np.concatenate(split_np(last), 0),
        flip,
        np.eye(2 * LANES).astype(jnp.bfloat16),
    )


def dot(a, b):
    return jnp.dot(a, b, preferred_element_type=F32)


def dot_t(a, b):
    return lax.dot_general(a, b, (((1,), (1,)), ((), ())), preferred_element_type=F32)


def split(x):
    high = x.astype(BF16)
    return high, (x - high.astype(F32)).astype(BF16)


def dot3(high, low, table):
    size = table.shape[0] // 2
    return dot(high, table[:size]) + dot(high, table[size:]) + dot(low, table[:size])


def outer_stage(pair, first, twists):
    rows = pair.shape[0]
    spread = dot(first, jnp.concatenate([pair, pair], 0))
    cosine = jnp.concatenate([twists[:, :LANES]] * 2, 1)
    sine = jnp.concatenate([twists[:, LANES:]] * 2, 1)
    real, imag = spread[:rows], spread[rows:]
    new_real = real * cosine + imag * sine
    new_imag = imag * cosine - real * sine
    return (
        jnp.concatenate([new_real[:, :LANES], new_imag[:, :LANES]], 1),
        jnp.concatenate([new_real[:, LANES:], new_imag[:, LANES:]], 1),
    )


def toeplitz(line):
    row = jnp.concatenate([line, jnp.zeros_like(line)], 1)
    block = jnp.broadcast_to(row, (LANES, 2 * LANES))
    return pltpu.roll(block, 0, 1, stride=1, stride_axis=0)


def wrap(i):
    return lax.rem(i + SIDE, SIDE)


class Here:
    def __init__(self):
        seq = lax.axis_index("seq")
        self.seq = seq
        self.y_hi = lax.axis_index("ch")
        self.core = seq % 2
        self.z = (seq // 2) % SIDE
        self.x = (seq // (2 * SIDE)) % SIDE
        self.y_lo = seq // (2 * PLANE)
        self.y = self.y_hi * 2 + self.y_lo

    def token_peers(self):
        xs = [wrap(self.x + d) for d in range(SIDE)]
        zs = [wrap(self.z + d) for d in range(SIDE)]
        cores, ys = [self.core, 1 - self.core], [self.y_lo, 1 - self.y_lo]
        for dx in range(SIDE):
            for dz in range(SIDE):
                for dy in range(2):
                    for dc in range(2):
                        if dx or dz or dy or dc:
                            cell = xs[dx] * SIDE + zs[dz]
                            yield (
                                (ys[dy] * PLANE + cell) * 2 + cores[dc],
                                (ys[dy] * 2 + cores[dc]) * PLANE + cell,
                            )

    def at(self, x=None, y=None, z=None, core=None):
        x = self.x if x is None else x
        y = self.y if y is None else y
        z = self.z if z is None else z
        core = self.core if core is None else core
        seq = (((y % 2) * SIDE + x) * SIDE + z) * 2 + core
        return {"seq": seq, "ch": y // 2}


def send(source, target, sends, recvs, device):
    copy = pltpu.make_async_remote_copy(
        src_ref=source,
        dst_ref=target,
        send_sem=sends,
        recv_sem=recvs,
        device_id=device,
        device_id_type=MESH,
    )
    copy.start()


def await_bytes(ref, sem):
    pltpu.make_async_copy(ref, ref, sem).wait()


class Ring:
    def __init__(self, here, axis, item, half, sends, recvs, source=None):
        self.at = lambda p: here.at(**{axis: p})
        self.place = getattr(here, axis)
        self.item, self.half = item, half
        self.sends, self.recvs = sends, recvs
        self.source = item(self.place) if source is None else source

    def step(self, i, source, target, to):
        send(source, target, self.sends.at[i], self.recvs.at[i], self.at(wrap(self.place + to)))

    def start(self):
        self.step(0, self.source, self.item(self.place), 1)
        self.step(1, self.source, self.item(self.place), -1)

    def relay(self):
        for i, to in ((0, 1), (1, -1)):
            other = wrap(self.place - to)
            await_bytes(self.item(other), self.recvs.at[i])
            half = self.half(self.item(other), i)
            self.step(2 + i, half, half, to)

    def finish(self):
        opposite = self.item(wrap(self.place + 2))
        for i in range(2):
            await_bytes(self.half(opposite, i), self.recvs.at[2 + i])

    def drain(self):
        opposite = self.item(wrap(self.place + 2))
        for i in range(2):
            await_bytes(self.item(self.place), self.sends.at[i])
            await_bytes(self.half(opposite, i), self.sends.at[2 + i])


def block_kernel(
    grad_ref, weight_ref, gate_ref,
    inner_ref, medium_ref, short_ref, conv_ref, filter_ref, taps_short_ref, taps_medium_ref,
    first_ref, twists_ref, forward_ref, inverse_ref, last_ref, flip_ref, eye_ref,
    arrived, back_ref, lags_ref,
    feats, weights, gates, total, turned, hidden,
    one_out, one_in, two_out, two_in, three_out, three_in, late,
    lines, zh, zl, gh, gl, spec, bands, taps, points, pairs, results, sums, parcels,
    local, spread_s, spread_r, gate_s, gate_r, feat_s, feat_r, pass_s, pass_r,
    ring_s, ring_r, late_sem, hidden_s, hidden_r, batch_s, batch_r, lag_s, lag_r,
):
    here = Here()
    me = here.y_lo * 2 + here.core
    cell = here.x * SIDE + here.z
    block = me * PLANE + cell
    columns = gates.shape[2]
    height = grad_ref.shape[0]
    rows, width = one_in.shape[0], one_in.shape[2]
    area = rows * width
    chunk = width // 2
    partner = here.at(core=1 - here.core)
    peers = list(here.token_peers())

    def column_peers():
        for dy in range(SIDE):
            for dc in range(2):
                if dy or dc:
                    yield dy * 2 + dc - 1, wrap(here.y + dy), (here.core + dc) % 2

    def plane_peers():
        for dx in range(SIDE):
            for dz in range(SIDE):
                if dx or dz:
                    yield wrap(here.x + dx), wrap(here.z + dz)

    barrier = pltpu.get_barrier_semaphore()
    for seq, _ in peers:
        pl.semaphore_signal(
            barrier, 1, device_id={"seq": seq, "ch": here.y_hi}, device_id_type=MESH
        )
    for y_lo in range(2):
        for core in range(2):
            there = here.at(y=(1 - here.y_hi) * 2 + y_lo, core=core)
            pl.semaphore_signal(barrier, 1, device_id=there, device_id_type=MESH)
    pl.semaphore_wait(barrier, len(peers) + 4)

    def weight_columns(y, core):
        return weight_ref.at[:, pl.ds(pl.multiple_of((y * 2 + core) * columns, columns), columns)]

    def gate_columns(index):
        return gate_ref.at[:, pl.ds(pl.multiple_of(index * columns, columns), columns)]

    own_rows = weights.at[here.y_lo, here.x, here.z, here.core * 2 + here.y_hi]
    for i, y, core in column_peers():
        send(
            weight_columns(y, core), own_rows, spread_s.at[i], spread_r.at[i],
            here.at(y=y, core=core),
        )
    copies = [
        pltpu.make_async_copy(weight_columns(here.y, here.core), own_rows, local.at[0]),
        pltpu.make_async_copy(grad_ref, feats.at[here.y_hi, me], local.at[1]),
        pltpu.make_async_copy(gate_columns(me), gates.at[me], local.at[2]),
    ]
    for copy in copies:
        copy.start()

    def feat(y, core):
        return feats.at[y // 2, (y % 2) * 2 + core]

    def half_tokens(ref, i):
        return ref.at[pl.ds(i * (height // 2), height // 2)]

    near_y = here.y_hi * 2 + 1 - here.y_lo
    far_y = wrap(here.y + 2 * here.y_lo - 1)
    opposite_y = wrap(here.y + 2)

    def feat_send(k, source, target, y):
        send(source, target, feat_s.at[k], feat_r.at[k], here.at(y=y))

    own_feat = feat(here.y, here.core)
    for i in range(2):
        feat_send(i, half_tokens(grad_ref, i), half_tokens(own_feat, i), near_y)
    feat_send(2, grad_ref, own_feat, far_y)

    def feat_relay(i):
        half = half_tokens(feat(near_y, here.core), i)
        await_bytes(half, feat_r.at[i])
        feat_send(3 + i, half, half, far_y)

    def pass_on(k, source, target):
        send(source, target, pass_s.at[k], pass_r.at[k], partner)

    pass_on(0, grad_ref, own_feat)
    share = [(0, 1), (1, 0), (1, 1)]

    def sharer(dy, dc):
        y_lo, core = (here.y_lo + dy) % 2, (here.core + dc) % 2
        return y_lo * 2 + core, here.at(y=here.y_hi * 2 + y_lo, core=core)

    for i, (dy, dc) in enumerate(share):
        index, device = sharer(dy, dc)
        send(gate_columns(index), gates.at[me], gate_s.at[i], gate_r.at[i], device)

    def exchange(batch, piece, arrive):
        for seq, other in peers:
            send(
                piece(seq, other), arrive, batch_s.at[batch], batch_r.at[batch],
                {"seq": seq, "ch": here.y_hi},
            )
        pltpu.make_async_copy(piece(here.seq, block), arrive, batch_r.at[batch]).start()

    span = 8

    def turn(*jobs):
        @pl.loop(0, rows // (2 * span))
        def _(pair):
            for j in range(2):
                b = 2 * pair + j
                part = pl.ds(pl.multiple_of(b * span * width, span * width), span * width)
                for value, put in jobs:
                    lined = dot_t(eye_ref[...], value(part)).astype(BF16)
                    put(pl.ds(b * span, span), lined.reshape(span, width, height))

    def into(out, k):
        def put(at, value):
            out[at, k] = value

        return put

    def into_two(at, value):
        two_out[at] = value

    def plain(ref):
        return lambda part: ref[:, part]

    def product(part):
        return (inner_ref[:, part].astype(F32) * medium_ref[:, part].astype(F32)).astype(BF16)

    def half_block(ref, i):
        return ref.at[pl.ds(i * 2, 2)]

    def block_ring(k, axis, item):
        return Ring(here, axis, item, half_block, ring_s.at[k], ring_r.at[k])

    first = [
        block_ring(0, "x", lambda x: weights.at[0, x, here.z]),
        block_ring(1, "z", lambda z: weights.at[1, here.x, z]),
    ]
    second = []
    for j, d in enumerate(ORDER):
        second.append((
            block_ring(2 + 2 * j, "z", lambda z, d=d: weights.at[0, wrap(here.x + d), z]),
            block_ring(3 + 2 * j, "x", lambda x, d=d: weights.at[1, x, wrap(here.z + d)]),
        ))

    turn((product, into(one_out, 0)), (plain(filter_ref), into(one_out, 1)))
    exchange(0, lambda seq, other: one_out.at[other], one_in.at[here.seq])

    for i, y, core in column_peers():
        source_y = wrap(2 * here.y - y + SIDE)
        await_bytes(
            weights.at[source_y % 2, here.x, here.z, core * 2 + source_y // 2], spread_r.at[i]
        )
    copies[0].wait()
    for ring in first:
        ring.start()
    for ring in second[0]:
        ring.start()
    turn((plain(inner_ref), into_two))
    for ring in first:
        ring.relay()
    for pair in second[1:3]:
        for ring in pair:
            ring.start()
    turn((plain(short_ref), into(three_out, 0)))
    for ring in second[0]:
        ring.relay()
    for ring in first:
        ring.finish()
    for ring in second[3]:
        ring.start()
    feat_relay(0)
    turn((plain(conv_ref), into(three_out, 1)))
    feat_relay(1)
    pass_on(1, feat(near_y, here.core), feat(near_y, here.core))

    def unpack(source, planes):
        @pl.loop(0, rows // 4)
        def _(b):
            for j in range(4):
                i = 4 * b + j
                at = pl.ds(pl.multiple_of(i * width, width), width)
                for k, plane in planes:
                    lines[plane, at, :] = source[i, k].astype(F32)

    def keep(parts, places):
        for part, place in zip(parts, places):
            high, low = split(part)
            there = pl.ds(pl.multiple_of(place, rows), rows)
            yield there, high, low

    await_bytes(one_in, batch_r.at[0])
    unpack(one_in, ((0, 0), (1, 1)))
    for ring in second[1]:
        ring.relay()

    def spread_pairs(part):
        size = width // 4

        @pl.loop(part * size // 2, (part + 1) * size // 2)
        def _(b):
            for j in range(2):
                c = 2 * b + j
                pick = pl.ds(c, rows, stride=width)
                pair = jnp.concatenate([lines[0, pick, :], lines[1, pick, :]], 1).astype(BF16)
                parts = outer_stage(pair, first_ref[...], twists_ref[...])
                for there, high, low in keep(parts, (c * rows, area + c * rows)):
                    zh[there, :] = high
                    zl[there, :] = low

    spread_pairs(0)
    await_bytes(feat(far_y, here.core), feat_r.at[2])
    pass_on(2, feat(far_y, here.core), feat(far_y, here.core))
    for ring in second[2]:
        ring.relay()
    spread_pairs(1)
    for ring in second[3]:
        ring.relay()
    spread_pairs(2)
    for i in range(2):
        half = half_tokens(feat(opposite_y, here.core), i)
        await_bytes(half, feat_r.at[3 + i])
        pass_on(3 + i, half, half)
    spread_pairs(3)
    step = 512

    def transform_pairs(begin, end):
        @pl.loop(begin, end)
        def _(b):
            at = pl.ds(pl.multiple_of(b * step, step), step)
            spec[at, :] = dot3(zh[at, :], zl[at, :], forward_ref[...])

    halves = area // step
    transform_pairs(0, halves)

    other_core = 1 - here.core
    copies[1].wait()
    for k, y in ((0, here.y), (1, near_y), (2, far_y)):
        await_bytes(feat(y, other_core), pass_r.at[k])
    for i in range(2):
        await_bytes(half_tokens(feat(opposite_y, other_core), i), pass_r.at[3 + i])
    exchange(1, lambda seq, other: two_out.at[other], two_in.at[here.seq])
    rows_of = weights.shape[3] * weights.shape[4]
    depth = SIDE * rows_of
    for j, d in enumerate(ORDER):
        for ring in second[j]:
            ring.finish()
        x, z = wrap(here.x + d), wrap(here.z + d)
        left = feats[0, :, :, pl.ds(pl.multiple_of(x * depth, depth), depth)]
        term = dot(left.reshape(4 * height, depth), weights[0, x].reshape(depth, columns))
        if j == 0:
            total[...] = term
        else:
            total[...] += term
        left = jnp.concatenate(
            [
                feats[1, :, :, pl.ds(pl.multiple_of(k * depth + z * rows_of, rows_of), rows_of)]
                for k in range(SIDE)
            ],
            2,
        )
        total[...] += dot(
            left.reshape(4 * height, depth), weights[1, :, z].reshape(depth, columns)
        )

    copies[2].wait()
    for i, (dy, dc) in enumerate(share):
        await_bytes(gates.at[sharer(dy, dc)[0]], gate_r.at[i])
    block_size = eye_ref.shape[0]
    cells = block_size // width
    for g in range(4):
        part = total[g * height : (g + 1) * height]
        long_grad = (part * gates[g].astype(F32)).astype(BF16)
        for k in range(columns // block_size):
            lined = dot_t(eye_ref[...], long_grad[:, k * block_size : (k + 1) * block_size])
            turned[k * cells : (k + 1) * cells, g // 2, g % 2] = lined.astype(BF16).reshape(
                cells, width, height
            )
        hidden[g] = part.astype(BF16)
    pltpu.make_async_copy(turned.at[cell], late.at[:, cell], late_sem.at[1]).start()
    for x, z in plane_peers():
        send(
            turned.at[x * SIDE + z], late.at[:, cell], late_sem.at[0], late_sem.at[1],
            here.at(x=x, z=z),
        )
    exchange(2, lambda seq, other: three_out.at[other], three_in.at[here.seq])
    for i, (dy, dc) in enumerate(share):
        index, device = sharer(dy, dc)
        send(hidden.at[index], arrived.at[me], hidden_s.at[i], hidden_r.at[i], device)
    own = pltpu.make_async_copy(hidden.at[me], arrived.at[me], local.at[1])
    own.start()

    place = pl.multiple_of((me * PLANE + here.x * SIDE) * width, LANES)
    chosen = lax.broadcasted_iota(jnp.int32, (width, LANES), 1)
    chosen = chosen == lax.broadcasted_iota(jnp.int32, (width, LANES), 0) + here.z * width
    chosen = chosen.astype(F32).astype(BF16)
    taps[0] = dot_t(chosen, taps_medium_ref[:, pl.ds(place, LANES)])
    sums[0, : width // 4, :LANES] = jnp.zeros((width // 4, LANES), F32)
    sums[0, :SHORT, :LANES] = taps_short_ref[:, pl.ds(place, LANES)].astype(F32)
    padded = jnp.concatenate(
        [sums[0, : width // 4, :LANES], jnp.zeros((LANES - width // 4, LANES), F32)], 0
    )
    taps[1] = dot_t(chosen, padded.astype(BF16))

    @pl.loop(0, width)
    def _(c):
        wide = pl.ds(pl.multiple_of(c * LANES, LANES), LANES)
        for k in range(2):
            bands[k, wide, :] = toeplitz(taps[k, pl.ds(c, 1), :]).astype(BF16)

    transform_pairs(halves, 2 * halves)
    await_bytes(late, late_sem.at[1])
    for y_lo in range(2):
        @pl.loop(0, PLANE // 2)
        def _(b):
            for j in range(2):
                for core in range(2):
                    i = 2 * b + j
                    place = ((y_lo * PLANE + i) * 2 + core) * width
                    at = pl.ds(pl.multiple_of(place, width), width)
                    lines[2, at, :] = late[y_lo, i, core].astype(F32)

    many = 4
    wide_step = many * rows
    row = lax.broadcasted_iota(jnp.int32, (rows, LANES), 0)

    def transform(start):
        @pl.loop(0, chunk // 8)
        def _(b):
            for j in range(4):
                c = 4 * b + j
                pair = jnp.concatenate(
                    [lines[2, pl.ds(start + 2 * c + k, rows, stride=width), :] for k in range(2)], 1
                ).astype(BF16)
                parts = outer_stage(pair, first_ref[...], twists_ref[...])
                for there, high, low in keep(parts, (2 * c * rows, (2 * c + 1) * rows)):
                    gh[there, :] = high
                    gl[there, :] = low

        @pl.loop(0, chunk // many)
        def _(b):
            at = pl.ds(pl.multiple_of(b * wide_step, wide_step), wide_step)
            grad = dot3(gh[at, :], gl[at, :], forward_ref[...])
            grad_real, grad_imag = grad[:, :LANES], grad[:, LANES:]
            cosine = jnp.concatenate([twists_ref[:, :LANES]] * many, 0)
            sine = jnp.concatenate([twists_ref[:, LANES:]] * many, 0)
            reals, imags = [], []
            for k in range(2):
                place = (1 - k) * area + start * rows + b * wide_step
                other = spec[pl.ds(pl.multiple_of(place, wide_step), wide_step), :]
                real, imag = other[:, :LANES], other[:, LANES:]
                term = jnp.concatenate(
                    [real * grad_real + imag * grad_imag, real * grad_imag - imag * grad_real], 1
                )
                back = dot3(*split(term), inverse_ref[...])
                real, imag = back[:, :LANES], back[:, LANES:]
                reals.append(real * cosine - imag * sine)
                imags.append(real * sine + imag * cosine)
            real, imag = jnp.concatenate(reals, 1), jnp.concatenate(imags, 1)
            for k in range(many):
                both = jnp.concatenate(
                    [real[k * rows : (k + 1) * rows], imag[k * rows : (k + 1) * rows]], 0
                )
                high, low = split(both)
                there = pl.ds(pl.multiple_of((b * many + k) * 2 * rows, 2 * rows), 2 * rows)
                zh[there, :] = high
                zl[there, :] = low

        @pl.loop(0, chunk // many)
        def _(b):
            for k in range(many):
                within = b * many + k
                c = start + within
                there = pl.ds(pl.multiple_of(within * 2 * rows, 2 * rows), 2 * rows)
                high, low = zh[there, :], zl[there, :]
                both = (
                    dot(last_ref[:rows], high) + dot(last_ref[:rows], low)
                    + dot(last_ref[rows:], high)
                )
                pick = pl.ds(within, rows, stride=chunk)
                points[pl.ds(pl.multiple_of(c * rows, rows), rows), :] = both[:, :LANES]
                results[0, pick, :] = both[:, :LANES]
                results[1, pick, :] = both[:, LANES:]

    def pack(k, source, to):
        @pl.loop(0, rows // 8)
        def _(group):
            for j in range(8):
                i = 8 * group + j
                at = pl.ds(pl.multiple_of(i * chunk, chunk), chunk)
                for a, b in zip(source, to):
                    parcels[i, k, b] = results[a, at, :].astype(BF16)

    def pair_of(ref, k):
        return ref.at[k, pl.ds(0, 2)]

    for k in range(2):
        transform(k * chunk)
        pack(k, (0, 1), (0, 1))
        exchange(3 + k, lambda seq, other: pair_of(parcels.at[seq], k), pair_of(back_ref.at[block], k))

    await_bytes(two_in, batch_r.at[1])
    await_bytes(three_in, batch_r.at[2])

    @pl.loop(0, rows // 4)
    def _(b):
        for j in range(4):
            i = 4 * b + j
            at = pl.ds(pl.multiple_of(i * width, width), width)
            lines[0, at, :] = two_in[i].astype(F32)
            for k in range(2):
                lines[1 + k, at, :] = three_in[i, k].astype(F32)

    def with_next(x):
        following = jnp.where(row == rows - 1, 0.0, pltpu.roll(x, rows - 1, 0))
        return jnp.concatenate([x, following], 1).astype(BF16)

    def diagonals(c, k, both):
        value = lines[1 + k, pl.ds(c, rows, stride=width), :].astype(BF16)
        products = dot(dot_t(flip_ref[...], value).astype(BF16), both)
        slid = pltpu.roll(products, 0, 1, stride=1, stride_axis=0)
        sums[k, pl.ds(c, 1), :] = jnp.sum(slid, axis=0, keepdims=True)

    @pl.loop(0, width // many)
    def _(b):
        for k in range(many):
            c = b * many + k
            wide = pl.ds(pl.multiple_of(c * LANES, LANES), LANES)
            there = pl.ds(pl.multiple_of(c * rows, rows), rows)
            gate = lines[0, pl.ds(c, rows, stride=width), :]
            both = with_next((points[there, :] * gate).astype(BF16).astype(F32))
            short_grad = dot_t(both, bands[0, wide, :]).astype(BF16).astype(F32)
            pair = with_next(short_grad)
            pairs[there, :] = pair
            diagonals(c, 0, both)
            diagonals(c, 1, pair)

    factor = (rows * LANES) ** -0.5
    lags = [pltpu.roll(sums[k], LANES + 1, 1)[:, :LANES] * factor for k in range(2)]
    square = jnp.concatenate([lags[1], jnp.zeros((LANES - width, LANES), F32)], 0)
    mine = lags_ref.at[here.y_lo, here.core]
    lags_ref[here.y_lo, here.core, here.x, here.z, :width] = lags[0].astype(BF16)
    lags_ref[here.y_lo, here.core, here.x, here.z, width:] = square.T[:PAD].astype(BF16)

    def lag_send(i, ref, device):
        send(ref, ref, lag_s.at[i], lag_r.at[i], device)

    for d in range(1, SIDE):
        lag_send(d - 1, mine.at[here.x, here.z], here.at(x=wrap(here.x + d)))

    def convolve(start):
        @pl.loop(0, chunk // many)
        def _(b):
            for k in range(many):
                within = b * many + k
                c = start + within
                wide = pl.ds(pl.multiple_of(c * LANES, LANES), LANES)
                there = pl.ds(pl.multiple_of(c * rows, rows), rows)
                results[0, pl.ds(within, rows, stride=chunk), :] = dot_t(
                    pairs[there, :], bands[1, wide, :]
                )

    for k in range(2):
        convolve(k * chunk)
        pack(k, (0,), (2,))
        if k == 0:
            for d in range(1, SIDE):
                await_bytes(mine.at[wrap(here.x - d), here.z], lag_r.at[d - 1])
            for d in range(1, SIDE):
                lag_send(2 + d, mine.at[:, here.z], here.at(z=wrap(here.z + d)))
        else:
            for d in range(1, SIDE):
                await_bytes(mine.at[:, wrap(here.z - d)], lag_r.at[2 + d])
            lag_send(6, mine, here.at(y=near_y))
            lag_send(7, mine, partner)
        exchange(5 + k, lambda seq, other: parcels.at[seq, k, 2], back_ref.at[block, k, 2])

    own.wait()
    for i, (dy, dc) in enumerate(share):
        await_bytes(arrived.at[sharer(dy, dc)[0]], hidden_r.at[i])
    await_bytes(lags_ref.at[1 - here.y_lo, here.core], lag_r.at[6])
    lag_send(8, lags_ref.at[1 - here.y_lo, here.core], partner)
    await_bytes(lags_ref.at[here.y_lo, 1 - here.core], lag_r.at[7])
    await_bytes(lags_ref.at[1 - here.y_lo, 1 - here.core], lag_r.at[8])

    for k in range(2):
        await_bytes(back_ref.at[:, k, pl.ds(0, 2)], batch_r.at[3 + k])
        await_bytes(back_ref.at[:, k, 2], batch_r.at[5 + k])
    most = pl.ds(0, rows - 1)
    for k, ref in enumerate((one_out, two_out, three_out)):
        await_bytes(ref.at[most], batch_s.at[k])
    for k in range(2):
        await_bytes(parcels.at[most, k, pl.ds(0, 2)], batch_s.at[3 + k])
        await_bytes(parcels.at[most, k, 2], batch_s.at[5 + k])
    await_bytes(turned.at[pl.ds(0, PLANE - 1)], late_sem.at[0])
    for i in range(7):
        await_bytes(own_rows, spread_s.at[i])
    for i in range(3):
        await_bytes(gates.at[me], gate_s.at[i])
        await_bytes(hidden.at[me], hidden_s.at[i])
        await_bytes(mine.at[here.x, here.z], lag_s.at[i])
        await_bytes(mine.at[:, here.z], lag_s.at[3 + i])
        await_bytes(mine, lag_s.at[6 + i])
    for i in range(3):
        await_bytes(own_feat, pass_s.at[i])
    await_bytes(own_feat, feat_s.at[2])
    for i in range(2):
        half = half_tokens(own_feat, i)
        await_bytes(half, pass_s.at[3 + i])
        await_bytes(half, feat_s.at[i])
        await_bytes(half, feat_s.at[3 + i])
    for ring in first:
        ring.drain()
    for pair in second:
        for ring in pair:
            ring.drain()


def block_call(grad, weight, gate, channelwise, constants):
    height, half = grad.shape
    depth, model = weight.shape
    columns = model // 8
    width = columns // PLANE
    rows = half // width
    area = rows * width
    chunk = width // 2
    anywhere = pl.BlockSpec(memory_space=pl.ANY)
    near = pl.BlockSpec(memory_space=pltpu.VMEM)
    dma = pltpu.SemaphoreType.DMA
    vmem = pltpu.VMEM
    return pl.pallas_call(
        block_kernel,
        out_shape=(
            jax.ShapeDtypeStruct((4, height, columns), BF16),
            jax.ShapeDtypeStruct((rows, 2, 3, chunk, height), BF16),
            jax.ShapeDtypeStruct((2, 2, SIDE, SIDE, width + PAD, height), BF16),
        ),
        in_specs=[anywhere] * 3 + [near] * (len(channelwise) + len(constants)),
        out_specs=(anywhere, anywhere, near),
        scratch_shapes=[
            vmem((2, 4, height, half), BF16),
            vmem((2, SIDE, SIDE, 4, depth, columns), BF16),
            vmem((4, height, columns), BF16),
            vmem((4 * height, columns), F32),
            vmem((PLANE, 2, 2, width, height), BF16),
            vmem((4, height, columns), BF16),
            vmem((rows, 2, width, height), BF16),
            vmem((rows, 2, width, height), BF16),
            vmem((rows, width, height), BF16),
            vmem((rows, width, height), BF16),
            vmem((rows, 2, width, height), BF16),
            vmem((rows, 2, width, height), BF16),
            vmem((2, PLANE, 2, width, height), BF16),
            vmem((3, area, height), F32),
            vmem((2 * area, 2 * height), BF16),
            vmem((2 * area, 2 * height), BF16),
            vmem((area // 2, 2 * height), BF16),
            vmem((area // 2, 2 * height), BF16),
            vmem((2 * area, 2 * height), F32),
            vmem((2, width * LANES, 2 * LANES), BF16),
            vmem((2, width, LANES), F32),
            vmem((area, height), F32),
            vmem((area, 2 * height), BF16),
            vmem((2, area // 2, height), F32),
            vmem((2, width, 2 * LANES), F32),
            vmem((rows, 2, 3, chunk, height), BF16),
            dma((3,)), dma((7,)), dma((7,)), dma((3,)), dma((3,)), dma((5,)), dma((5,)),
            dma((5,)), dma((5,)), dma((10, 4)), dma((10, 4)), dma((2,)), dma((3,)), dma((3,)),
            dma((7,)), dma((7,)), dma((9,)), dma((9,)),
        ],
        compiler_params=pltpu.CompilerParams(
            collective_id=0, has_side_effects=True, vmem_limit_bytes=VMEM_LIMIT
        ),
        cost_estimate=pl.CostEstimate(
            flops=16 * 10**9, bytes_accessed=32 * 2**20, transcendentals=0
        ),
        name="block",
    )(grad, weight, gate, *channelwise, *constants)


def unturn_kernel(
    in_ref, lags_ref, medium_ref, hidden_ref, long_ref, eye_ref,
    outer_out, inner_out, input_out, filter_out, lags_out, short_out,
):
    size, height = inner_out.shape[1], in_ref.shape[4]
    blocks = in_ref.shape[0]
    width = size // blocks

    def lined(value):
        return dot_t(eye_ref[...], value.reshape(size, height))

    outer_out[...] = (hidden_ref[0].astype(F32) * long_ref[...].astype(F32)).astype(BF16)
    inner_out[...] = (lined(in_ref[:, :, 0]) * medium_ref[...].astype(F32)).astype(BF16)
    filter_out[...] = lined(in_ref[:, :, 1])
    input_out[...] = lined(in_ref[:, :, 2]).astype(BF16)
    lags_out[...] = lined(lags_ref[:, :width])
    lane = lax.broadcasted_iota(jnp.int32, (height, size), 0)
    column = lax.broadcasted_iota(jnp.int32, (height, size), 1)
    short = jnp.zeros((PAD, size), F32)
    for b in range(blocks):
        place = (column == lane + b * width) & (lane < width)
        short += dot(lags_ref[b, width:], place.astype(F32).astype(BF16))
    short_out[...] = short[:SHORT]


def from_blocks(block, lags, medium_out, hidden, long_out):
    devices, parts, items, chunk, height = block.shape
    span = devices // 4
    size = span * parts * chunk
    channels = devices * parts * chunk
    rows = pl.BlockSpec((height, size), lambda i: (0, i))
    eye = np.eye(height).astype(jnp.bfloat16)
    return pl.pallas_call(
        unturn_kernel,
        grid=(devices // span,),
        out_shape=[
            jax.ShapeDtypeStruct((height, channels), t) for t in (BF16, BF16, BF16, F32, F32)
        ] + [jax.ShapeDtypeStruct((SHORT, channels), F32)],
        in_specs=[
            pl.BlockSpec((span, parts, items, chunk, height), lambda i: (i, 0, 0, 0, 0)),
            pl.BlockSpec((span, lags.shape[1], height), lambda i: (i, 0, 0)),
            rows,
            pl.BlockSpec((1, height, size), lambda i: (i, 0, 0)),
            rows,
            pl.BlockSpec((height, height), lambda i: (0, 0)),
        ],
        out_specs=[rows] * 5 + [pl.BlockSpec((SHORT, size), lambda i: (0, i))],
        cost_estimate=pl.CostEstimate(
            flops=0, bytes_accessed=24 * height * channels, transcendentals=0
        ),
        name="from_blocks",
    )(block, lags, medium_out, hidden, long_out, eye)


def per_device(
    out_grad, out_weight, outer_gate, long_out, inner_gate, conv_input,
    short_out, medium_out, long_filter, taps_short, taps_medium,
):
    channels = outer_gate.shape[1]
    devices = lax.axis_size("seq")
    width = channels // devices
    hidden, results, lags = block_call(
        out_grad, out_weight, outer_gate,
        (inner_gate, medium_out, short_out, conv_input, long_filter, taps_short, taps_medium),
        tables(devices),
    )
    lags = lags.reshape(devices, width + PAD, LANES)
    outer, inner, short, filt, medium_taps, short_taps = from_blocks(
        results, lags, medium_out, hidden, long_out
    )
    return outer, inner, short, filt, short_taps, medium_taps


def solution(mesh):
    rows = P("seq", "ch")
    return jax.shard_map(
        per_device,
        mesh=mesh,
        in_specs=(rows, P(("seq", "ch"), None)) + (rows,) * 7 + (P(None, "ch"),) * 2,
        out_specs=(rows,) * 4 + (P(None, "ch"),) * 2,
        check_vma=False,
    )
```

```python
import math

import jax
import jax.numpy as jnp
import numpy as np
from jax import lax
from jax.experimental import pallas as pl
from jax.experimental.pallas import tpu as pltpu
from jax.sharding import PartitionSpec as P

SHORT = 7
MEDIUM = 128
LANES = 128
F32 = jnp.float32
BF16 = jnp.bfloat16
VMEM_LIMIT = 60 * 1024 * 1024
PAD = 16
SIDE = 4
PLANE = SIDE * SIDE
ORDER = (0, 3, 1, 2)
MESH = pl.DeviceIdType.MESH


def split_np(table):
    high = table.astype(np.float32).astype(jnp.bfloat16)
    low = (table - high.astype(np.float64)).astype(np.float32).astype(jnp.bfloat16)
    return high, low


def tables(rows):
    total = 2 * rows * LANES
    freq = np.arange(rows)[:, None] + 0.5
    place = np.arange(rows)[None, :]
    angle = 2.0 * np.pi * freq * place / (2 * rows)
    first = np.concatenate([np.cos(angle), -np.sin(angle)], 0)
    first = np.concatenate(split_np(first), 1)
    twist = 2.0 * np.pi * freq * np.arange(LANES)[None, :] / total
    inner = 2.0 * np.pi * np.outer(np.arange(LANES), np.arange(LANES)) / LANES
    cosine, sine = np.cos(inner), np.sin(inner)
    forward = np.block([[cosine, -sine], [sine, cosine]])
    inverse = np.block([[cosine, sine], [-sine, cosine]])
    scale = (rows * LANES) ** -0.5 * 2.0 / total
    last = np.concatenate([np.cos(angle.T), -np.sin(angle.T)], 1) * scale
    twists = np.concatenate([np.cos(twist), np.sin(twist)], 1).astype(np.float32)
    flip = np.eye(LANES)[::-1].astype(jnp.bfloat16)
    return (
        first,
        twists,
        np.concatenate(split_np(forward), 0),
        np.concatenate(split_np(inverse), 0),
        np.concatenate(split_np(last), 0),
        flip,
        np.eye(2 * LANES).astype(jnp.bfloat16),
    )


def dot(a, b):
    return jnp.dot(a, b, preferred_element_type=F32)


def dot_t(a, b):
    return lax.dot_general(a, b, (((1,), (1,)), ((), ())), preferred_element_type=F32)


def split(x):
    high = x.astype(BF16)
    return high, (x - high.astype(F32)).astype(BF16)


def dot3(high, low, table):
    size = table.shape[0] // 2
    return dot(high, table[:size]) + dot(high, table[size:]) + dot(low, table[:size])


def outer_stage(pair, first, twists):
    rows = pair.shape[0]
    spread = dot(first, jnp.concatenate([pair, pair], 0))
    cosine = jnp.concatenate([twists[:, :LANES]] * 2, 1)
    sine = jnp.concatenate([twists[:, LANES:]] * 2, 1)
    real, imag = spread[:rows], spread[rows:]
    new_real = real * cosine + imag * sine
    new_imag = imag * cosine - real * sine
    return (
        jnp.concatenate([new_real[:, :LANES], new_imag[:, :LANES]], 1),
        jnp.concatenate([new_real[:, LANES:], new_imag[:, LANES:]], 1),
    )


def toeplitz(line):
    row = jnp.concatenate([line, jnp.zeros_like(line)], 1)
    block = jnp.broadcast_to(row, (LANES, 2 * LANES))
    return pltpu.roll(block, 0, 1, stride=1, stride_axis=0)


def wrap(i):
    return lax.rem(i + SIDE, SIDE)


class Here:
    def __init__(self):
        seq = lax.axis_index("seq")
        self.seq = seq
        self.y_hi = lax.axis_index("ch")
        self.core = seq % 2
        self.z = (seq // 2) % SIDE
        self.x = (seq // (2 * SIDE)) % SIDE
        self.y_lo = seq // (2 * PLANE)
        self.y = self.y_hi * 2 + self.y_lo

    def token_peers(self):
        xs = [wrap(self.x + d) for d in range(SIDE)]
        zs = [wrap(self.z + d) for d in range(SIDE)]
        cores, ys = [self.core, 1 - self.core], [self.y_lo, 1 - self.y_lo]
        for dx in range(SIDE):
            for dz in range(SIDE):
                for dy in range(2):
                    for dc in range(2):
                        if dx or dz or dy or dc:
                            cell = xs[dx] * SIDE + zs[dz]
                            yield (
                                (ys[dy] * PLANE + cell) * 2 + cores[dc],
                                (ys[dy] * 2 + cores[dc]) * PLANE + cell,
                            )

    def at(self, x=None, y=None, z=None, core=None):
        x = self.x if x is None else x
        y = self.y if y is None else y
        z = self.z if z is None else z
        core = self.core if core is None else core
        seq = (((y % 2) * SIDE + x) * SIDE + z) * 2 + core
        return {"seq": seq, "ch": y // 2}


def send(source, target, sends, recvs, device):
    copy = pltpu.make_async_remote_copy(
        src_ref=source,
        dst_ref=target,
        send_sem=sends,
        recv_sem=recvs,
        device_id=device,
        device_id_type=MESH,
    )
    copy.start()


def await_bytes(ref, sem):
    pltpu.make_async_copy(ref, ref, sem).wait()


class Ring:
    def __init__(self, here, axis, item, half, sends, recvs, source=None):
        self.at = lambda p: here.at(**{axis: p})
        self.place = getattr(here, axis)
        self.item, self.half = item, half
        self.sends, self.recvs = sends, recvs
        self.source = item(self.place) if source is None else source

    def step(self, i, source, target, to):
        send(source, target, self.sends.at[i], self.recvs.at[i], self.at(wrap(self.place + to)))

    def start(self):
        self.step(0, self.source, self.item(self.place), 1)
        self.step(1, self.source, self.item(self.place), -1)

    def relay(self):
        for i, to in ((0, 1), (1, -1)):
            other = wrap(self.place - to)
            await_bytes(self.item(other), self.recvs.at[i])
            half = self.half(self.item(other), i)
            self.step(2 + i, half, half, to)

    def finish(self):
        opposite = self.item(wrap(self.place + 2))
        for i in range(2):
            await_bytes(self.half(opposite, i), self.recvs.at[2 + i])

    def drain(self):
        opposite = self.item(wrap(self.place + 2))
        for i in range(2):
            await_bytes(self.item(self.place), self.sends.at[i])
            await_bytes(self.half(opposite, i), self.sends.at[2 + i])


def block_kernel(
    grad_ref, weight_ref, gate_ref,
    inner_ref, medium_ref, short_ref, conv_ref, filter_ref, taps_short_ref, taps_medium_ref,
    first_ref, twists_ref, forward_ref, inverse_ref, last_ref, flip_ref, eye_ref,
    arrived, back_ref, lags_ref,
    feats, weights, gates, total, turned, hidden,
    one_out, one_in, two_out, two_in, three_out, three_in, late,
    lines, zh, zl, gh, gl, spec, bands, taps, points, boths, pairs, results, sums, parcels,
    local, spread_s, spread_r, gate_s, gate_r, feat_s, feat_r, pass_s, pass_r,
    ring_s, ring_r, late_sem, hidden_s, hidden_r, batch_s, batch_r, lag_s, lag_r,
):
    here = Here()
    me = here.y_lo * 2 + here.core
    cell = here.x * SIDE + here.z
    block = me * PLANE + cell
    columns = gates.shape[2]
    height = grad_ref.shape[0]
    rows, width = one_in.shape[0], one_in.shape[2]
    area = rows * width
    chunk = width // 2
    partner = here.at(core=1 - here.core)
    peers = list(here.token_peers())

    def column_peers():
        for dy in range(SIDE):
            for dc in range(2):
                if dy or dc:
                    yield dy * 2 + dc - 1, wrap(here.y + dy), (here.core + dc) % 2

    def plane_peers():
        for dx in range(SIDE):
            for dz in range(SIDE):
                if dx or dz:
                    yield wrap(here.x + dx), wrap(here.z + dz)

    barrier = pltpu.get_barrier_semaphore()
    for seq, _ in peers:
        pl.semaphore_signal(
            barrier, 1, device_id={"seq": seq, "ch": here.y_hi}, device_id_type=MESH
        )
    for y_lo in range(2):
        for core in range(2):
            there = here.at(y=(1 - here.y_hi) * 2 + y_lo, core=core)
            pl.semaphore_signal(barrier, 1, device_id=there, device_id_type=MESH)
    pl.semaphore_wait(barrier, len(peers) + 4)

    def weight_columns(y, core):
        return weight_ref.at[:, pl.ds(pl.multiple_of((y * 2 + core) * columns, columns), columns)]

    def gate_columns(index):
        return gate_ref.at[:, pl.ds(pl.multiple_of(index * columns, columns), columns)]

    own_rows = weights.at[here.y_lo, here.x, here.z, here.core * 2 + here.y_hi]
    for i, y, core in column_peers():
        send(
            weight_columns(y, core), own_rows, spread_s.at[i], spread_r.at[i],
            here.at(y=y, core=core),
        )
    copies = [
        pltpu.make_async_copy(weight_columns(here.y, here.core), own_rows, local.at[0]),
        pltpu.make_async_copy(grad_ref, feats.at[here.y_hi, me], local.at[1]),
        pltpu.make_async_copy(gate_columns(me), gates.at[me], local.at[2]),
    ]
    for copy in copies:
        copy.start()

    def feat(y, core):
        return feats.at[y // 2, (y % 2) * 2 + core]

    def half_tokens(ref, i):
        return ref.at[pl.ds(i * (height // 2), height // 2)]

    near_y = here.y_hi * 2 + 1 - here.y_lo
    far_y = wrap(here.y + 2 * here.y_lo - 1)
    opposite_y = wrap(here.y + 2)

    def feat_send(k, source, target, y):
        send(source, target, feat_s.at[k], feat_r.at[k], here.at(y=y))

    own_feat = feat(here.y, here.core)
    for i in range(2):
        feat_send(i, half_tokens(grad_ref, i), half_tokens(own_feat, i), near_y)
    feat_send(2, grad_ref, own_feat, far_y)

    def feat_relay(i):
        half = half_tokens(feat(near_y, here.core), i)
        await_bytes(half, feat_r.at[i])
        feat_send(3 + i, half, half, far_y)

    def pass_on(k, source, target):
        send(source, target, pass_s.at[k], pass_r.at[k], partner)

    pass_on(0, grad_ref, own_feat)
    share = [(0, 1), (1, 0), (1, 1)]

    def sharer(dy, dc):
        y_lo, core = (here.y_lo + dy) % 2, (here.core + dc) % 2
        return y_lo * 2 + core, here.at(y=here.y_hi * 2 + y_lo, core=core)

    for i, (dy, dc) in enumerate(share):
        index, device = sharer(dy, dc)
        send(gate_columns(index), gates.at[me], gate_s.at[i], gate_r.at[i], device)

    def exchange(batch, piece, arrive):
        for seq, other in peers:
            send(
                piece(seq, other), arrive, batch_s.at[batch], batch_r.at[batch],
                {"seq": seq, "ch": here.y_hi},
            )
        pltpu.make_async_copy(piece(here.seq, block), arrive, batch_r.at[batch]).start()

    span = 8

    def turn(*jobs):
        @pl.loop(0, rows // (2 * span))
        def _(pair):
            for j in range(2):
                b = 2 * pair + j
                part = pl.ds(pl.multiple_of(b * span * width, span * width), span * width)
                for value, put in jobs:
                    lined = dot_t(eye_ref[...], value(part)).astype(BF16)
                    put(pl.ds(b * span, span), lined.reshape(span, width, height))

    def into(out, k):
        def put(at, value):
            out[at, k] = value

        return put

    def into_two(at, value):
        two_out[at] = value

    def plain(ref):
        return lambda part: ref[:, part]

    def product(part):
        return (inner_ref[:, part].astype(F32) * medium_ref[:, part].astype(F32)).astype(BF16)

    def half_block(ref, i):
        return ref.at[pl.ds(i * 2, 2)]

    def block_ring(k, axis, item):
        return Ring(here, axis, item, half_block, ring_s.at[k], ring_r.at[k])

    first = [
        block_ring(0, "x", lambda x: weights.at[0, x, here.z]),
        block_ring(1, "z", lambda z: weights.at[1, here.x, z]),
    ]
    second = []
    for j, d in enumerate(ORDER):
        second.append((
            block_ring(2 + 2 * j, "z", lambda z, d=d: weights.at[0, wrap(here.x + d), z]),
            block_ring(3 + 2 * j, "x", lambda x, d=d: weights.at[1, x, wrap(here.z + d)]),
        ))

    turn((product, into(one_out, 0)), (plain(filter_ref), into(one_out, 1)))
    exchange(0, lambda seq, other: one_out.at[other], one_in.at[here.seq])

    for i, y, core in column_peers():
        source_y = wrap(2 * here.y - y + SIDE)
        await_bytes(
            weights.at[source_y % 2, here.x, here.z, core * 2 + source_y // 2], spread_r.at[i]
        )
    copies[0].wait()
    for ring in first:
        ring.start()
    for ring in second[0]:
        ring.start()
    turn((plain(inner_ref), into_two))
    for ring in first:
        ring.relay()
    for pair in second[1:3]:
        for ring in pair:
            ring.start()
    turn((plain(short_ref), into(three_out, 0)))
    for ring in second[0]:
        ring.relay()
    for ring in first:
        ring.finish()
    for ring in second[3]:
        ring.start()
    feat_relay(0)
    turn((plain(conv_ref), into(three_out, 1)))
    feat_relay(1)
    pass_on(1, feat(near_y, here.core), feat(near_y, here.core))

    def unpack(source, planes):
        @pl.loop(0, rows // 4)
        def _(b):
            for j in range(4):
                i = 4 * b + j
                at = pl.ds(pl.multiple_of(i * width, width), width)
                for k, plane in planes:
                    lines[plane, at, :] = source[i, k].astype(F32)

    def keep(parts, places):
        for part, place in zip(parts, places):
            high, low = split(part)
            there = pl.ds(pl.multiple_of(place, rows), rows)
            yield there, high, low

    await_bytes(one_in, batch_r.at[0])
    unpack(one_in, ((0, 0), (1, 1)))
    for ring in second[1]:
        ring.relay()

    def spread_pairs(part):
        size = width // 4

        @pl.loop(part * size // 2, (part + 1) * size // 2)
        def _(b):
            for j in range(2):
                c = 2 * b + j
                pick = pl.ds(c, rows, stride=width)
                pair = jnp.concatenate([lines[0, pick, :], lines[1, pick, :]], 1).astype(BF16)
                parts = outer_stage(pair, first_ref[...], twists_ref[...])
                for there, high, low in keep(parts, (c * rows, area + c * rows)):
                    zh[there, :] = high
                    zl[there, :] = low

    spread_pairs(0)
    await_bytes(feat(far_y, here.core), feat_r.at[2])
    pass_on(2, feat(far_y, here.core), feat(far_y, here.core))
    for ring in second[2]:
        ring.relay()
    spread_pairs(1)
    for ring in second[3]:
        ring.relay()
    spread_pairs(2)
    for i in range(2):
        half = half_tokens(feat(opposite_y, here.core), i)
        await_bytes(half, feat_r.at[3 + i])
        pass_on(3 + i, half, half)
    spread_pairs(3)
    step = 512

    def transform_pairs(begin, end):
        @pl.loop(begin, end)
        def _(b):
            at = pl.ds(pl.multiple_of(b * step, step), step)
            spec[at, :] = dot3(zh[at, :], zl[at, :], forward_ref[...])

    halves = area // step
    transform_pairs(0, halves)

    other_core = 1 - here.core
    copies[1].wait()
    for k, y in ((0, here.y), (1, near_y), (2, far_y)):
        await_bytes(feat(y, other_core), pass_r.at[k])
    for i in range(2):
        await_bytes(half_tokens(feat(opposite_y, other_core), i), pass_r.at[3 + i])
    exchange(1, lambda seq, other: two_out.at[other], two_in.at[here.seq])
    rows_of = weights.shape[3] * weights.shape[4]
    depth = SIDE * rows_of
    for j, d in enumerate(ORDER):
        for ring in second[j]:
            ring.finish()
        x, z = wrap(here.x + d), wrap(here.z + d)
        left = feats[0, :, :, pl.ds(pl.multiple_of(x * depth, depth), depth)]
        term = dot(left.reshape(4 * height, depth), weights[0, x].reshape(depth, columns))
        if j == 0:
            total[...] = term
        else:
            total[...] += term
        left = jnp.concatenate(
            [
                feats[1, :, :, pl.ds(pl.multiple_of(k * depth + z * rows_of, rows_of), rows_of)]
                for k in range(SIDE)
            ],
            2,
        )
        total[...] += dot(
            left.reshape(4 * height, depth), weights[1, :, z].reshape(depth, columns)
        )

    copies[2].wait()
    for i, (dy, dc) in enumerate(share):
        await_bytes(gates.at[sharer(dy, dc)[0]], gate_r.at[i])
    block_size = eye_ref.shape[0]
    cells = block_size // width
    for g in range(4):
        part = total[g * height : (g + 1) * height]
        long_grad = (part * gates[g].astype(F32)).astype(BF16)
        for k in range(columns // block_size):
            lined = dot_t(eye_ref[...], long_grad[:, k * block_size : (k + 1) * block_size])
            turned[k * cells : (k + 1) * cells, g // 2, g % 2] = lined.astype(BF16).reshape(
                cells, width, height
            )
        hidden[g] = part.astype(BF16)
    pltpu.make_async_copy(turned.at[cell], late.at[:, cell], late_sem.at[1]).start()
    for x, z in plane_peers():
        send(
            turned.at[x * SIDE + z], late.at[:, cell], late_sem.at[0], late_sem.at[1],
            here.at(x=x, z=z),
        )
    exchange(2, lambda seq, other: three_out.at[other], three_in.at[here.seq])
    for i, (dy, dc) in enumerate(share):
        index, device = sharer(dy, dc)
        send(hidden.at[index], arrived.at[me], hidden_s.at[i], hidden_r.at[i], device)
    own = pltpu.make_async_copy(hidden.at[me], arrived.at[me], local.at[1])
    own.start()

    place = pl.multiple_of((me * PLANE + here.x * SIDE) * width, LANES)
    chosen = lax.broadcasted_iota(jnp.int32, (width, LANES), 1)
    chosen = chosen == lax.broadcasted_iota(jnp.int32, (width, LANES), 0) + here.z * width
    chosen = chosen.astype(F32).astype(BF16)
    taps[0] = dot_t(chosen, taps_medium_ref[:, pl.ds(place, LANES)])
    sums[0, : width // 4, :LANES] = jnp.zeros((width // 4, LANES), F32)
    sums[0, :SHORT, :LANES] = taps_short_ref[:, pl.ds(place, LANES)].astype(F32)
    padded = jnp.concatenate(
        [sums[0, : width // 4, :LANES], jnp.zeros((LANES - width // 4, LANES), F32)], 0
    )
    taps[1] = dot_t(chosen, padded.astype(BF16))

    @pl.loop(0, width)
    def _(c):
        wide = pl.ds(pl.multiple_of(c * LANES, LANES), LANES)
        for k in range(2):
            bands[k, wide, :] = toeplitz(taps[k, pl.ds(c, 1), :]).astype(BF16)

    transform_pairs(halves, 2 * halves)
    await_bytes(late, late_sem.at[1])
    for y_lo in range(2):
        @pl.loop(0, PLANE // 2)
        def _(b):
            for j in range(2):
                for core in range(2):
                    i = 2 * b + j
                    place = ((y_lo * PLANE + i) * 2 + core) * width
                    at = pl.ds(pl.multiple_of(place, width), width)
                    lines[2, at, :] = late[y_lo, i, core].astype(F32)

    many = 4
    wide_step = many * rows
    row = lax.broadcasted_iota(jnp.int32, (rows, LANES), 0)

    def transform(start):
        @pl.loop(0, chunk // 8)
        def _(b):
            for j in range(4):
                c = 4 * b + j
                pair = jnp.concatenate(
                    [lines[2, pl.ds(start + 2 * c + k, rows, stride=width), :] for k in range(2)], 1
                ).astype(BF16)
                parts = outer_stage(pair, first_ref[...], twists_ref[...])
                for there, high, low in keep(parts, (2 * c * rows, (2 * c + 1) * rows)):
                    gh[there, :] = high
                    gl[there, :] = low

        @pl.loop(0, chunk // many)
        def _(b):
            at = pl.ds(pl.multiple_of(b * wide_step, wide_step), wide_step)
            grad = dot3(gh[at, :], gl[at, :], forward_ref[...])
            grad_real, grad_imag = grad[:, :LANES], grad[:, LANES:]
            cosine = jnp.concatenate([twists_ref[:, :LANES]] * many, 0)
            sine = jnp.concatenate([twists_ref[:, LANES:]] * many, 0)
            reals, imags = [], []
            for k in range(2):
                place = (1 - k) * area + start * rows + b * wide_step
                other = spec[pl.ds(pl.multiple_of(place, wide_step), wide_step), :]
                real, imag = other[:, :LANES], other[:, LANES:]
                term = jnp.concatenate(
                    [real * grad_real + imag * grad_imag, real * grad_imag - imag * grad_real], 1
                )
                back = dot3(*split(term), inverse_ref[...])
                real, imag = back[:, :LANES], back[:, LANES:]
                reals.append(real * cosine - imag * sine)
                imags.append(real * sine + imag * cosine)
            real, imag = jnp.concatenate(reals, 1), jnp.concatenate(imags, 1)
            for k in range(many):
                both = jnp.concatenate(
                    [real[k * rows : (k + 1) * rows], imag[k * rows : (k + 1) * rows]], 0
                )
                high, low = split(both)
                there = pl.ds(pl.multiple_of((b * many + k) * 2 * rows, 2 * rows), 2 * rows)
                zh[there, :] = high
                zl[there, :] = low

        @pl.loop(0, chunk // many)
        def _(b):
            for k in range(many):
                within = b * many + k
                c = start + within
                there = pl.ds(pl.multiple_of(within * 2 * rows, 2 * rows), 2 * rows)
                high, low = zh[there, :], zl[there, :]
                both = (
                    dot(last_ref[:rows], high) + dot(last_ref[:rows], low)
                    + dot(last_ref[rows:], high)
                )
                pick = pl.ds(within, rows, stride=chunk)
                points[pl.ds(pl.multiple_of(c * rows, rows), rows), :] = both[:, :LANES]
                results[0, pick, :] = both[:, :LANES]
                results[1, pick, :] = both[:, LANES:]

    def pack(k, source, to):
        @pl.loop(0, rows // 8)
        def _(group):
            for j in range(8):
                i = 8 * group + j
                at = pl.ds(pl.multiple_of(i * chunk, chunk), chunk)
                for a, b in zip(source, to):
                    parcels[i, k, b] = results[a, at, :].astype(BF16)

    def pair_of(ref, k):
        return ref.at[k, pl.ds(0, 2)]

    for k in range(2):
        transform(k * chunk)
        pack(k, (0, 1), (0, 1))
        exchange(3 + k, lambda seq, other: pair_of(parcels.at[seq], k), pair_of(back_ref.at[block], k))

    await_bytes(two_in, batch_r.at[1])

    @pl.loop(0, rows // 8)
    def _(b):
        for j in range(8):
            i = 8 * b + j
            at = pl.ds(pl.multiple_of(i * width, width), width)
            lines[0, at, :] = two_in[i].astype(F32)

    def with_next(x):
        following = jnp.where(row == rows - 1, 0.0, pltpu.roll(x, rows - 1, 0))
        return jnp.concatenate([x, following], 1).astype(BF16)

    def diagonals(c, k, both):
        value = lines[1 + k, pl.ds(c, rows, stride=width), :].astype(BF16)
        products = dot(dot_t(flip_ref[...], value).astype(BF16), both)
        slid = pltpu.roll(products, 0, 1, stride=1, stride_axis=0)
        sums[k, pl.ds(c, 1), :] = jnp.sum(slid, axis=0, keepdims=True)

    @pl.loop(0, width // many)
    def _(b):
        for k in range(many):
            c = b * many + k
            wide = pl.ds(pl.multiple_of(c * LANES, LANES), LANES)
            there = pl.ds(pl.multiple_of(c * rows, rows), rows)
            gate = lines[0, pl.ds(c, rows, stride=width), :]
            both = with_next((points[there, :] * gate).astype(BF16).astype(F32))
            short_grad = dot_t(both, bands[0, wide, :]).astype(BF16).astype(F32)
            pair = with_next(short_grad)
            boths[there, :] = both
            pairs[there, :] = pair

    await_bytes(three_in, batch_r.at[2])
    unpack(three_in, ((0, 1), (1, 2)))

    @pl.loop(0, width // many)
    def _(b):
        for k in range(many):
            c = b * many + k
            there = pl.ds(pl.multiple_of(c * rows, rows), rows)
            diagonals(c, 0, boths[there, :])
            diagonals(c, 1, pairs[there, :])

    factor = (rows * LANES) ** -0.5
    lags = [pltpu.roll(sums[k], LANES + 1, 1)[:, :LANES] * factor for k in range(2)]
    square = jnp.concatenate([lags[1], jnp.zeros((LANES - width, LANES), F32)], 0)
    mine = lags_ref.at[here.y_lo, here.core]
    lags_ref[here.y_lo, here.core, here.x, here.z, :width] = lags[0].astype(BF16)
    lags_ref[here.y_lo, here.core, here.x, here.z, width:] = square.T[:PAD].astype(BF16)

    def lag_send(i, ref, device):
        send(ref, ref, lag_s.at[i], lag_r.at[i], device)

    own_lags = mine.at[here.x, here.z]
    for dx in range(SIDE):
        for dz in range(SIDE):
            x, z = wrap(here.x + dx), wrap(here.z + dz)
            lag_send(7, own_lags, here.at(y=near_y, x=x, z=z))
            if dx or dz:
                lag_send(dx - 1 if dx else 2 + dz, own_lags, here.at(x=x, z=z))

    def convolve(start):
        @pl.loop(0, chunk // many)
        def _(b):
            for k in range(many):
                within = b * many + k
                c = start + within
                wide = pl.ds(pl.multiple_of(c * LANES, LANES), LANES)
                there = pl.ds(pl.multiple_of(c * rows, rows), rows)
                results[0, pl.ds(within, rows, stride=chunk), :] = dot_t(
                    pairs[there, :], bands[1, wide, :]
                )

    for k in range(2):
        convolve(k * chunk)
        pack(k, (0,), (2,))
        exchange(5 + k, lambda seq, other: parcels.at[seq, k, 2], back_ref.at[block, k, 2])

    own.wait()
    for i, (dy, dc) in enumerate(share):
        await_bytes(arrived.at[sharer(dy, dc)[0]], hidden_r.at[i])
    for d in range(1, SIDE):
        await_bytes(mine.at[wrap(here.x - d)], lag_r.at[d - 1])
        await_bytes(mine.at[here.x, wrap(here.z - d)], lag_r.at[2 + d])
    lag_send(6, mine, partner)
    across = lags_ref.at[1 - here.y_lo, here.core]
    await_bytes(across, lag_r.at[7])
    lag_send(8, across, partner)
    await_bytes(lags_ref.at[here.y_lo, 1 - here.core], lag_r.at[6])
    await_bytes(lags_ref.at[1 - here.y_lo, 1 - here.core], lag_r.at[8])

    for k in range(2):
        await_bytes(back_ref.at[:, k, pl.ds(0, 2)], batch_r.at[3 + k])
        await_bytes(back_ref.at[:, k, 2], batch_r.at[5 + k])
    most = pl.ds(0, rows - 1)
    for k, ref in enumerate((one_out, two_out, three_out)):
        await_bytes(ref.at[most], batch_s.at[k])
    for k in range(2):
        await_bytes(parcels.at[most, k, pl.ds(0, 2)], batch_s.at[3 + k])
        await_bytes(parcels.at[most, k, 2], batch_s.at[5 + k])
    await_bytes(turned.at[pl.ds(0, PLANE - 1)], late_sem.at[0])
    for i in range(7):
        await_bytes(own_rows, spread_s.at[i])
    for i in range(3):
        await_bytes(gates.at[me], gate_s.at[i])
        await_bytes(hidden.at[me], hidden_s.at[i])
        await_bytes(mine.at[here.x], lag_s.at[i])
        await_bytes(own_lags, lag_s.at[3 + i])
        await_bytes(mine, lag_s.at[6 + i])
    for i in range(3):
        await_bytes(own_feat, pass_s.at[i])
    await_bytes(own_feat, feat_s.at[2])
    for i in range(2):
        half = half_tokens(own_feat, i)
        await_bytes(half, pass_s.at[3 + i])
        await_bytes(half, feat_s.at[i])
        await_bytes(half, feat_s.at[3 + i])
    for ring in first:
        ring.drain()
    for pair in second:
        for ring in pair:
            ring.drain()


def block_call(grad, weight, gate, channelwise, constants):
    height, half = grad.shape
    depth, model = weight.shape
    columns = model // 8
    width = columns // PLANE
    rows = half // width
    area = rows * width
    chunk = width // 2
    anywhere = pl.BlockSpec(memory_space=pl.ANY)
    near = pl.BlockSpec(memory_space=pltpu.VMEM)
    dma = pltpu.SemaphoreType.DMA
    vmem = pltpu.VMEM
    return pl.pallas_call(
        block_kernel,
        out_shape=(
            jax.ShapeDtypeStruct((4, height, columns), BF16),
            jax.ShapeDtypeStruct((rows, 2, 3, chunk, height), BF16),
            jax.ShapeDtypeStruct((2, 2, SIDE, SIDE, width + PAD, height), BF16),
        ),
        in_specs=[anywhere] * 3 + [near] * (len(channelwise) + len(constants)),
        out_specs=(anywhere, anywhere, near),
        scratch_shapes=[
            vmem((2, 4, height, half), BF16),
            vmem((2, SIDE, SIDE, 4, depth, columns), BF16),
            vmem((4, height, columns), BF16),
            vmem((4 * height, columns), F32),
            vmem((PLANE, 2, 2, width, height), BF16),
            vmem((4, height, columns), BF16),
            vmem((rows, 2, width, height), BF16),
            vmem((rows, 2, width, height), BF16),
            vmem((rows, width, height), BF16),
            vmem((rows, width, height), BF16),
            vmem((rows, 2, width, height), BF16),
            vmem((rows, 2, width, height), BF16),
            vmem((2, PLANE, 2, width, height), BF16),
            vmem((3, area, height), F32),
            vmem((2 * area, 2 * height), BF16),
            vmem((2 * area, 2 * height), BF16),
            vmem((area // 2, 2 * height), BF16),
            vmem((area // 2, 2 * height), BF16),
            vmem((2 * area, 2 * height), F32),
            vmem((2, width * LANES, 2 * LANES), BF16),
            vmem((2, width, LANES), F32),
            vmem((area, height), F32),
            vmem((area, 2 * height), BF16),
            vmem((area, 2 * height), BF16),
            vmem((2, area // 2, height), F32),
            vmem((2, width, 2 * LANES), F32),
            vmem((rows, 2, 3, chunk, height), BF16),
            dma((3,)), dma((7,)), dma((7,)), dma((3,)), dma((3,)), dma((5,)), dma((5,)),
            dma((5,)), dma((5,)), dma((10, 4)), dma((10, 4)), dma((2,)), dma((3,)), dma((3,)),
            dma((7,)), dma((7,)), dma((9,)), dma((9,)),
        ],
        compiler_params=pltpu.CompilerParams(
            collective_id=0, has_side_effects=True, vmem_limit_bytes=VMEM_LIMIT
        ),
        cost_estimate=pl.CostEstimate(
            flops=16 * 10**9, bytes_accessed=32 * 2**20, transcendentals=0
        ),
        name="block",
    )(grad, weight, gate, *channelwise, *constants)


def unturn_kernel(
    in_ref, lags_ref, medium_ref, hidden_ref, long_ref, eye_ref,
    outer_out, inner_out, input_out, filter_out, lags_out, short_out,
):
    size, height = inner_out.shape[1], in_ref.shape[4]
    blocks = in_ref.shape[0]
    width = size // blocks

    def lined(value):
        return dot_t(eye_ref[...], value.reshape(size, height))

    outer_out[...] = (hidden_ref[0].astype(F32) * long_ref[...].astype(F32)).astype(BF16)
    inner_out[...] = (lined(in_ref[:, :, 0]) * medium_ref[...].astype(F32)).astype(BF16)
    filter_out[...] = lined(in_ref[:, :, 1])
    input_out[...] = lined(in_ref[:, :, 2]).astype(BF16)
    lags_out[...] = lined(lags_ref[:, :width])
    lane = lax.broadcasted_iota(jnp.int32, (height, size), 0)
    column = lax.broadcasted_iota(jnp.int32, (height, size), 1)
    short = jnp.zeros((PAD, size), F32)
    for b in range(blocks):
        place = (column == lane + b * width) & (lane < width)
        short += dot(lags_ref[b, width:], place.astype(F32).astype(BF16))
    short_out[...] = short[:SHORT]


def from_blocks(block, lags, medium_out, hidden, long_out):
    devices, parts, items, chunk, height = block.shape
    span = devices // 4
    size = span * parts * chunk
    channels = devices * parts * chunk
    rows = pl.BlockSpec((height, size), lambda i: (0, i))
    eye = np.eye(height).astype(jnp.bfloat16)
    return pl.pallas_call(
        unturn_kernel,
        grid=(devices // span,),
        out_shape=[
            jax.ShapeDtypeStruct((height, channels), t) for t in (BF16, BF16, BF16, F32, F32)
        ] + [jax.ShapeDtypeStruct((SHORT, channels), F32)],
        in_specs=[
            pl.BlockSpec((span, parts, items, chunk, height), lambda i: (i, 0, 0, 0, 0)),
            pl.BlockSpec((span, lags.shape[1], height), lambda i: (i, 0, 0)),
            rows,
            pl.BlockSpec((1, height, size), lambda i: (i, 0, 0)),
            rows,
            pl.BlockSpec((height, height), lambda i: (0, 0)),
        ],
        out_specs=[rows] * 5 + [pl.BlockSpec((SHORT, size), lambda i: (0, i))],
        cost_estimate=pl.CostEstimate(
            flops=0, bytes_accessed=24 * height * channels, transcendentals=0
        ),
        name="from_blocks",
    )(block, lags, medium_out, hidden, long_out, eye)


def per_device(
    out_grad, out_weight, outer_gate, long_out, inner_gate, conv_input,
    short_out, medium_out, long_filter, taps_short, taps_medium,
):
    channels = outer_gate.shape[1]
    devices = lax.axis_size("seq")
    width = channels // devices
    hidden, results, lags = block_call(
        out_grad, out_weight, outer_gate,
        (inner_gate, medium_out, short_out, conv_input, long_filter, taps_short, taps_medium),
        tables(devices),
    )
    lags = lags.reshape(devices, width + PAD, LANES)
    outer, inner, short, filt, medium_taps, short_taps = from_blocks(
        results, lags, medium_out, hidden, long_out
    )
    return outer, inner, short, filt, short_taps, medium_taps


def solution(mesh):
    rows = P("seq", "ch")
    return jax.shard_map(
        per_device,
        mesh=mesh,
        in_specs=(rows, P(("seq", "ch"), None)) + (rows,) * 7 + (P(None, "ch"),) * 2,
        out_specs=(rows,) * 4 + (P(None, "ch"),) * 2,
        check_vma=False,
    )
```

```python
import math

import jax
import jax.numpy as jnp
import numpy as np
from jax import lax
from jax.experimental import pallas as pl
from jax.experimental.pallas import tpu as pltpu
from jax.sharding import PartitionSpec as P

SHORT = 7
MEDIUM = 128
LANES = 128
F32 = jnp.float32
BF16 = jnp.bfloat16
VMEM_LIMIT = 60 * 1024 * 1024
PAD = 16
SIDE = 4
PLANE = SIDE * SIDE
ORDER = (0, 3, 1, 2)
MESH = pl.DeviceIdType.MESH


def split_np(table):
    high = table.astype(np.float32).astype(jnp.bfloat16)
    low = (table - high.astype(np.float64)).astype(np.float32).astype(jnp.bfloat16)
    return high, low


def tables(rows):
    total = 2 * rows * LANES
    freq = np.arange(rows)[:, None] + 0.5
    place = np.arange(rows)[None, :]
    angle = 2.0 * np.pi * freq * place / (2 * rows)
    first = np.concatenate([np.cos(angle), -np.sin(angle)], 0)
    first = np.concatenate(split_np(first), 1)
    twist = 2.0 * np.pi * freq * np.arange(LANES)[None, :] / total
    inner = 2.0 * np.pi * np.outer(np.arange(LANES), np.arange(LANES)) / LANES
    cosine, sine = np.cos(inner), np.sin(inner)
    forward = np.block([[cosine, -sine], [sine, cosine]])
    inverse = np.block([[cosine, sine], [-sine, cosine]])
    scale = (rows * LANES) ** -0.5 * 2.0 / total
    last = np.concatenate([np.cos(angle.T), -np.sin(angle.T)], 1) * scale
    twists = np.concatenate([np.cos(twist), np.sin(twist)], 1).astype(np.float32)
    flip = np.eye(LANES)[::-1].astype(jnp.bfloat16)
    return (
        first,
        twists,
        np.concatenate(split_np(forward), 0),
        np.concatenate(split_np(inverse), 0),
        np.concatenate(split_np(last), 0),
        flip,
        np.eye(2 * LANES).astype(jnp.bfloat16),
    )


def dot(a, b):
    return jnp.dot(a, b, preferred_element_type=F32)


def dot_t(a, b):
    return lax.dot_general(a, b, (((1,), (1,)), ((), ())), preferred_element_type=F32)


def split(x):
    high = x.astype(BF16)
    return high, (x - high.astype(F32)).astype(BF16)


def dot3(high, low, table):
    size = table.shape[0] // 2
    return dot(high, table[:size]) + dot(high, table[size:]) + dot(low, table[:size])


def outer_stage(pair, first, twists):
    rows = pair.shape[0]
    spread = dot(first, jnp.concatenate([pair, pair], 0))
    cosine = jnp.concatenate([twists[:, :LANES]] * 2, 1)
    sine = jnp.concatenate([twists[:, LANES:]] * 2, 1)
    real, imag = spread[:rows], spread[rows:]
    new_real = real * cosine + imag * sine
    new_imag = imag * cosine - real * sine
    return (
        jnp.concatenate([new_real[:, :LANES], new_imag[:, :LANES]], 1),
        jnp.concatenate([new_real[:, LANES:], new_imag[:, LANES:]], 1),
    )


def toeplitz(line):
    row = jnp.concatenate([line, jnp.zeros_like(line)], 1)
    block = jnp.broadcast_to(row, (LANES, 2 * LANES))
    return pltpu.roll(block, 0, 1, stride=1, stride_axis=0)


def wrap(i):
    return lax.rem(i + SIDE, SIDE)


class Here:
    def __init__(self):
        seq = lax.axis_index("seq")
        self.seq = seq
        self.y_hi = lax.axis_index("ch")
        self.core = seq % 2
        self.z = (seq // 2) % SIDE
        self.x = (seq // (2 * SIDE)) % SIDE
        self.y_lo = seq // (2 * PLANE)
        self.y = self.y_hi * 2 + self.y_lo

    def token_peers(self):
        xs = [wrap(self.x + d) for d in range(SIDE)]
        zs = [wrap(self.z + d) for d in range(SIDE)]
        cores, ys = [self.core, 1 - self.core], [self.y_lo, 1 - self.y_lo]
        for dx in range(SIDE):
            for dz in range(SIDE):
                for dy in range(2):
                    for dc in range(2):
                        if dx or dz or dy or dc:
                            cell = xs[dx] * SIDE + zs[dz]
                            yield (
                                (ys[dy] * PLANE + cell) * 2 + cores[dc],
                                (ys[dy] * 2 + cores[dc]) * PLANE + cell,
                            )

    def at(self, x=None, y=None, z=None, core=None):
        x = self.x if x is None else x
        y = self.y if y is None else y
        z = self.z if z is None else z
        core = self.core if core is None else core
        seq = (((y % 2) * SIDE + x) * SIDE + z) * 2 + core
        return {"seq": seq, "ch": y // 2}


def send(source, target, sends, recvs, device):
    copy = pltpu.make_async_remote_copy(
        src_ref=source,
        dst_ref=target,
        send_sem=sends,
        recv_sem=recvs,
        device_id=device,
        device_id_type=MESH,
    )
    copy.start()


def await_bytes(ref, sem):
    pltpu.make_async_copy(ref, ref, sem).wait()


class Ring:
    def __init__(self, here, axis, item, half, sends, recvs, source=None):
        self.at = lambda p: here.at(**{axis: p})
        self.place = getattr(here, axis)
        self.item, self.half = item, half
        self.sends, self.recvs = sends, recvs
        self.source = item(self.place) if source is None else source

    def step(self, i, source, target, to):
        send(source, target, self.sends.at[i], self.recvs.at[i], self.at(wrap(self.place + to)))

    def start(self):
        self.step(0, self.source, self.item(self.place), 1)
        self.step(1, self.source, self.item(self.place), -1)

    def relay(self):
        for i, to in ((0, 1), (1, -1)):
            other = wrap(self.place - to)
            await_bytes(self.item(other), self.recvs.at[i])
            half = self.half(self.item(other), i)
            self.step(2 + i, half, half, to)

    def finish(self):
        opposite = self.item(wrap(self.place + 2))
        for i in range(2):
            await_bytes(self.half(opposite, i), self.recvs.at[2 + i])

    def drain(self):
        opposite = self.item(wrap(self.place + 2))
        for i in range(2):
            await_bytes(self.item(self.place), self.sends.at[i])
            await_bytes(self.half(opposite, i), self.sends.at[2 + i])


def block_kernel(
    grad_ref, weight_ref, gate_ref,
    inner_ref, medium_ref, short_ref, conv_ref, filter_ref, taps_short_ref, taps_medium_ref,
    first_ref, twists_ref, forward_ref, inverse_ref, last_ref, flip_ref, eye_ref,
    arrived, back_ref, lags_ref,
    feats, weights, gates, total, turned, hidden,
    one_out, one_in, two_out, two_in, three_out, three_in, late,
    lines, zh, zl, gh, gl, spec, bands, taps, points, boths, pairs, results, sums, parcels,
    local, spread_s, spread_r, gate_s, gate_r, feat_s, feat_r, pass_s, pass_r,
    ring_s, ring_r, late_sem, hidden_s, hidden_r, batch_s, batch_r, lag_s, lag_r,
):
    here = Here()
    me = here.y_lo * 2 + here.core
    cell = here.x * SIDE + here.z
    block = me * PLANE + cell
    columns = gates.shape[2]
    height = grad_ref.shape[0]
    rows, width = one_in.shape[0], one_in.shape[2]
    area = rows * width
    chunk = width // 2
    partner = here.at(core=1 - here.core)
    peers = list(here.token_peers())

    def column_peers():
        for dy in range(SIDE):
            for dc in range(2):
                if dy or dc:
                    yield dy * 2 + dc - 1, wrap(here.y + dy), (here.core + dc) % 2

    def plane_peers():
        for dx in range(SIDE):
            for dz in range(SIDE):
                if dx or dz:
                    yield wrap(here.x + dx), wrap(here.z + dz)

    barrier = pltpu.get_barrier_semaphore()
    for seq, _ in peers:
        pl.semaphore_signal(
            barrier, 1, device_id={"seq": seq, "ch": here.y_hi}, device_id_type=MESH
        )
    for y_lo in range(2):
        for core in range(2):
            there = here.at(y=(1 - here.y_hi) * 2 + y_lo, core=core)
            pl.semaphore_signal(barrier, 1, device_id=there, device_id_type=MESH)
    pl.semaphore_wait(barrier, len(peers) + 4)

    def weight_columns(y, core):
        return weight_ref.at[:, pl.ds(pl.multiple_of((y * 2 + core) * columns, columns), columns)]

    def gate_columns(index):
        return gate_ref.at[:, pl.ds(pl.multiple_of(index * columns, columns), columns)]

    own_rows = weights.at[here.y_lo, here.x, here.z, here.core * 2 + here.y_hi]
    for i, y, core in column_peers():
        send(
            weight_columns(y, core), own_rows, spread_s.at[i], spread_r.at[i],
            here.at(y=y, core=core),
        )
    copies = [
        pltpu.make_async_copy(weight_columns(here.y, here.core), own_rows, local.at[0]),
        pltpu.make_async_copy(grad_ref, feats.at[here.y_hi, me], local.at[1]),
        pltpu.make_async_copy(gate_columns(me), gates.at[me], local.at[2]),
    ]
    for copy in copies:
        copy.start()

    def feat(y, core):
        return feats.at[y // 2, (y % 2) * 2 + core]

    def half_tokens(ref, i):
        return ref.at[pl.ds(i * (height // 2), height // 2)]

    near_y = here.y_hi * 2 + 1 - here.y_lo
    far_y = wrap(here.y + 2 * here.y_lo - 1)
    opposite_y = wrap(here.y + 2)

    def feat_send(k, source, target, y):
        send(source, target, feat_s.at[k], feat_r.at[k], here.at(y=y))

    own_feat = feat(here.y, here.core)
    for i in range(2):
        feat_send(i, half_tokens(grad_ref, i), half_tokens(own_feat, i), near_y)
    feat_send(2, grad_ref, own_feat, far_y)

    def feat_relay(i):
        half = half_tokens(feat(near_y, here.core), i)
        await_bytes(half, feat_r.at[i])
        feat_send(3 + i, half, half, far_y)

    def pass_on(k, source, target):
        send(source, target, pass_s.at[k], pass_r.at[k], partner)

    pass_on(0, grad_ref, own_feat)
    share = [(0, 1), (1, 0), (1, 1)]

    def sharer(dy, dc):
        y_lo, core = (here.y_lo + dy) % 2, (here.core + dc) % 2
        return y_lo * 2 + core, here.at(y=here.y_hi * 2 + y_lo, core=core)

    for i, (dy, dc) in enumerate(share):
        index, device = sharer(dy, dc)
        send(gate_columns(index), gates.at[me], gate_s.at[i], gate_r.at[i], device)

    def exchange(batch, piece, arrive):
        for seq, other in peers:
            send(
                piece(seq, other), arrive, batch_s.at[batch], batch_r.at[batch],
                {"seq": seq, "ch": here.y_hi},
            )
        pltpu.make_async_copy(piece(here.seq, block), arrive, batch_r.at[batch]).start()

    span = 8

    def turn(*jobs):
        @pl.loop(0, rows // (2 * span))
        def _(pair):
            for j in range(2):
                b = 2 * pair + j
                part = pl.ds(pl.multiple_of(b * span * width, span * width), span * width)
                for value, put in jobs:
                    lined = dot_t(eye_ref[...], value(part)).astype(BF16)
                    put(pl.ds(b * span, span), lined.reshape(span, width, height))

    def into(out, k):
        def put(at, value):
            out[at, k] = value

        return put

    def into_two(at, value):
        two_out[at] = value

    def plain(ref):
        return lambda part: ref[:, part]

    def product(part):
        return (inner_ref[:, part].astype(F32) * medium_ref[:, part].astype(F32)).astype(BF16)

    def half_block(ref, i):
        return ref.at[pl.ds(i * 2, 2)]

    def block_ring(k, axis, item):
        return Ring(here, axis, item, half_block, ring_s.at[k], ring_r.at[k])

    first = [
        block_ring(0, "x", lambda x: weights.at[0, x, here.z]),
        block_ring(1, "z", lambda z: weights.at[1, here.x, z]),
    ]
    second = []
    for j, d in enumerate(ORDER):
        second.append((
            block_ring(2 + 2 * j, "z", lambda z, d=d: weights.at[0, wrap(here.x + d), z]),
            block_ring(3 + 2 * j, "x", lambda x, d=d: weights.at[1, x, wrap(here.z + d)]),
        ))

    turn((product, into(one_out, 0)), (plain(filter_ref), into(one_out, 1)))
    exchange(0, lambda seq, other: one_out.at[other], one_in.at[here.seq])

    for i, y, core in column_peers():
        source_y = wrap(2 * here.y - y + SIDE)
        await_bytes(
            weights.at[source_y % 2, here.x, here.z, core * 2 + source_y // 2], spread_r.at[i]
        )
    copies[0].wait()
    for ring in first:
        ring.start()
    for ring in second[0]:
        ring.start()
    turn((plain(inner_ref), into_two))
    for ring in first:
        ring.relay()
    for pair in second[1:3]:
        for ring in pair:
            ring.start()
    for ring in second[0]:
        ring.relay()
    for ring in first:
        ring.finish()
    for ring in second[3]:
        ring.start()
    feat_relay(0)
    feat_relay(1)
    pass_on(1, feat(near_y, here.core), feat(near_y, here.core))

    def unpack(source, planes):
        @pl.loop(0, rows // 4)
        def _(b):
            for j in range(4):
                i = 4 * b + j
                at = pl.ds(pl.multiple_of(i * width, width), width)
                for k, plane in planes:
                    lines[plane, at, :] = source[i, k].astype(F32)

    def keep(parts, places):
        for part, place in zip(parts, places):
            high, low = split(part)
            there = pl.ds(pl.multiple_of(place, rows), rows)
            yield there, high, low

    await_bytes(one_in, batch_r.at[0])
    unpack(one_in, ((0, 0), (1, 1)))
    for ring in second[1]:
        ring.relay()

    def spread_pairs(part):
        size = width // 4

        @pl.loop(part * size // 2, (part + 1) * size // 2)
        def _(b):
            for j in range(2):
                c = 2 * b + j
                pick = pl.ds(c, rows, stride=width)
                pair = jnp.concatenate([lines[0, pick, :], lines[1, pick, :]], 1).astype(BF16)
                parts = outer_stage(pair, first_ref[...], twists_ref[...])
                for there, high, low in keep(parts, (c * rows, area + c * rows)):
                    zh[there, :] = high
                    zl[there, :] = low

    spread_pairs(0)
    await_bytes(feat(far_y, here.core), feat_r.at[2])
    pass_on(2, feat(far_y, here.core), feat(far_y, here.core))
    for ring in second[2]:
        ring.relay()
    spread_pairs(1)
    for ring in second[3]:
        ring.relay()
    spread_pairs(2)
    for i in range(2):
        half = half_tokens(feat(opposite_y, here.core), i)
        await_bytes(half, feat_r.at[3 + i])
        pass_on(3 + i, half, half)
    spread_pairs(3)
    step = 512

    def transform_pairs(begin, end):
        @pl.loop(begin, end)
        def _(b):
            at = pl.ds(pl.multiple_of(b * step, step), step)
            spec[at, :] = dot3(zh[at, :], zl[at, :], forward_ref[...])

    halves = area // step

    other_core = 1 - here.core
    copies[1].wait()
    for k, y in ((0, here.y), (1, near_y), (2, far_y)):
        await_bytes(feat(y, other_core), pass_r.at[k])
    for i in range(2):
        await_bytes(half_tokens(feat(opposite_y, other_core), i), pass_r.at[3 + i])
    exchange(1, lambda seq, other: two_out.at[other], two_in.at[here.seq])
    rows_of = weights.shape[3] * weights.shape[4]
    depth = SIDE * rows_of
    for j, d in enumerate(ORDER):
        for ring in second[j]:
            ring.finish()
        x, z = wrap(here.x + d), wrap(here.z + d)
        left = feats[0, :, :, pl.ds(pl.multiple_of(x * depth, depth), depth)]
        term = dot(left.reshape(4 * height, depth), weights[0, x].reshape(depth, columns))
        if j == 0:
            total[...] = term
        else:
            total[...] += term
        left = jnp.concatenate(
            [
                feats[1, :, :, pl.ds(pl.multiple_of(k * depth + z * rows_of, rows_of), rows_of)]
                for k in range(SIDE)
            ],
            2,
        )
        total[...] += dot(
            left.reshape(4 * height, depth), weights[1, :, z].reshape(depth, columns)
        )

    copies[2].wait()
    for i, (dy, dc) in enumerate(share):
        await_bytes(gates.at[sharer(dy, dc)[0]], gate_r.at[i])
    block_size = eye_ref.shape[0]
    cells = block_size // width
    for g in range(4):
        part = total[g * height : (g + 1) * height]
        long_grad = (part * gates[g].astype(F32)).astype(BF16)
        for k in range(columns // block_size):
            lined = dot_t(eye_ref[...], long_grad[:, k * block_size : (k + 1) * block_size])
            turned[k * cells : (k + 1) * cells, g // 2, g % 2] = lined.astype(BF16).reshape(
                cells, width, height
            )
        hidden[g] = part.astype(BF16)
    pltpu.make_async_copy(turned.at[cell], late.at[:, cell], late_sem.at[1]).start()
    for x, z in plane_peers():
        send(
            turned.at[x * SIDE + z], late.at[:, cell], late_sem.at[0], late_sem.at[1],
            here.at(x=x, z=z),
        )
    turn((plain(short_ref), into(three_out, 0)), (plain(conv_ref), into(three_out, 1)))
    exchange(2, lambda seq, other: three_out.at[other], three_in.at[here.seq])
    for i, (dy, dc) in enumerate(share):
        index, device = sharer(dy, dc)
        send(hidden.at[index], arrived.at[me], hidden_s.at[i], hidden_r.at[i], device)
    own = pltpu.make_async_copy(hidden.at[me], arrived.at[me], local.at[1])
    own.start()

    place = pl.multiple_of((me * PLANE + here.x * SIDE) * width, LANES)
    chosen = lax.broadcasted_iota(jnp.int32, (width, LANES), 1)
    chosen = chosen == lax.broadcasted_iota(jnp.int32, (width, LANES), 0) + here.z * width
    chosen = chosen.astype(F32).astype(BF16)
    taps[0] = dot_t(chosen, taps_medium_ref[:, pl.ds(place, LANES)])
    sums[0, : width // 4, :LANES] = jnp.zeros((width // 4, LANES), F32)
    sums[0, :SHORT, :LANES] = taps_short_ref[:, pl.ds(place, LANES)].astype(F32)
    padded = jnp.concatenate(
        [sums[0, : width // 4, :LANES], jnp.zeros((LANES - width // 4, LANES), F32)], 0
    )
    taps[1] = dot_t(chosen, padded.astype(BF16))

    @pl.loop(0, width)
    def _(c):
        wide = pl.ds(pl.multiple_of(c * LANES, LANES), LANES)
        for k in range(2):
            bands[k, wide, :] = toeplitz(taps[k, pl.ds(c, 1), :]).astype(BF16)

    transform_pairs(0, 2 * halves)
    await_bytes(late, late_sem.at[1])
    for y_lo in range(2):
        @pl.loop(0, PLANE // 2)
        def _(b):
            for j in range(2):
                for core in range(2):
                    i = 2 * b + j
                    place = ((y_lo * PLANE + i) * 2 + core) * width
                    at = pl.ds(pl.multiple_of(place, width), width)
                    lines[2, at, :] = late[y_lo, i, core].astype(F32)

    many = 4
    wide_step = many * rows
    row = lax.broadcasted_iota(jnp.int32, (rows, LANES), 0)

    def transform(start):
        @pl.loop(0, chunk // 8)
        def _(b):
            for j in range(4):
                c = 4 * b + j
                pair = jnp.concatenate(
                    [lines[2, pl.ds(start + 2 * c + k, rows, stride=width), :] for k in range(2)], 1
                ).astype(BF16)
                parts = outer_stage(pair, first_ref[...], twists_ref[...])
                for there, high, low in keep(parts, (2 * c * rows, (2 * c + 1) * rows)):
                    gh[there, :] = high
                    gl[there, :] = low

        @pl.loop(0, chunk // many)
        def _(b):
            at = pl.ds(pl.multiple_of(b * wide_step, wide_step), wide_step)
            grad = dot3(gh[at, :], gl[at, :], forward_ref[...])
            grad_real, grad_imag = grad[:, :LANES], grad[:, LANES:]
            cosine = jnp.concatenate([twists_ref[:, :LANES]] * many, 0)
            sine = jnp.concatenate([twists_ref[:, LANES:]] * many, 0)
            reals, imags = [], []
            for k in range(2):
                place = (1 - k) * area + start * rows + b * wide_step
                other = spec[pl.ds(pl.multiple_of(place, wide_step), wide_step), :]
                real, imag = other[:, :LANES], other[:, LANES:]
                term = jnp.concatenate(
                    [real * grad_real + imag * grad_imag, real * grad_imag - imag * grad_real], 1
                )
                back = dot3(*split(term), inverse_ref[...])
                real, imag = back[:, :LANES], back[:, LANES:]
                reals.append(real * cosine - imag * sine)
                imags.append(real * sine + imag * cosine)
            real, imag = jnp.concatenate(reals, 1), jnp.concatenate(imags, 1)
            for k in range(many):
                both = jnp.concatenate(
                    [real[k * rows : (k + 1) * rows], imag[k * rows : (k + 1) * rows]], 0
                )
                high, low = split(both)
                there = pl.ds(pl.multiple_of((b * many + k) * 2 * rows, 2 * rows), 2 * rows)
                zh[there, :] = high
                zl[there, :] = low

        @pl.loop(0, chunk // many)
        def _(b):
            for k in range(many):
                within = b * many + k
                c = start + within
                there = pl.ds(pl.multiple_of(within * 2 * rows, 2 * rows), 2 * rows)
                high, low = zh[there, :], zl[there, :]
                both = (
                    dot(last_ref[:rows], high) + dot(last_ref[:rows], low)
                    + dot(last_ref[rows:], high)
                )
                pick = pl.ds(within, rows, stride=chunk)
                points[pl.ds(pl.multiple_of(c * rows, rows), rows), :] = both[:, :LANES]
                results[0, pick, :] = both[:, :LANES]
                results[1, pick, :] = both[:, LANES:]

    def pack(k, source, to):
        @pl.loop(0, rows // 8)
        def _(group):
            for j in range(8):
                i = 8 * group + j
                at = pl.ds(pl.multiple_of(i * chunk, chunk), chunk)
                for a, b in zip(source, to):
                    parcels[i, k, b] = results[a, at, :].astype(BF16)

    def pair_of(ref, k):
        return ref.at[k, pl.ds(0, 2)]

    for k in range(2):
        transform(k * chunk)
        pack(k, (0, 1), (0, 1))
        exchange(3 + k, lambda seq, other: pair_of(parcels.at[seq], k), pair_of(back_ref.at[block], k))

    await_bytes(two_in, batch_r.at[1])

    @pl.loop(0, rows // 8)
    def _(b):
        for j in range(8):
            i = 8 * b + j
            at = pl.ds(pl.multiple_of(i * width, width), width)
            lines[0, at, :] = two_in[i].astype(F32)

    def with_next(x):
        following = jnp.where(row == rows - 1, 0.0, pltpu.roll(x, rows - 1, 0))
        return jnp.concatenate([x, following], 1).astype(BF16)

    def diagonals(c, k, both):
        value = lines[1 + k, pl.ds(c, rows, stride=width), :].astype(BF16)
        products = dot(dot_t(flip_ref[...], value).astype(BF16), both)
        slid = pltpu.roll(products, 0, 1, stride=1, stride_axis=0)
        sums[k, pl.ds(c, 1), :] = jnp.sum(slid, axis=0, keepdims=True)

    @pl.loop(0, width // many)
    def _(b):
        for k in range(many):
            c = b * many + k
            wide = pl.ds(pl.multiple_of(c * LANES, LANES), LANES)
            there = pl.ds(pl.multiple_of(c * rows, rows), rows)
            gate = lines[0, pl.ds(c, rows, stride=width), :]
            both = with_next((points[there, :] * gate).astype(BF16).astype(F32))
            short_grad = dot_t(both, bands[0, wide, :]).astype(BF16).astype(F32)
            pair = with_next(short_grad)
            boths[there, :] = both
            pairs[there, :] = pair

    await_bytes(three_in, batch_r.at[2])
    unpack(three_in, ((0, 1), (1, 2)))

    @pl.loop(0, width // many)
    def _(b):
        for k in range(many):
            c = b * many + k
            there = pl.ds(pl.multiple_of(c * rows, rows), rows)
            diagonals(c, 0, boths[there, :])
            diagonals(c, 1, pairs[there, :])

    factor = (rows * LANES) ** -0.5
    lags = [pltpu.roll(sums[k], LANES + 1, 1)[:, :LANES] * factor for k in range(2)]
    square = jnp.concatenate([lags[1], jnp.zeros((LANES - width, LANES), F32)], 0)
    mine = lags_ref.at[here.y_lo, here.core]
    lags_ref[here.y_lo, here.core, here.x, here.z, :width] = lags[0].astype(BF16)
    lags_ref[here.y_lo, here.core, here.x, here.z, width:] = square.T[:PAD].astype(BF16)

    def lag_send(i, ref, device):
        send(ref, ref, lag_s.at[i], lag_r.at[i], device)

    own_lags = mine.at[here.x, here.z]
    for dx in range(SIDE):
        for dz in range(SIDE):
            x, z = wrap(here.x + dx), wrap(here.z + dz)
            lag_send(7, own_lags, here.at(y=near_y, x=x, z=z))
            if dx or dz:
                lag_send(dx - 1 if dx else 2 + dz, own_lags, here.at(x=x, z=z))

    def convolve(start):
        @pl.loop(0, chunk // many)
        def _(b):
            for k in range(many):
                within = b * many + k
                c = start + within
                wide = pl.ds(pl.multiple_of(c * LANES, LANES), LANES)
                there = pl.ds(pl.multiple_of(c * rows, rows), rows)
                results[0, pl.ds(within, rows, stride=chunk), :] = dot_t(
                    pairs[there, :], bands[1, wide, :]
                )

    for k in range(2):
        convolve(k * chunk)
        pack(k, (0,), (2,))
        exchange(5 + k, lambda seq, other: parcels.at[seq, k, 2], back_ref.at[block, k, 2])

    own.wait()
    for i, (dy, dc) in enumerate(share):
        await_bytes(arrived.at[sharer(dy, dc)[0]], hidden_r.at[i])
    for d in range(1, SIDE):
        await_bytes(mine.at[wrap(here.x - d)], lag_r.at[d - 1])
        await_bytes(mine.at[here.x, wrap(here.z - d)], lag_r.at[2 + d])
    lag_send(6, mine, partner)
    across = lags_ref.at[1 - here.y_lo, here.core]
    await_bytes(across, lag_r.at[7])
    lag_send(8, across, partner)
    await_bytes(lags_ref.at[here.y_lo, 1 - here.core], lag_r.at[6])
    await_bytes(lags_ref.at[1 - here.y_lo, 1 - here.core], lag_r.at[8])

    for k in range(2):
        await_bytes(back_ref.at[:, k, pl.ds(0, 2)], batch_r.at[3 + k])
        await_bytes(back_ref.at[:, k, 2], batch_r.at[5 + k])
    most = pl.ds(0, rows - 1)
    for k, ref in enumerate((one_out, two_out, three_out)):
        await_bytes(ref.at[most], batch_s.at[k])
    for k in range(2):
        await_bytes(parcels.at[most, k, pl.ds(0, 2)], batch_s.at[3 + k])
        await_bytes(parcels.at[most, k, 2], batch_s.at[5 + k])
    await_bytes(turned.at[pl.ds(0, PLANE - 1)], late_sem.at[0])
    for i in range(7):
        await_bytes(own_rows, spread_s.at[i])
    for i in range(3):
        await_bytes(gates.at[me], gate_s.at[i])
        await_bytes(hidden.at[me], hidden_s.at[i])
        await_bytes(mine.at[here.x], lag_s.at[i])
        await_bytes(own_lags, lag_s.at[3 + i])
        await_bytes(mine, lag_s.at[6 + i])
    for i in range(3):
        await_bytes(own_feat, pass_s.at[i])
    await_bytes(own_feat, feat_s.at[2])
    for i in range(2):
        half = half_tokens(own_feat, i)
        await_bytes(half, pass_s.at[3 + i])
        await_bytes(half, feat_s.at[i])
        await_bytes(half, feat_s.at[3 + i])
    for ring in first:
        ring.drain()
    for pair in second:
        for ring in pair:
            ring.drain()


def block_call(grad, weight, gate, channelwise, constants):
    height, half = grad.shape
    depth, model = weight.shape
    columns = model // 8
    width = columns // PLANE
    rows = half // width
    area = rows * width
    chunk = width // 2
    anywhere = pl.BlockSpec(memory_space=pl.ANY)
    near = pl.BlockSpec(memory_space=pltpu.VMEM)
    dma = pltpu.SemaphoreType.DMA
    vmem = pltpu.VMEM
    return pl.pallas_call(
        block_kernel,
        out_shape=(
            jax.ShapeDtypeStruct((4, height, columns), BF16),
            jax.ShapeDtypeStruct((rows, 2, 3, chunk, height), BF16),
            jax.ShapeDtypeStruct((2, 2, SIDE, SIDE, width + PAD, height), BF16),
        ),
        in_specs=[anywhere] * 3 + [near] * (len(channelwise) + len(constants)),
        out_specs=(anywhere, anywhere, near),
        scratch_shapes=[
            vmem((2, 4, height, half), BF16),
            vmem((2, SIDE, SIDE, 4, depth, columns), BF16),
            vmem((4, height, columns), BF16),
            vmem((4 * height, columns), F32),
            vmem((PLANE, 2, 2, width, height), BF16),
            vmem((4, height, columns), BF16),
            vmem((rows, 2, width, height), BF16),
            vmem((rows, 2, width, height), BF16),
            vmem((rows, width, height), BF16),
            vmem((rows, width, height), BF16),
            vmem((rows, 2, width, height), BF16),
            vmem((rows, 2, width, height), BF16),
            vmem((2, PLANE, 2, width, height), BF16),
            vmem((3, area, height), F32),
            vmem((2 * area, 2 * height), BF16),
            vmem((2 * area, 2 * height), BF16),
            vmem((area // 2, 2 * height), BF16),
            vmem((area // 2, 2 * height), BF16),
            vmem((2 * area, 2 * height), F32),
            vmem((2, width * LANES, 2 * LANES), BF16),
            vmem((2, width, LANES), F32),
            vmem((area, height), F32),
            vmem((area, 2 * height), BF16),
            vmem((area, 2 * height), BF16),
            vmem((2, area // 2, height), F32),
            vmem((2, width, 2 * LANES), F32),
            vmem((rows, 2, 3, chunk, height), BF16),
            dma((3,)), dma((7,)), dma((7,)), dma((3,)), dma((3,)), dma((5,)), dma((5,)),
            dma((5,)), dma((5,)), dma((10, 4)), dma((10, 4)), dma((2,)), dma((3,)), dma((3,)),
            dma((7,)), dma((7,)), dma((9,)), dma((9,)),
        ],
        compiler_params=pltpu.CompilerParams(
            collective_id=0, has_side_effects=True, vmem_limit_bytes=VMEM_LIMIT
        ),
        cost_estimate=pl.CostEstimate(
            flops=16 * 10**9, bytes_accessed=32 * 2**20, transcendentals=0
        ),
        name="block",
    )(grad, weight, gate, *channelwise, *constants)


def unturn_kernel(
    in_ref, lags_ref, medium_ref, hidden_ref, long_ref, eye_ref,
    outer_out, inner_out, input_out, filter_out, lags_out, short_out,
):
    size, height = inner_out.shape[1], in_ref.shape[4]
    blocks = in_ref.shape[0]
    width = size // blocks

    def lined(value):
        return dot_t(eye_ref[...], value.reshape(size, height))

    outer_out[...] = (hidden_ref[0].astype(F32) * long_ref[...].astype(F32)).astype(BF16)
    inner_out[...] = (lined(in_ref[:, :, 0]) * medium_ref[...].astype(F32)).astype(BF16)
    filter_out[...] = lined(in_ref[:, :, 1])
    input_out[...] = lined(in_ref[:, :, 2]).astype(BF16)
    lags_out[...] = lined(lags_ref[:, :width])
    lane = lax.broadcasted_iota(jnp.int32, (height, size), 0)
    column = lax.broadcasted_iota(jnp.int32, (height, size), 1)
    short = jnp.zeros((PAD, size), F32)
    for b in range(blocks):
        place = (column == lane + b * width) & (lane < width)
        short += dot(lags_ref[b, width:], place.astype(F32).astype(BF16))
    short_out[...] = short[:SHORT]


def from_blocks(block, lags, medium_out, hidden, long_out):
    devices, parts, items, chunk, height = block.shape
    span = devices // 4
    size = span * parts * chunk
    channels = devices * parts * chunk
    rows = pl.BlockSpec((height, size), lambda i: (0, i))
    eye = np.eye(height).astype(jnp.bfloat16)
    return pl.pallas_call(
        unturn_kernel,
        grid=(devices // span,),
        out_shape=[
            jax.ShapeDtypeStruct((height, channels), t) for t in (BF16, BF16, BF16, F32, F32)
        ] + [jax.ShapeDtypeStruct((SHORT, channels), F32)],
        in_specs=[
            pl.BlockSpec((span, parts, items, chunk, height), lambda i: (i, 0, 0, 0, 0)),
            pl.BlockSpec((span, lags.shape[1], height), lambda i: (i, 0, 0)),
            rows,
            pl.BlockSpec((1, height, size), lambda i: (i, 0, 0)),
            rows,
            pl.BlockSpec((height, height), lambda i: (0, 0)),
        ],
        out_specs=[rows] * 5 + [pl.BlockSpec((SHORT, size), lambda i: (0, i))],
        cost_estimate=pl.CostEstimate(
            flops=0, bytes_accessed=24 * height * channels, transcendentals=0
        ),
        name="from_blocks",
    )(block, lags, medium_out, hidden, long_out, eye)


def per_device(
    out_grad, out_weight, outer_gate, long_out, inner_gate, conv_input,
    short_out, medium_out, long_filter, taps_short, taps_medium,
):
    channels = outer_gate.shape[1]
    devices = lax.axis_size("seq")
    width = channels // devices
    hidden, results, lags = block_call(
        out_grad, out_weight, outer_gate,
        (inner_gate, medium_out, short_out, conv_input, long_filter, taps_short, taps_medium),
        tables(devices),
    )
    lags = lags.reshape(devices, width + PAD, LANES)
    outer, inner, short, filt, medium_taps, short_taps = from_blocks(
        results, lags, medium_out, hidden, long_out
    )
    return outer, inner, short, filt, short_taps, medium_taps


def solution(mesh):
    rows = P("seq", "ch")
    return jax.shard_map(
        per_device,
        mesh=mesh,
        in_specs=(rows, P(("seq", "ch"), None)) + (rows,) * 7 + (P(None, "ch"),) * 2,
        out_specs=(rows,) * 4 + (P(None, "ch"),) * 2,
        check_vma=False,
    )
```

```python
import math

import jax
import jax.numpy as jnp
import numpy as np
from jax import lax
from jax.experimental import pallas as pl
from jax.experimental.pallas import tpu as pltpu
from jax.sharding import PartitionSpec as P

SHORT = 7
MEDIUM = 128
LANES = 128
F32 = jnp.float32
BF16 = jnp.bfloat16
VMEM_LIMIT = 60 * 1024 * 1024
PAD = 16
SIDE = 4
PLANE = SIDE * SIDE
ORDER = (0, 3, 1, 2)
MESH = pl.DeviceIdType.MESH


def split_np(table):
    high = table.astype(np.float32).astype(jnp.bfloat16)
    low = (table - high.astype(np.float64)).astype(np.float32).astype(jnp.bfloat16)
    return high, low


def tables(rows):
    total = 2 * rows * LANES
    freq = np.arange(rows)[:, None] + 0.5
    place = np.arange(rows)[None, :]
    angle = 2.0 * np.pi * freq * place / (2 * rows)
    first = np.concatenate([np.cos(angle), -np.sin(angle)], 0)
    first = np.concatenate(split_np(first), 1)
    twist = 2.0 * np.pi * freq * np.arange(LANES)[None, :] / total
    inner = 2.0 * np.pi * np.outer(np.arange(LANES), np.arange(LANES)) / LANES
    cosine, sine = np.cos(inner), np.sin(inner)
    forward = np.block([[cosine, -sine], [sine, cosine]])
    inverse = np.block([[cosine, sine], [-sine, cosine]])
    scale = (rows * LANES) ** -0.5 * 2.0 / total
    last = np.concatenate([np.cos(angle.T), -np.sin(angle.T)], 1) * scale
    twists = np.concatenate([np.cos(twist), np.sin(twist)], 1).astype(np.float32)
    flip = np.eye(LANES)[::-1].astype(jnp.bfloat16)
    return (
        first,
        twists,
        np.concatenate(split_np(forward), 0),
        np.concatenate(split_np(inverse), 0),
        np.concatenate(split_np(last), 0),
        flip,
        np.eye(2 * LANES).astype(jnp.bfloat16),
    )


def dot(a, b):
    return jnp.dot(a, b, preferred_element_type=F32)


def dot_t(a, b):
    return lax.dot_general(a, b, (((1,), (1,)), ((), ())), preferred_element_type=F32)


def split(x):
    high = x.astype(BF16)
    return high, (x - high.astype(F32)).astype(BF16)


def dot3(high, low, table):
    size = table.shape[0] // 2
    return dot(high, table[:size]) + dot(high, table[size:]) + dot(low, table[:size])


def outer_stage(pair, first, twists):
    rows = pair.shape[0]
    spread = dot(first, jnp.concatenate([pair, pair], 0))
    cosine = jnp.concatenate([twists[:, :LANES]] * 2, 1)
    sine = jnp.concatenate([twists[:, LANES:]] * 2, 1)
    real, imag = spread[:rows], spread[rows:]
    new_real = real * cosine + imag * sine
    new_imag = imag * cosine - real * sine
    return (
        jnp.concatenate([new_real[:, :LANES], new_imag[:, :LANES]], 1),
        jnp.concatenate([new_real[:, LANES:], new_imag[:, LANES:]], 1),
    )


def toeplitz(line):
    row = jnp.concatenate([line, jnp.zeros_like(line)], 1)
    block = jnp.broadcast_to(row, (LANES, 2 * LANES))
    return pltpu.roll(block, 0, 1, stride=1, stride_axis=0)


def wrap(i):
    return lax.rem(i + SIDE, SIDE)


class Here:
    def __init__(self):
        seq = lax.axis_index("seq")
        self.seq = seq
        self.y_hi = lax.axis_index("ch")
        self.core = seq % 2
        self.z = (seq // 2) % SIDE
        self.x = (seq // (2 * SIDE)) % SIDE
        self.y_lo = seq // (2 * PLANE)
        self.y = self.y_hi * 2 + self.y_lo

    def token_peers(self):
        xs = [wrap(self.x + d) for d in range(SIDE)]
        zs = [wrap(self.z + d) for d in range(SIDE)]
        cores, ys = [self.core, 1 - self.core], [self.y_lo, 1 - self.y_lo]
        for dx in range(SIDE):
            for dz in range(SIDE):
                for dy in range(2):
                    for dc in range(2):
                        if dx or dz or dy or dc:
                            cell = xs[dx] * SIDE + zs[dz]
                            yield (
                                (ys[dy] * PLANE + cell) * 2 + cores[dc],
                                (ys[dy] * 2 + cores[dc]) * PLANE + cell,
                            )

    def at(self, x=None, y=None, z=None, core=None):
        x = self.x if x is None else x
        y = self.y if y is None else y
        z = self.z if z is None else z
        core = self.core if core is None else core
        seq = (((y % 2) * SIDE + x) * SIDE + z) * 2 + core
        return {"seq": seq, "ch": y // 2}


def send(source, target, sends, recvs, device):
    copy = pltpu.make_async_remote_copy(
        src_ref=source,
        dst_ref=target,
        send_sem=sends,
        recv_sem=recvs,
        device_id=device,
        device_id_type=MESH,
    )
    copy.start()


def await_bytes(ref, sem):
    pltpu.make_async_copy(ref, ref, sem).wait()


class Ring:
    def __init__(self, here, axis, item, half, sends, recvs, source=None):
        self.at = lambda p: here.at(**{axis: p})
        self.place = getattr(here, axis)
        self.item, self.half = item, half
        self.sends, self.recvs = sends, recvs
        self.source = item(self.place) if source is None else source

    def step(self, i, source, target, to):
        send(source, target, self.sends.at[i], self.recvs.at[i], self.at(wrap(self.place + to)))

    def start(self):
        self.step(0, self.source, self.item(self.place), 1)
        self.step(1, self.source, self.item(self.place), -1)

    def relay(self):
        for i, to in ((0, 1), (1, -1)):
            other = wrap(self.place - to)
            await_bytes(self.item(other), self.recvs.at[i])
            half = self.half(self.item(other), i)
            self.step(2 + i, half, half, to)

    def finish(self):
        opposite = self.item(wrap(self.place + 2))
        for i in range(2):
            await_bytes(self.half(opposite, i), self.recvs.at[2 + i])

    def drain(self):
        opposite = self.item(wrap(self.place + 2))
        for i in range(2):
            await_bytes(self.item(self.place), self.sends.at[i])
            await_bytes(self.half(opposite, i), self.sends.at[2 + i])


def block_kernel(
    grad_ref, weight_ref, gate_ref,
    inner_ref, medium_ref, short_ref, conv_ref, filter_ref, taps_short_ref, taps_medium_ref,
    first_ref, twists_ref, forward_ref, inverse_ref, last_ref, flip_ref, eye_ref,
    arrived, back_ref, lags_ref,
    feats, weights, gates, total, turned, hidden,
    one_out, one_in, two_out, two_in, three_out, three_in, late,
    lines, zh, zl, gh, gl, spec, bands, taps, points, boths, pairs, results, sums, parcels,
    local, spread_s, spread_r, gate_s, gate_r, feat_s, feat_r, pass_s, pass_r,
    ring_s, ring_r, late_sem, hidden_s, hidden_r, batch_s, batch_r, lag_s, lag_r,
):
    here = Here()
    me = here.y_lo * 2 + here.core
    cell = here.x * SIDE + here.z
    block = me * PLANE + cell
    columns = gates.shape[2]
    height = grad_ref.shape[0]
    rows, width = one_in.shape[0], one_in.shape[2]
    area = rows * width
    chunk = width // 2
    partner = here.at(core=1 - here.core)
    peers = list(here.token_peers())

    def column_peers():
        for dy in range(SIDE):
            for dc in range(2):
                if dy or dc:
                    yield dy * 2 + dc - 1, wrap(here.y + dy), (here.core + dc) % 2

    def plane_peers():
        for dx in range(SIDE):
            for dz in range(SIDE):
                if dx or dz:
                    yield wrap(here.x + dx), wrap(here.z + dz)

    barrier = pltpu.get_barrier_semaphore()
    for seq, _ in peers:
        pl.semaphore_signal(
            barrier, 1, device_id={"seq": seq, "ch": here.y_hi}, device_id_type=MESH
        )
    for y_lo in range(2):
        for core in range(2):
            there = here.at(y=(1 - here.y_hi) * 2 + y_lo, core=core)
            pl.semaphore_signal(barrier, 1, device_id=there, device_id_type=MESH)
    pl.semaphore_wait(barrier, len(peers) + 4)

    def weight_columns(y, core):
        return weight_ref.at[:, pl.ds(pl.multiple_of((y * 2 + core) * columns, columns), columns)]

    def gate_columns(index):
        return gate_ref.at[:, pl.ds(pl.multiple_of(index * columns, columns), columns)]

    own_rows = weights.at[here.y_lo, here.x, here.z, here.core * 2 + here.y_hi]
    for i, y, core in column_peers():
        send(
            weight_columns(y, core), own_rows, spread_s.at[i], spread_r.at[i],
            here.at(y=y, core=core),
        )
    copies = [
        pltpu.make_async_copy(weight_columns(here.y, here.core), own_rows, local.at[0]),
        pltpu.make_async_copy(grad_ref, feats.at[here.y_hi, me], local.at[1]),
        pltpu.make_async_copy(gate_columns(me), gates.at[me], local.at[2]),
    ]
    for copy in copies:
        copy.start()

    def feat(y, core):
        return feats.at[y // 2, (y % 2) * 2 + core]

    def half_tokens(ref, i):
        return ref.at[pl.ds(i * (height // 2), height // 2)]

    near_y = here.y_hi * 2 + 1 - here.y_lo
    far_y = wrap(here.y + 2 * here.y_lo - 1)
    opposite_y = wrap(here.y + 2)

    def feat_send(k, source, target, y):
        send(source, target, feat_s.at[k], feat_r.at[k], here.at(y=y))

    own_feat = feat(here.y, here.core)
    for i in range(2):
        feat_send(i, half_tokens(grad_ref, i), half_tokens(own_feat, i), near_y)
    feat_send(2, grad_ref, own_feat, far_y)

    def feat_relay(i):
        half = half_tokens(feat(near_y, here.core), i)
        await_bytes(half, feat_r.at[i])
        feat_send(3 + i, half, half, far_y)

    def pass_on(k, source, target):
        send(source, target, pass_s.at[k], pass_r.at[k], partner)

    pass_on(0, grad_ref, own_feat)
    share = [(0, 1), (1, 0), (1, 1)]

    def sharer(dy, dc):
        y_lo, core = (here.y_lo + dy) % 2, (here.core + dc) % 2
        return y_lo * 2 + core, here.at(y=here.y_hi * 2 + y_lo, core=core)

    for i, (dy, dc) in enumerate(share):
        index, device = sharer(dy, dc)
        send(gate_columns(index), gates.at[me], gate_s.at[i], gate_r.at[i], device)

    def exchange(batch, piece, arrive):
        for seq, other in peers:
            send(
                piece(seq, other), arrive, batch_s.at[batch], batch_r.at[batch],
                {"seq": seq, "ch": here.y_hi},
            )
        pltpu.make_async_copy(piece(here.seq, block), arrive, batch_r.at[batch]).start()

    span = 8

    def turn(*jobs):
        @pl.loop(0, rows // (2 * span))
        def _(pair):
            for j in range(2):
                b = 2 * pair + j
                part = pl.ds(pl.multiple_of(b * span * width, span * width), span * width)
                for value, put in jobs:
                    lined = dot_t(eye_ref[...], value(part)).astype(BF16)
                    put(pl.ds(b * span, span), lined.reshape(span, width, height))

    def into(out, k):
        def put(at, value):
            out[at, k] = value

        return put

    def into_two(at, value):
        two_out[at] = value

    def plain(ref):
        return lambda part: ref[:, part]

    def product(part):
        return (inner_ref[:, part].astype(F32) * medium_ref[:, part].astype(F32)).astype(BF16)

    def half_block(ref, i):
        return ref.at[pl.ds(i * 2, 2)]

    def block_ring(k, axis, item):
        return Ring(here, axis, item, half_block, ring_s.at[k], ring_r.at[k])

    first = [
        block_ring(0, "x", lambda x: weights.at[0, x, here.z]),
        block_ring(1, "z", lambda z: weights.at[1, here.x, z]),
    ]
    second = []
    for j, d in enumerate(ORDER):
        second.append((
            block_ring(2 + 2 * j, "z", lambda z, d=d: weights.at[0, wrap(here.x + d), z]),
            block_ring(3 + 2 * j, "x", lambda x, d=d: weights.at[1, x, wrap(here.z + d)]),
        ))

    turn((product, into(one_out, 0)), (plain(filter_ref), into(one_out, 1)))
    exchange(0, lambda seq, other: one_out.at[other], one_in.at[here.seq])

    for i, y, core in column_peers():
        source_y = wrap(2 * here.y - y + SIDE)
        await_bytes(
            weights.at[source_y % 2, here.x, here.z, core * 2 + source_y // 2], spread_r.at[i]
        )
    copies[0].wait()
    for ring in first:
        ring.start()
    for ring in second[0]:
        ring.start()
    turn((plain(inner_ref), into_two))
    for ring in first:
        ring.relay()
    for pair in second[1:3]:
        for ring in pair:
            ring.start()
    turn((plain(short_ref), into(three_out, 0)))
    for ring in second[0]:
        ring.relay()
    for ring in first:
        ring.finish()
    for ring in second[3]:
        ring.start()
    feat_relay(0)
    turn((plain(conv_ref), into(three_out, 1)))
    feat_relay(1)
    pass_on(1, feat(near_y, here.core), feat(near_y, here.core))

    def unpack(source, planes):
        @pl.loop(0, rows // 4)
        def _(b):
            for j in range(4):
                i = 4 * b + j
                at = pl.ds(pl.multiple_of(i * width, width), width)
                for k, plane in planes:
                    lines[plane, at, :] = source[i, k].astype(F32)

    def keep(parts, places):
        for part, place in zip(parts, places):
            high, low = split(part)
            there = pl.ds(pl.multiple_of(place, rows), rows)
            yield there, high, low

    await_bytes(one_in, batch_r.at[0])
    unpack(one_in, ((0, 0), (1, 1)))
    for ring in second[1]:
        ring.relay()

    def spread_pairs(part):
        size = width // 4

        @pl.loop(part * size // 2, (part + 1) * size // 2)
        def _(b):
            for j in range(2):
                c = 2 * b + j
                pick = pl.ds(c, rows, stride=width)
                pair = jnp.concatenate([lines[0, pick, :], lines[1, pick, :]], 1).astype(BF16)
                parts = outer_stage(pair, first_ref[...], twists_ref[...])
                for there, high, low in keep(parts, (c * rows, area + c * rows)):
                    zh[there, :] = high
                    zl[there, :] = low

    spread_pairs(0)
    await_bytes(feat(far_y, here.core), feat_r.at[2])
    pass_on(2, feat(far_y, here.core), feat(far_y, here.core))
    for ring in second[2]:
        ring.relay()
    spread_pairs(1)
    for ring in second[3]:
        ring.relay()
    spread_pairs(2)
    for i in range(2):
        half = half_tokens(feat(opposite_y, here.core), i)
        await_bytes(half, feat_r.at[3 + i])
        pass_on(3 + i, half, half)
    spread_pairs(3)
    step = 512

    def transform_pairs(begin, end):
        @pl.loop(begin, end)
        def _(b):
            at = pl.ds(pl.multiple_of(b * step, step), step)
            spec[at, :] = dot3(zh[at, :], zl[at, :], forward_ref[...])

    halves = area // step

    other_core = 1 - here.core
    copies[1].wait()
    for k, y in ((0, here.y), (1, near_y), (2, far_y)):
        await_bytes(feat(y, other_core), pass_r.at[k])
    for i in range(2):
        await_bytes(half_tokens(feat(opposite_y, other_core), i), pass_r.at[3 + i])
    exchange(1, lambda seq, other: two_out.at[other], two_in.at[here.seq])
    rows_of = weights.shape[3] * weights.shape[4]
    depth = SIDE * rows_of
    for j, d in enumerate(ORDER):
        for ring in second[j]:
            ring.finish()
        x, z = wrap(here.x + d), wrap(here.z + d)
        left = feats[0, :, :, pl.ds(pl.multiple_of(x * depth, depth), depth)]
        term = dot(left.reshape(4 * height, depth), weights[0, x].reshape(depth, columns))
        if j == 0:
            total[...] = term
        else:
            total[...] += term
        left = jnp.concatenate(
            [
                feats[1, :, :, pl.ds(pl.multiple_of(k * depth + z * rows_of, rows_of), rows_of)]
                for k in range(SIDE)
            ],
            2,
        )
        total[...] += dot(
            left.reshape(4 * height, depth), weights[1, :, z].reshape(depth, columns)
        )

    copies[2].wait()
    for i, (dy, dc) in enumerate(share):
        await_bytes(gates.at[sharer(dy, dc)[0]], gate_r.at[i])
    block_size = eye_ref.shape[0]
    cells = block_size // width
    for g in range(4):
        part = total[g * height : (g + 1) * height]
        long_grad = (part * gates[g].astype(F32)).astype(BF16)
        for k in range(columns // block_size):
            lined = dot_t(eye_ref[...], long_grad[:, k * block_size : (k + 1) * block_size])
            turned[k * cells : (k + 1) * cells, g // 2, g % 2] = lined.astype(BF16).reshape(
                cells, width, height
            )
        hidden[g] = part.astype(BF16)
    pltpu.make_async_copy(turned.at[cell], late.at[:, cell], late_sem.at[1]).start()
    for x, z in plane_peers():
        send(
            turned.at[x * SIDE + z], late.at[:, cell], late_sem.at[0], late_sem.at[1],
            here.at(x=x, z=z),
        )
    exchange(2, lambda seq, other: three_out.at[other], three_in.at[here.seq])
    for i, (dy, dc) in enumerate(share):
        index, device = sharer(dy, dc)
        send(hidden.at[index], arrived.at[me], hidden_s.at[i], hidden_r.at[i], device)
    own = pltpu.make_async_copy(hidden.at[me], arrived.at[me], local.at[1])
    own.start()

    place = pl.multiple_of((me * PLANE + here.x * SIDE) * width, LANES)
    chosen = lax.broadcasted_iota(jnp.int32, (width, LANES), 1)
    chosen = chosen == lax.broadcasted_iota(jnp.int32, (width, LANES), 0) + here.z * width
    chosen = chosen.astype(F32).astype(BF16)
    taps[0] = dot_t(chosen, taps_medium_ref[:, pl.ds(place, LANES)])
    sums[0, : width // 4, :LANES] = jnp.zeros((width // 4, LANES), F32)
    sums[0, :SHORT, :LANES] = taps_short_ref[:, pl.ds(place, LANES)].astype(F32)
    padded = jnp.concatenate(
        [sums[0, : width // 4, :LANES], jnp.zeros((LANES - width // 4, LANES), F32)], 0
    )
    taps[1] = dot_t(chosen, padded.astype(BF16))

    @pl.loop(0, width)
    def _(c):
        wide = pl.ds(pl.multiple_of(c * LANES, LANES), LANES)
        for k in range(2):
            bands[k, wide, :] = toeplitz(taps[k, pl.ds(c, 1), :]).astype(BF16)

    transform_pairs(0, 2 * halves)
    await_bytes(late, late_sem.at[1])
    for y_lo in range(2):
        @pl.loop(0, PLANE // 2)
        def _(b):
            for j in range(2):
                for core in range(2):
                    i = 2 * b + j
                    place = ((y_lo * PLANE + i) * 2 + core) * width
                    at = pl.ds(pl.multiple_of(place, width), width)
                    lines[2, at, :] = late[y_lo, i, core].astype(F32)

    many = 4
    wide_step = many * rows
    row = lax.broadcasted_iota(jnp.int32, (rows, LANES), 0)

    def transform(start):
        @pl.loop(0, chunk // 8)
        def _(b):
            for j in range(4):
                c = 4 * b + j
                pair = jnp.concatenate(
                    [lines[2, pl.ds(start + 2 * c + k, rows, stride=width), :] for k in range(2)], 1
                ).astype(BF16)
                parts = outer_stage(pair, first_ref[...], twists_ref[...])
                for there, high, low in keep(parts, (2 * c * rows, (2 * c + 1) * rows)):
                    gh[there, :] = high
                    gl[there, :] = low

        @pl.loop(0, chunk // many)
        def _(b):
            at = pl.ds(pl.multiple_of(b * wide_step, wide_step), wide_step)
            grad = dot3(gh[at, :], gl[at, :], forward_ref[...])
            grad_real, grad_imag = grad[:, :LANES], grad[:, LANES:]
            cosine = jnp.concatenate([twists_ref[:, :LANES]] * many, 0)
            sine = jnp.concatenate([twists_ref[:, LANES:]] * many, 0)
            reals, imags = [], []
            for k in range(2):
                place = (1 - k) * area + start * rows + b * wide_step
                other = spec[pl.ds(pl.multiple_of(place, wide_step), wide_step), :]
                real, imag = other[:, :LANES], other[:, LANES:]
                term = jnp.concatenate(
                    [real * grad_real + imag * grad_imag, real * grad_imag - imag * grad_real], 1
                )
                back = dot3(*split(term), inverse_ref[...])
                real, imag = back[:, :LANES], back[:, LANES:]
                reals.append(real * cosine - imag * sine)
                imags.append(real * sine + imag * cosine)
            real, imag = jnp.concatenate(reals, 1), jnp.concatenate(imags, 1)
            for k in range(many):
                both = jnp.concatenate(
                    [real[k * rows : (k + 1) * rows], imag[k * rows : (k + 1) * rows]], 0
                )
                high, low = split(both)
                there = pl.ds(pl.multiple_of((b * many + k) * 2 * rows, 2 * rows), 2 * rows)
                zh[there, :] = high
                zl[there, :] = low

        @pl.loop(0, chunk // many)
        def _(b):
            for k in range(many):
                within = b * many + k
                c = start + within
                there = pl.ds(pl.multiple_of(within * 2 * rows, 2 * rows), 2 * rows)
                high, low = zh[there, :], zl[there, :]
                both = (
                    dot(last_ref[:rows], high) + dot(last_ref[:rows], low)
                    + dot(last_ref[rows:], high)
                )
                pick = pl.ds(within, rows, stride=chunk)
                points[pl.ds(pl.multiple_of(c * rows, rows), rows), :] = both[:, :LANES]
                results[0, pick, :] = both[:, :LANES]
                results[1, pick, :] = both[:, LANES:]

    def pack(k, source, to):
        @pl.loop(0, rows // 8)
        def _(group):
            for j in range(8):
                i = 8 * group + j
                at = pl.ds(pl.multiple_of(i * chunk, chunk), chunk)
                for a, b in zip(source, to):
                    parcels[i, k, b] = results[a, at, :].astype(BF16)

    def pair_of(ref, k):
        return ref.at[k, pl.ds(0, 2)]

    for k in range(2):
        transform(k * chunk)
        pack(k, (0, 1), (0, 1))
        exchange(3 + k, lambda seq, other: pair_of(parcels.at[seq], k), pair_of(back_ref.at[block], k))

    await_bytes(two_in, batch_r.at[1])

    @pl.loop(0, rows // 8)
    def _(b):
        for j in range(8):
            i = 8 * b + j
            at = pl.ds(pl.multiple_of(i * width, width), width)
            lines[0, at, :] = two_in[i].astype(F32)

    def with_next(x):
        following = jnp.where(row == rows - 1, 0.0, pltpu.roll(x, rows - 1, 0))
        return jnp.concatenate([x, following], 1).astype(BF16)

    def diagonals(c, k, both):
        value = lines[1 + k, pl.ds(c, rows, stride=width), :].astype(BF16)
        products = dot(dot_t(flip_ref[...], value).astype(BF16), both)
        slid = pltpu.roll(products, 0, 1, stride=1, stride_axis=0)
        sums[k, pl.ds(c, 1), :] = jnp.sum(slid, axis=0, keepdims=True)

    @pl.loop(0, width // many)
    def _(b):
        for k in range(many):
            c = b * many + k
            wide = pl.ds(pl.multiple_of(c * LANES, LANES), LANES)
            there = pl.ds(pl.multiple_of(c * rows, rows), rows)
            gate = lines[0, pl.ds(c, rows, stride=width), :]
            both = with_next((points[there, :] * gate).astype(BF16).astype(F32))
            short_grad = dot_t(both, bands[0, wide, :]).astype(BF16).astype(F32)
            pair = with_next(short_grad)
            boths[there, :] = both
            pairs[there, :] = pair

    await_bytes(three_in, batch_r.at[2])
    unpack(three_in, ((0, 1), (1, 2)))

    @pl.loop(0, width // many)
    def _(b):
        for k in range(many):
            c = b * many + k
            there = pl.ds(pl.multiple_of(c * rows, rows), rows)
            diagonals(c, 0, boths[there, :])
            diagonals(c, 1, pairs[there, :])

    factor = (rows * LANES) ** -0.5
    lags = [pltpu.roll(sums[k], LANES + 1, 1)[:, :LANES] * factor for k in range(2)]
    square = jnp.concatenate([lags[1], jnp.zeros((LANES - width, LANES), F32)], 0)
    mine = lags_ref.at[here.y_lo, here.core]
    lags_ref[here.y_lo, here.core, here.x, here.z, :width] = lags[0].astype(BF16)
    lags_ref[here.y_lo, here.core, here.x, here.z, width:] = square.T[:PAD].astype(BF16)

    def lag_send(i, ref, device):
        send(ref, ref, lag_s.at[i], lag_r.at[i], device)

    own_lags = mine.at[here.x, here.z]
    for dx in range(SIDE):
        for dz in range(SIDE):
            x, z = wrap(here.x + dx), wrap(here.z + dz)
            lag_send(7, own_lags, here.at(y=near_y, x=x, z=z))
            if dx or dz:
                lag_send(dx - 1 if dx else 2 + dz, own_lags, here.at(x=x, z=z))

    def convolve(start):
        @pl.loop(0, chunk // many)
        def _(b):
            for k in range(many):
                within = b * many + k
                c = start + within
                wide = pl.ds(pl.multiple_of(c * LANES, LANES), LANES)
                there = pl.ds(pl.multiple_of(c * rows, rows), rows)
                results[0, pl.ds(within, rows, stride=chunk), :] = dot_t(
                    pairs[there, :], bands[1, wide, :]
                )

    for k in range(2):
        convolve(k * chunk)
        pack(k, (0,), (2,))
        exchange(5 + k, lambda seq, other: parcels.at[seq, k, 2], back_ref.at[block, k, 2])

    own.wait()
    for i, (dy, dc) in enumerate(share):
        await_bytes(arrived.at[sharer(dy, dc)[0]], hidden_r.at[i])
    for d in range(1, SIDE):
        await_bytes(mine.at[wrap(here.x - d)], lag_r.at[d - 1])
        await_bytes(mine.at[here.x, wrap(here.z - d)], lag_r.at[2 + d])
    lag_send(6, mine, partner)
    across = lags_ref.at[1 - here.y_lo, here.core]
    await_bytes(across, lag_r.at[7])
    lag_send(8, across, partner)
    await_bytes(lags_ref.at[here.y_lo, 1 - here.core], lag_r.at[6])
    await_bytes(lags_ref.at[1 - here.y_lo, 1 - here.core], lag_r.at[8])

    for k in range(2):
        await_bytes(back_ref.at[:, k, pl.ds(0, 2)], batch_r.at[3 + k])
        await_bytes(back_ref.at[:, k, 2], batch_r.at[5 + k])
    most = pl.ds(0, rows - 1)
    for k, ref in enumerate((one_out, two_out, three_out)):
        await_bytes(ref.at[most], batch_s.at[k])
    for k in range(2):
        await_bytes(parcels.at[most, k, pl.ds(0, 2)], batch_s.at[3 + k])
        await_bytes(parcels.at[most, k, 2], batch_s.at[5 + k])
    await_bytes(turned.at[pl.ds(0, PLANE - 1)], late_sem.at[0])
    for i in range(7):
        await_bytes(own_rows, spread_s.at[i])
    for i in range(3):
        await_bytes(gates.at[me], gate_s.at[i])
        await_bytes(hidden.at[me], hidden_s.at[i])
        await_bytes(mine.at[here.x], lag_s.at[i])
        await_bytes(own_lags, lag_s.at[3 + i])
        await_bytes(mine, lag_s.at[6 + i])
    for i in range(3):
        await_bytes(own_feat, pass_s.at[i])
    await_bytes(own_feat, feat_s.at[2])
    for i in range(2):
        half = half_tokens(own_feat, i)
        await_bytes(half, pass_s.at[3 + i])
        await_bytes(half, feat_s.at[i])
        await_bytes(half, feat_s.at[3 + i])
    for ring in first:
        ring.drain()
    for pair in second:
        for ring in pair:
            ring.drain()


def block_call(grad, weight, gate, channelwise, constants):
    height, half = grad.shape
    depth, model = weight.shape
    columns = model // 8
    width = columns // PLANE
    rows = half // width
    area = rows * width
    chunk = width // 2
    anywhere = pl.BlockSpec(memory_space=pl.ANY)
    near = pl.BlockSpec(memory_space=pltpu.VMEM)
    dma = pltpu.SemaphoreType.DMA
    vmem = pltpu.VMEM
    return pl.pallas_call(
        block_kernel,
        out_shape=(
            jax.ShapeDtypeStruct((4, height, columns), BF16),
            jax.ShapeDtypeStruct((rows, 2, 3, chunk, height), BF16),
            jax.ShapeDtypeStruct((2, 2, SIDE, SIDE, width + PAD, height), BF16),
        ),
        in_specs=[anywhere] * 3 + [near] * (len(channelwise) + len(constants)),
        out_specs=(anywhere, anywhere, near),
        scratch_shapes=[
            vmem((2, 4, height, half), BF16),
            vmem((2, SIDE, SIDE, 4, depth, columns), BF16),
            vmem((4, height, columns), BF16),
            vmem((4 * height, columns), F32),
            vmem((PLANE, 2, 2, width, height), BF16),
            vmem((4, height, columns), BF16),
            vmem((rows, 2, width, height), BF16),
            vmem((rows, 2, width, height), BF16),
            vmem((rows, width, height), BF16),
            vmem((rows, width, height), BF16),
            vmem((rows, 2, width, height), BF16),
            vmem((rows, 2, width, height), BF16),
            vmem((2, PLANE, 2, width, height), BF16),
            vmem((3, area, height), F32),
            vmem((2 * area, 2 * height), BF16),
            vmem((2 * area, 2 * height), BF16),
            vmem((area // 2, 2 * height), BF16),
            vmem((area // 2, 2 * height), BF16),
            vmem((2 * area, 2 * height), F32),
            vmem((2, width * LANES, 2 * LANES), BF16),
            vmem((2, width, LANES), F32),
            vmem((area, height), F32),
            vmem((area, 2 * height), BF16),
            vmem((area, 2 * height), BF16),
            vmem((2, area // 2, height), F32),
            vmem((2, width, 2 * LANES), F32),
            vmem((rows, 2, 3, chunk, height), BF16),
            dma((3,)), dma((7,)), dma((7,)), dma((3,)), dma((3,)), dma((5,)), dma((5,)),
            dma((5,)), dma((5,)), dma((10, 4)), dma((10, 4)), dma((2,)), dma((3,)), dma((3,)),
            dma((7,)), dma((7,)), dma((9,)), dma((9,)),
        ],
        compiler_params=pltpu.CompilerParams(
            collective_id=0, has_side_effects=True, vmem_limit_bytes=VMEM_LIMIT
        ),
        cost_estimate=pl.CostEstimate(
            flops=16 * 10**9, bytes_accessed=32 * 2**20, transcendentals=0
        ),
        name="block",
    )(grad, weight, gate, *channelwise, *constants)


def unturn_kernel(
    in_ref, lags_ref, medium_ref, hidden_ref, long_ref, eye_ref,
    outer_out, inner_out, input_out, filter_out, lags_out, short_out,
):
    size, height = inner_out.shape[1], in_ref.shape[4]
    blocks = in_ref.shape[0]
    width = size // blocks

    def lined(value):
        return dot_t(eye_ref[...], value.reshape(size, height))

    outer_out[...] = (hidden_ref[0].astype(F32) * long_ref[...].astype(F32)).astype(BF16)
    inner_out[...] = (lined(in_ref[:, :, 0]) * medium_ref[...].astype(F32)).astype(BF16)
    filter_out[...] = lined(in_ref[:, :, 1])
    input_out[...] = lined(in_ref[:, :, 2]).astype(BF16)
    lags_out[...] = lined(lags_ref[:, :width])
    lane = lax.broadcasted_iota(jnp.int32, (height, size), 0)
    column = lax.broadcasted_iota(jnp.int32, (height, size), 1)
    short = jnp.zeros((PAD, size), F32)
    for b in range(blocks):
        place = (column == lane + b * width) & (lane < width)
        short += dot(lags_ref[b, width:], place.astype(F32).astype(BF16))
    short_out[...] = short[:SHORT]


def from_blocks(block, lags, medium_out, hidden, long_out):
    devices, parts, items, chunk, height = block.shape
    span = devices // 4
    size = span * parts * chunk
    channels = devices * parts * chunk
    rows = pl.BlockSpec((height, size), lambda i: (0, i))
    eye = np.eye(height).astype(jnp.bfloat16)
    return pl.pallas_call(
        unturn_kernel,
        grid=(devices // span,),
        out_shape=[
            jax.ShapeDtypeStruct((height, channels), t) for t in (BF16, BF16, BF16, F32, F32)
        ] + [jax.ShapeDtypeStruct((SHORT, channels), F32)],
        in_specs=[
            pl.BlockSpec((span, parts, items, chunk, height), lambda i: (i, 0, 0, 0, 0)),
            pl.BlockSpec((span, lags.shape[1], height), lambda i: (i, 0, 0)),
            rows,
            pl.BlockSpec((1, height, size), lambda i: (i, 0, 0)),
            rows,
            pl.BlockSpec((height, height), lambda i: (0, 0)),
        ],
        out_specs=[rows] * 5 + [pl.BlockSpec((SHORT, size), lambda i: (0, i))],
        cost_estimate=pl.CostEstimate(
            flops=0, bytes_accessed=24 * height * channels, transcendentals=0
        ),
        name="from_blocks",
    )(block, lags, medium_out, hidden, long_out, eye)


def per_device(
    out_grad, out_weight, outer_gate, long_out, inner_gate, conv_input,
    short_out, medium_out, long_filter, taps_short, taps_medium,
):
    channels = outer_gate.shape[1]
    devices = lax.axis_size("seq")
    width = channels // devices
    hidden, results, lags = block_call(
        out_grad, out_weight, outer_gate,
        (inner_gate, medium_out, short_out, conv_input, long_filter, taps_short, taps_medium),
        tables(devices),
    )
    lags = lags.reshape(devices, width + PAD, LANES)
    outer, inner, short, filt, medium_taps, short_taps = from_blocks(
        results, lags, medium_out, hidden, long_out
    )
    return outer, inner, short, filt, short_taps, medium_taps


def solution(mesh):
    rows = P("seq", "ch")
    return jax.shard_map(
        per_device,
        mesh=mesh,
        in_specs=(rows, P(("seq", "ch"), None)) + (rows,) * 7 + (P(None, "ch"),) * 2,
        out_specs=(rows,) * 4 + (P(None, "ch"),) * 2,
        check_vma=False,
    )
```
